32 devices in a mesh: groups: 2 (over y), cable: 4 (over z), bins: 2 (over x), pairs: 2 (over core).
Axes of the slice: x: 2, y: 2, z: 4, core: 2. Of those that a mesh axis runs over, the one named last changes fastest.
Arguments:
- spectra: bfloat16 [4, 16, 256, 2048], P('groups', None, 'cable', 'bins'), parts along dimension 0, may hold values from -6 to 6
- counts: int32 [8], P(('groups', 'cable')), parts along dimension 0, may hold values from 1 to 4, as said below
- owners: int32 [8, 4], P(('groups', 'cable')), parts along dimension 0, may hold values from 0 to 1
Outputs:
- stacks: float32 [4, 4, 320, 2048], P('groups', 'cable', 'pairs', 'bins'), parts along dimension 0
The draws below stay inside these ranges and needn't reach their ends.
There are 2 independent parts, one for each index of `groups`. The reference program is written for one: setup_inputs(seed, part) draws one part's arguments, and reference() takes and returns one part's arrays. A program takes and returns all parts, laid end to end along the dimension named above; each array names one. Nothing has to cross between parts.
Inputs may be any that keep to these rules, and one draw needn't show every extreme that they name: `counts`: block 0 keeps 4 offsets and block 1 keeps 1.
All inputs are finite; a program needn't handle non-finite values.
Results may differ from the reference program's by a relative error of at most 0.0017.
Values may be sent and summed in bfloat16 or wider, within the bound.
A program may use at most 128 MiB of HBM per device.

```python
import math
import jax
import jax.numpy as jnp
from jax import lax

NF = 2048
BLOCK_CH = 64
WINDOWS = 16
REACH = 3
HALF_WIDTH = 32
BLOCKS = 4
CH = 256
LAGS = 320


def draw_counts(key, part):
    values = jax.random.randint(key, (BLOCKS,), 1, REACH + 2)
    return values.at[0].set(REACH + 1).at[1].set(1)


def touch_ends(drawn, key, low, top_value):
    longest = drawn.shape.index(max(drawn.shape))
    spots = []
    for shift in (0, 1):
        where = [jax.random.randint(jax.random.fold_in(key, axis), (), 0, length) for axis, length in enumerate(drawn.shape)]
        where[longest] = (where[longest] + shift) % drawn.shape[longest]
        spots.append(tuple(where))
    return drawn.at[spots[0]].set(low).at[spots[1]].set(top_value)


def steps_of(key, extent, split, low, largest):
    gain = 1.0
    for dim, shards_of in split:
        draws = jax.random.uniform(jax.random.fold_in(jax.random.fold_in(key, 6), dim), (shards_of,), jnp.float32, low / len(split), largest / len(split))
        gain = gain * jnp.repeat(jnp.exp(draws), extent[dim] // shards_of).reshape((-1,) + (1,) * (len(extent) - 1 - dim))
    return gain


def gaussian(stream_key, shape, spread, reach, split=(), kind=jnp.bfloat16):
    level = steps_of(stream_key, shape, split, -0.22, 0.18) if split else 1.0
    array = jax.random.normal(stream_key, shape, jnp.float32) * spread * level
    return jnp.minimum(jnp.maximum(array, -reach), reach).astype(kind)


def setup_inputs(seed: int = 0, part: int = 0) -> dict:
    arg_keys = jax.random.split(jax.random.key(seed), 4)
    part_splits = jax.random.split(jax.random.fold_in(arg_keys[3], part), 4)
    spectra = gaussian(part_splits[0], (2, WINDOWS, CH, NF), 1.0, 6.0, ((2, 4), (3, 2)))
    counts = draw_counts(jax.random.fold_in(jax.random.fold_in(arg_keys[3], part), 71), part)
    owners = touch_ends(jax.random.randint(part_splits[2], (BLOCKS, REACH + 1), 0, 2), jax.random.fold_in(part_splits[2], 1), 0, 1).astype(jnp.int32)
    return dict(spectra=spectra, counts=counts, owners=owners)


epsilon = 1e-06

def whiten_rows(spectra):
    real_part = spectra[0].astype(jnp.float32)
    imag_part = spectra[1].astype(jnp.float32)
    power_sum = real_part * real_part + imag_part * imag_part
    padded = jnp.pad(power_sum, ((0, 0), (0, 0), (HALF_WIDTH, HALF_WIDTH)))
    window_len = 2 * HALF_WIDTH + 1
    window_sum = lax.reduce_window(padded, jnp.zeros((), padded.dtype), lax.add, (1, 1, window_len), (1, 1, 1), 'VALID')
    inverse_amp = lax.rsqrt(window_sum / window_len + epsilon)
    return jnp.stack([(real_part * inverse_amp).astype(jnp.bfloat16), (imag_part * inverse_amp).astype(jnp.bfloat16)])

def cross_blocks(source, receiver):
    left_real = jnp.concatenate([source[0], source[1]], axis=0).astype(jnp.float32)
    left_imag = jnp.concatenate([source[1], -source[0]], axis=0).astype(jnp.float32)
    right_both = jnp.concatenate([receiver[0], receiver[1]], axis=0).astype(jnp.float32)
    factor = 1.0 / math.sqrt(source.shape[1] * source.shape[2])
    corr_real = (jnp.einsum('wif,wjf->fij', left_real, right_both) * factor).astype(jnp.bfloat16)
    corr_imag = (jnp.einsum('wif,wjf->fij', left_imag, right_both) * factor).astype(jnp.bfloat16)
    return (corr_real, corr_imag)

def lag_stack(pair_block):
    values = pair_block.astype(jnp.float32)[:, ::-1, :]
    freq_count, row_count, col_count = values.shape
    padded = jnp.pad(values, ((0, 0), (0, 0), (0, row_count)))
    flattened = padded.reshape(freq_count, row_count * (col_count + row_count))
    flattened = flattened[:, :row_count * (col_count + row_count - 1)]
    return flattened.reshape(freq_count, row_count, col_count + row_count - 1).sum(axis=1)

def reference(spectra, counts, owners):
    white = whiten_rows(spectra)
    stacks = jnp.zeros((2, BLOCKS, LAGS, NF), jnp.float32)
    for block_index in range(BLOCKS):
        source = white[:, :, block_index * BLOCK_CH:(block_index + 1) * BLOCK_CH]
        live_count = jnp.minimum(counts[block_index], BLOCKS - block_index)
        for offset in range(REACH + 1):
            if block_index + offset < BLOCKS:
                far_index = block_index + offset
                receiver = white[:, :, far_index * BLOCK_CH:(far_index + 1) * BLOCK_CH]
                corr_real, corr_imag = cross_blocks(source, receiver)
                lag_piece = jnp.stack([lag_stack(corr_real), lag_stack(corr_imag)])
                lag_piece = jnp.swapaxes(lag_piece, 1, 2)[:, None]
                weight = (offset < live_count).astype(jnp.float32)
                target = (block_index + offset * owners[block_index, offset]).astype(jnp.int32)
                first_lag = (jnp.int32(0), target, jnp.int32(offset * BLOCK_CH), jnp.int32(0))
                current = lax.dynamic_slice(stacks, first_lag, lag_piece.shape)
                stacks = lax.dynamic_update_slice(stacks, current + weight * lag_piece, first_lag)
    return stacks
```

```python
import math

import jax
import jax.numpy as jnp
import numpy as np
from jax import lax
from jax.experimental import pallas as pl
from jax.experimental.pallas import tpu as pltpu
from jax.sharding import PartitionSpec as P

REACH = 3
HALF_WIDTH = 32


epsilon = 1e-06
band_rows = 16


def with_halo(x, sides, width):
    for axis, dim in sides:
        count, length = (lax.axis_size(axis), x.shape[dim])
        up = [(i, (i + 1) % count) for i in range(count - 1)]
        down = [(j, i) for i, j in up]
        last = lax.slice_in_dim(x, length - width, length, axis=dim)
        first = lax.slice_in_dim(x, 0, width, axis=dim)
        before = lax.ppermute(last, axis, up)
        after = lax.ppermute(first, axis, down)
        x = jnp.concatenate([before, x, after], axis=dim)
    return x


def from_behind(block, axis, distance):
    devices = range(lax.axis_size(axis))
    route = [(i - distance, i) for i in devices if i - distance in devices]
    return lax.ppermute(block, axis, route)


def whiten_rows(spectra):
    real_part = spectra[0].astype(jnp.float32)
    imag_part = spectra[1].astype(jnp.float32)
    power_sum = real_part * real_part + imag_part * imag_part
    padded = with_halo(power_sum, (("bins", 2),), HALF_WIDTH)
    window_len = 2 * HALF_WIDTH + 1
    window_sum = lax.reduce_window(
        padded, jnp.zeros((), padded.dtype), lax.add, (1, 1, window_len), (1, 1, 1), "VALID"
    )
    inverse_amp = lax.rsqrt(window_sum / window_len + epsilon)
    return jnp.stack(
        [
            (real_part * inverse_amp).astype(jnp.bfloat16),
            (imag_part * inverse_amp).astype(jnp.bfloat16),
        ]
    )


def make_lag_table(col_count):
    flattened = jnp.arange(band_rows * col_count)
    row_of = flattened // col_count
    col_of = flattened % col_count
    lag_lanes = jnp.arange(col_count + band_rows - 1)
    return (lag_lanes[None, :] == (col_of - row_of + band_rows - 1)[:, None]).astype(jnp.bfloat16)


def lag_stack(pair_block, lag_table):
    freq_count, row_count, col_count = pair_block.shape
    group_count = row_count // band_rows
    grouped = pair_block.reshape(freq_count, group_count, band_rows * col_count)
    banded = jnp.einsum("fgk,ku->fgu", grouped, lag_table, preferred_element_type=jnp.float32)
    lag_sums = jnp.zeros((freq_count, col_count + row_count - 1), jnp.float32)
    for row_group in range(group_count):
        first_lag = row_count - band_rows * (row_group + 1)
        lag_sums = lag_sums.at[:, first_lag : first_lag + col_count + band_rows - 1].add(
            banded[:, row_group]
        )
    return lag_sums.T


def correlate(left_rows, right_rows, factor, lag_table):
    left_real = jnp.concatenate([left_rows[0], left_rows[1]], axis=0)
    left_imag = jnp.concatenate([left_rows[1], -left_rows[0]], axis=0)
    right_both = jnp.concatenate([right_rows[0], right_rows[1]], axis=0)
    corr_real = (
        jnp.einsum("wif,wjf->fij", left_real, right_both, preferred_element_type=jnp.float32)
        * factor
    ).astype(jnp.bfloat16)
    corr_imag = (
        jnp.einsum("wif,wjf->fij", left_imag, right_both, preferred_element_type=jnp.float32)
        * factor
    ).astype(jnp.bfloat16)
    return jnp.stack([lag_stack(corr_real, lag_table), lag_stack(corr_imag, lag_table)])


def general_shards(spectra, counts, owners):
    pair_devs = lax.axis_size("pairs")
    member = lax.axis_index("pairs")
    channels = spectra.shape[2]
    half_rows = channels // pair_devs
    source = whiten_rows(spectra)
    receiver = lax.dynamic_slice_in_dim(source, member * half_rows, half_rows, 2)
    block_count = lax.axis_size("cable")
    cable_index = lax.axis_index("cable")
    live_count = jnp.minimum(counts[0], block_count - cable_index)
    panels = {0: receiver}
    for offset in range(1, REACH + 1):
        panels[offset] = from_behind(receiver, "cable", -offset)
    factor = 1.0 / math.sqrt(source.shape[1] * channels)
    lag_table = make_lag_table(half_rows)
    freq_count = source.shape[3]
    stacks = jnp.zeros((2, (REACH + 2) * channels, freq_count), jnp.float32)
    for offset in range(REACH + 1):
        lag_piece = correlate(source, panels[offset], factor, lag_table)
        weight = (offset < live_count).astype(jnp.float32)
        if offset == 0:
            kept_here = weight * lag_piece
        else:
            sent_away = owners[0, offset].astype(jnp.float32)
            arrived = from_behind(weight * sent_away * lag_piece, "cable", offset)
            kept_here = weight * (1.0 - sent_away) * lag_piece + arrived
        first_lag = offset * channels + member * half_rows
        current = lax.dynamic_slice_in_dim(stacks, first_lag, kept_here.shape[1], 1)
        stacks = lax.dynamic_update_slice_in_dim(stacks, current + kept_here, first_lag, 1)
    summed = lax.psum_scatter(stacks, "pairs", scatter_dimension=1, tiled=True)
    return summed[:, None]


EDGE = 128
BAND = 128
GROUP = 2
EARLY = 9
TABLE_ROWS = 2048
F32 = jnp.float32
BF16 = jnp.bfloat16
MESH = pl.DeviceIdType.MESH


def channel_transforms(channels, factor):
    points = 2 * channels
    index = np.arange(points)
    angle = 2 * np.pi * np.outer(index, np.arange(channels)) / points
    cos, sin = np.cos(angle), np.sin(angle)
    forward = split_high_low(np.block([[cos, sin], [-sin, cos]]))
    angle = 2 * np.pi * np.outer(index - (channels - 1), index) / points
    cos, sin = np.cos(angle), np.sin(angle)
    cos[-1], sin[-1] = 0.0, 0.0
    inverse = split_high_low(np.block([[cos, sin], [-sin, cos]]) * (factor / points))
    return forward, inverse


def split_high_low(full):
    high = full.astype(jnp.bfloat16)
    low = (full - high.astype(np.float64)).astype(jnp.bfloat16)
    return np.concatenate([high, low], axis=1)


def smoothing_window():
    distance = np.arange(BAND + 2 * EDGE)[:, None] - (np.arange(BAND)[None, :] + EDGE)
    ones = (np.abs(distance) <= HALF_WIDTH).astype(jnp.bfloat16)
    return np.concatenate([ones, ones], axis=0)


def stack_kernel(
    spectra_ref, counts_ref, owners_ref, tables_ref, out_ref,
    x_ref, window_ref, forward_ref, inverse_ref, flag_ref, seen,
    white, white0, white1, white2, white3, spec, one, two, three, sums_a, sums_b, sums_c,
    stack, near_out, far_out, inbox, swapped,
    load_sem, constant_sem, edge_send, edge_recv, flag_send, flag_recv,
    block_send, block_recv, result_send, result_recv, swap_send, swap_recv,
):
    windows, channels = x_ref.shape[1:3]
    half = x_ref.shape[3] - 2 * EDGE
    bands, groups = half // BAND, windows // GROUP
    pieces = bands * groups
    points = 2 * channels
    kept = out_ref.shape[1]
    blocks, halves = lax.axis_size("cable"), lax.axis_size("pairs")
    z, m = lax.axis_index("cable"), lax.axis_index("pairs")
    cuts, x = lax.axis_size("bins"), lax.axis_index("bins")
    bins = spectra_ref.shape[3]
    first = m == 0
    second = m == 1
    mirrored = x
    partner = {"pairs": 1 - m}

    def remote(source, target, send, recv, device):
        return pltpu.make_async_remote_copy(
            src_ref=source, dst_ref=target, send_sem=send, recv_sem=recv, device_id=device, device_id_type=MESH
        )

    received = (white0, white1, white2, white3)

    def own_to(block, s, lane, device):
        return remote(
            white.at[s], received[block].at[s], block_send.at[lane, s], block_recv.at[block, s], {"cable": device}
        )

    def pass_on(s, lane, device):
        return remote(
            white0.at[s], white0.at[s], block_send.at[lane, s], block_recv.at[0, s], {"cable": device}
        )

    def arrived(block, s):
        own_to(block, s, 0, 0).wait_recv()

    def sent(s, lane):
        own_to(0, s, lane, 0).wait_send()

    def place(c):
        return c + mirrored * (bands - 1 - 2 * c)

    def results(c, source, sender, buffer, begin, low, high, device, lane):
        copies = {}
        for target in range(halves):
            top, end = max(low, target * kept), min(high, (target + 1) * kept)
            if top < end:
                copies[target] = remote(
                    buffer.at[c, :, top - begin : end - begin],
                    inbox.at[source, sender, c, :, top - target * kept : end - target * kept],
                    result_send.at[lane, target, c],
                    result_recv.at[source, sender, c],
                    {"cable": device, "pairs": target},
                )
        return copies

    def start_all(copies):
        for copy in copies.values():
            copy.start()

    def finish_all(copies):
        for copy in copies.values():
            copy.wait_send()

    one_pair = channels + points
    two_pairs = 2 * channels + points
    three_pairs = 3 * channels + points

    def near_from_1(c, sender=m):
        return results(c, 1, sender, near_out, channels, channels, one_pair, 0, 0)

    def near_from_1_all(c, sender=m):
        return results(c, 1, sender, near_out, channels, channels, three_pairs, 0, 0)

    def near_from_2(c, sender=m):
        return results(c, 2, sender, near_out, 2 * channels, 2 * channels, three_pairs, 0, 0)

    def near_from_3(c, sender=m):
        return results(c, 3, sender, near_out, channels, 3 * channels, three_pairs, 0, 0)

    def near_pair_23(c, sender=m):
        return results(c, 3, sender, far_out, channels, channels, one_pair, 2, 1)

    def far_from_2(c, sender=m):
        return results(c, 2, sender, far_out, channels, channels, three_pairs, 3, 1)

    def far_pair_01(c, source, sender=m):
        return results(c, source, sender, near_out, channels, channels, one_pair, 1, 0)

    def far_pair_02(c, source, sender=m):
        return results(c, source, sender, far_out, 2 * channels, 2 * channels, two_pairs, 2, 1)

    def far_pair_03(c, source, sender=m):
        return results(c, source, sender, far_out, channels, 3 * channels, three_pairs, 3, 2)

    def swap(c):
        rows = pl.ds(pl.multiple_of((1 - m) * kept, 8), kept)
        return remote(stack.at[c, :, rows], swapped.at[c], swap_send.at[c], swap_recv.at[c], partner)

    def load(q):
        near = pl.multiple_of(m * (half - EDGE), EDGE)
        begin = pl.multiple_of((1 - m) * EDGE, EDGE)
        rows = pl.ds(q * GROUP, GROUP)
        return pltpu.make_async_copy(
            spectra_ref.at[:, rows, :, pl.ds(near, half + EDGE)],
            x_ref.at[:, rows, :, pl.ds(begin, half + EDGE)],
            load_sem.at[q],
        )

    constants, top = [], 0
    for i, table in enumerate((window_ref, forward_ref, inverse_ref)):
        rows, columns = table.shape
        source = tables_ref.at[top : top + rows, :columns]
        constants.append(pltpu.make_async_copy(source, table, constant_sem.at[i]))
        top += rows

    edge_lanes = pl.ds(pl.multiple_of(m * (half + EDGE), EDGE), EDGE)

    def edge():
        source = pl.ds(pl.multiple_of((1 - m) * (bins - EDGE), EDGE), EDGE)
        return remote(
            spectra_ref.at[:, :, :, source],
            x_ref.at[:, :, :, edge_lanes],
            edge_send.at[0],
            edge_recv.at[0],
            {"bins": 1 - x},
        )

    def flags_to(source, device, lane):
        return remote(
            flag_ref, seen.at[source], flag_send.at[lane], flag_recv.at[source], {"cable": device}
        )

    load(0).start()
    constants[0].start()
    for q in range(1, groups):
        load(q).start()
    constants[1].start()
    constants[2].start()
    live = jnp.minimum(counts_ref[0], blocks - z)
    for offset in range(REACH + 1):
        flag_ref[offset : offset + 1, :] = jnp.full((1, BAND), owners_ref[0, offset].astype(F32))
        weight = jnp.where(offset < live, 1.0, 0.0)
        flag_ref[REACH + 1 + offset : REACH + 2 + offset, :] = jnp.full((1, BAND), weight)
    barrier = pltpu.get_barrier_semaphore()
    for step in range(1, blocks):
        pl.semaphore_signal(barrier, inc=1, device_id={"cable": lax.rem(z + step, blocks)}, device_id_type=MESH)
        across = {"cable": lax.rem(z + step, blocks), "pairs": 1 - m}
        pl.semaphore_signal(barrier, inc=1, device_id=across, device_id_type=MESH)
    pl.semaphore_signal(barrier, inc=1, device_id=partner, device_id_type=MESH)
    pl.semaphore_signal(barrier, inc=1, device_id={"bins": 1 - x}, device_id_type=MESH)
    sends_edge = x == m
    takes_edge = x != m

    def whiten(q, begin, count, store):
        lanes = pl.ds(pl.multiple_of(begin, BAND), count * BAND + 2 * EDGE)
        reals, imags, highs, lows = [], [], [], []
        for i in range(GROUP):
            real = x_ref[0, q * GROUP + i, :, lanes].astype(F32)
            imag = x_ref[1, q * GROUP + i, :, lanes].astype(F32)
            power = real * real + imag * imag
            high = power.astype(BF16)
            reals.append(real)
            imags.append(imag)
            highs.append(high)
            lows.append((power - high.astype(F32)).astype(BF16))
        high = jnp.concatenate(highs, axis=0)
        low = jnp.concatenate(lows, axis=0)
        for j in range(count):
            reach = slice(j * BAND, (j + 1) * BAND + 2 * EDGE)
            terms = jnp.concatenate([high[:, reach], low[:, reach]], axis=1)
            total = jnp.dot(terms, window_ref[...], preferred_element_type=F32)
            gain = lax.rsqrt(total / (2 * HALF_WIDTH + 1) + epsilon)
            here = slice(EDGE + j * BAND, EDGE + (j + 1) * BAND)
            slot = store(j) * groups + q
            for i in range(GROUP):
                rows = gain[i * channels : (i + 1) * channels]
                white[slot, i, :channels] = (reals[i][:, here] * rows).astype(BF16)
                white[slot, i, channels:] = (imags[i][:, here] * rows).astype(BF16)

    def whiten_inner(q):
        load(q).wait()
        whiten(q, mirrored * BAND, bands - 1, lambda j: j + mirrored * (bands - 2 - 2 * j))

    def send_inner(q):
        @pl.when(z == 0)
        def _():
            own_to(0, q + groups * m, 0, 1).start()

        @pl.when((z == 1) & second)
        def _():
            own_to(1, q, 1, 0).start()

        @pl.when((z == 2) & second)
        def _():
            own_to(2, q, 0, 0).start()
            own_to(2, q, 1, 3).start()

        @pl.when(z == 3)
        def _():
            own_to(3, q, 0, 2 - 2 * m).start()

    def relay(i):
        s = i + groups * m
        arrived(0, s)
        pass_on(s, 0, 2).start()

    def relay_if(condition, i):
        @pl.when((z == 1) & condition)
        def _():
            relay(i)

    def send_range(block, begin, end, lane, device):
        @pl.loop(begin, end)
        def _(s):
            own_to(block, s, lane, device).start()

    constants[0].wait()
    whiten_inner(0)
    pl.semaphore_wait(barrier, 2 * blocks)

    @pl.when(sends_edge)
    def _():
        edge().start()

    send_inner(0)

    @pl.when(z == 0)
    def _():
        for device in range(1, blocks):
            flags_to(0, device, device - 1).start()

    @pl.when(z == 2)
    def _():
        flags_to(1, 3, 0).start()

    @pl.when(~takes_edge)
    def _():
        x_ref[:, :, :, edge_lanes] = jnp.zeros((2, windows, channels, EDGE), x_ref.dtype)

    def inner_step(q, carry):
        whiten_inner(q)
        send_inner(q)
        relay_if((q >= 3) & (lax.rem(q, 2) == 1), lax.div(q - 3, 2))
        return carry

    lax.fori_loop(1, groups, inner_step, 0)

    @pl.when(z == 0)
    def _():
        send_range(0, groups + groups * m, 3 * groups, 0, 1)

    @pl.when((z == 2) & second)
    def _():
        send_range(2, groups, 2 * groups, 1, 3)

    @pl.when((z == 3) & second)
    def _():
        send_range(3, 2 * groups, 3 * groups, 0, 2)

    @pl.when(takes_edge)
    def _():
        edge().wait_recv()

    def last_step(q, carry):
        whiten(q, (1 - mirrored) * (bands - 1) * BAND, 1, lambda j: bands - 1)
        s = (bands - 1) * groups + q

        @pl.when(z == 0)
        def _():
            own_to(0, s, 0, 1).start()

        @pl.when((z == 2) & first)
        def _():
            own_to(2, s, 0, 1).start()
            own_to(2, s, 1, 3).start()

        @pl.when(z == 3)
        def _():
            own_to(3, s, 0, 1 + m).start()

        relay_if(lax.rem(q, 4) == 3, 3 + lax.div(q, 4))
        return carry

    lax.fori_loop(0, groups, last_step, 0)

    @pl.when((z == 3) & first)
    def _():
        send_range(3, groups, 3 * groups, 0, 2)

    constants[1].wait()
    constants[2].wait()

    def transform(buffer, s):
        wide = jnp.concatenate([buffer[s, i] for i in range(GROUP)], axis=1)
        return jnp.dot(forward_ref[...], jnp.concatenate([wide, wide], axis=0), preferred_element_type=F32)

    tile = 32

    def power_into(total, s):
        for k in range(0, points, tile):
            gained = total[k : k + tile]
            for i in range(GROUP):
                lanes = slice(i * BAND, (i + 1) * BAND)
                real = spec[s, k : k + tile, lanes]
                imag = spec[s, points + k : points + k + tile, lanes]
                gained = gained + (real * real + imag * imag)
            total[k : k + tile] = gained

    def cross_into(total, near, far):
        for k in range(0, points, tile):
            gained_real = total[k : k + tile]
            gained_imag = total[points + k : points + k + tile]
            for i in range(GROUP):
                lanes = slice(i * BAND, (i + 1) * BAND)
                near_real = near[k : k + tile, lanes]
                near_imag = near[points + k : points + k + tile, lanes]
                far_real = far[k : k + tile, lanes]
                far_imag = far[points + k : points + k + tile, lanes]
                gained_real = gained_real + (near_real * far_real + near_imag * far_imag)
                gained_imag = gained_imag + (near_imag * far_real - near_real * far_imag)
            total[k : k + tile] = gained_real
            total[points + k : points + k + tile] = gained_imag

    def lags_of(values, columns):
        high = values.astype(BF16)
        low = (values - high.astype(F32)).astype(BF16)
        table = inverse_ref[:, :columns]
        rest = inverse_ref[:, 2 * points : 2 * points + columns]
        return jnp.dot(
            jnp.concatenate([table, rest, table], axis=1),
            jnp.concatenate([high, high, low], axis=0),
            preferred_element_type=F32,
        )

    def lags_of_many(*totals):
        both = lags_of(jnp.concatenate([total[...] for total in totals], axis=1), 2 * points)
        return [both[:, i * BAND : (i + 1) * BAND] for i in range(len(totals))]

    def add_piece(c, begin, piece):
        rows = pl.ds(begin, points)
        stack[c, 0, rows] += piece[:points]
        stack[c, 1, rows] += piece[points:]

    def clear(*totals):
        for total in totals:
            total[...] = jnp.zeros_like(total)

    def over_windows(step):
        def body(q, carry):
            step(q)
            return carry

        lax.fori_loop(0, groups, body, 0)

    def over_bands(begin, end, band):
        def body(c, carry):
            band(c)
            return carry

        lax.fori_loop(begin, end, body, 0)

    def own_band(c):
        clear(sums_a)

        def step(q):
            s = c * groups + q
            spec[s] = transform(white, s)
            power_into(sums_a, s)

        over_windows(step)
        stack[c] = jnp.zeros(stack.shape[1:], F32)
        add_piece(c, 0, flag_ref[REACH + 1 : REACH + 2, :] * lags_of(sums_a[:points], points))
        relay_if(c >= 0, EARLY - bands + c)

    over_bands(0, bands, own_band)

    def owner_of(flags, offset):
        return flags[offset : offset + 1, :]

    def far_share(flags, offset):
        return owner_of(flags, offset) * flags[REACH + 1 + offset : REACH + 2 + offset, :]

    def near_share(flags, offset):
        return (1.0 - owner_of(flags, offset)) * flags[REACH + 1 + offset : REACH + 2 + offset, :]

    def store_rows(buffer, c, begin, piece, rows=slice(0, 2 * channels)):
        count = rows.stop - rows.start
        for part in range(2):
            top = part * points
            buffer[c, part, begin : begin + count] = piece[top + rows.start : top + rows.stop].astype(buffer.dtype)

    def store_sums(buffer, c, parts):
        for part in range(2):
            top = part * points
            for k in range(len(parts) + 1):
                terms = []
                if k < len(parts):
                    terms.append(parts[k][top : top + channels])
                if k > 0:
                    terms.append(parts[k - 1][top + channels : top + points])
                total = terms[0] if len(terms) == 1 else terms[0] + terms[1]
                buffer[c, part, k * channels : (k + 1) * channels] = total.astype(buffer.dtype)

    zero_flags, two_flags = seen.at[0], seen.at[1]

    @pl.when(z == 0)
    def _():
        @pl.when(second)
        def _():
            clear(sums_a, sums_b, sums_c)

            def step(q):
                for block, total, held in ((1, sums_a, one), (2, sums_b, two), (3, sums_c, three)):
                    arrived(block, q)
                    held[...] = transform(received[block], q)
                    cross_into(total, spec.at[q], held)

            over_windows(step)
            pairs = lags_of_many(sums_a, sums_b, sums_c)
            for offset in range(1, REACH + 1):
                add_piece(0, offset * channels, near_share(flag_ref, offset) * pairs[offset - 1])
            store_rows(near_out, 0, 0, far_share(flag_ref, 1) * pairs[0])
            store_rows(far_out, 0, 0, far_share(flag_ref, 2) * pairs[1])
            store_rows(far_out, 0, points, far_share(flag_ref, 3) * pairs[2])
            start_all(far_pair_01(0, 0))
            start_all(far_pair_02(0, 0))
            start_all(far_pair_03(0, 0))

        @pl.loop(0, bands)
        def _(c):
            swap(c).start()

    @pl.when(z == 1)
    def _():
        flags_to(0, 1, 0).wait_recv()

        @pl.when(second)
        def _():
            swap(0).start()

        def band(c):
            clear(sums_a)

            def step(q):
                s = c * groups + q
                i = s - groups * m

                @pl.when(i + EARLY < 3 * groups)
                def _():
                    relay(i + EARLY)

                one[...] = transform(white0, s)
                cross_into(sums_a, one, spec.at[s])

                @pl.when(first & (c == bands - 2))
                def _():
                    late = (bands - 1) * groups + q
                    arrived(2, late)
                    spec[q] = transform(white2, late)
                    arrived(3, late)
                    spec[groups + q] = transform(white3, late)

            over_windows(step)
            piece = lags_of(sums_a[...], 2 * points)
            store_rows(near_out, c, 0, near_share(zero_flags, 1) * piece)
            start_all(near_from_1(c))
            add_piece(c, channels, far_share(zero_flags, 1) * piece)
            swap(c).start()

        over_bands(m, m + bands - 1, band)

        @pl.when(first)
        def _():
            c = bands - 1
            clear(sums_a, sums_b, sums_c)

            def step(q):
                s = c * groups + q
                arrived(0, s)
                one[...] = transform(white0, s)
                cross_into(sums_a, one, spec.at[s])
                cross_into(sums_b, one, spec.at[q])
                cross_into(sums_c, one, spec.at[groups + q])

            over_windows(step)
            pairs = lags_of_many(sums_a, sums_b, sums_c)
            store_sums(near_out, c, [near_share(zero_flags, o) * pairs[o - 1] for o in range(1, REACH + 1)])
            start_all(near_from_1_all(c))
            store_rows(far_out, c, points, far_share(zero_flags, 3) * pairs[2])
            start_all(far_pair_03(c, 1))
            store_rows(far_out, c, 0, far_share(zero_flags, 2) * pairs[1])
            start_all(far_pair_02(c, 1))
            add_piece(c, channels, far_share(zero_flags, 1) * pairs[0])
            swap(c).start()

    @pl.when(z == 2)
    def _():
        flags_to(0, 2, 0).wait_recv()

        @pl.when(first)
        def _():
            swap(bands - 1).start()

        @pl.when(second)
        def _():
            swap(0).start()
            clear(sums_a)

            def step(q):
                s = groups + q
                arrived(0, s)
                pass_on(s, 2, 3).start()
                one[...] = transform(white0, s)
                cross_into(sums_a, one, spec.at[s])

            over_windows(step)
            piece = lags_of(sums_a[...], 2 * points)
            store_rows(near_out, 1, 0, near_share(zero_flags, 2) * piece)
            near_out[1, :, points : points + channels] = jnp.zeros((2, channels, BAND), near_out.dtype)
            start_all(near_from_2(1))
            add_piece(1, 2 * channels, far_share(zero_flags, 2) * piece)
            swap(1).start()

        def band(c):
            clear(sums_a, sums_b, sums_c)

            def step(q):
                s = c * groups + q
                arrived(3, s)
                three[...] = transform(white3, s)
                cross_into(sums_b, spec.at[s], three)

                @pl.when(q == groups - 1)
                def _():
                    sums_b[...] = lags_of(sums_b[...], 2 * points)

                arrived(0, s)
                one[...] = transform(white0, s)
                cross_into(sums_a, one, spec.at[s])
                cross_into(sums_c, one, three)

            over_windows(step)
            near, beyond = lags_of_many(sums_a, sums_c)
            store_sums(near_out, c, [near_share(zero_flags, 2) * near, near_share(zero_flags, 3) * beyond])
            start_all(near_from_2(c))
            ahead = sums_b[...]
            store_rows(far_out, c, 0, far_share(flag_ref, 1) * ahead)
            store_rows(far_out, c, points, far_share(zero_flags, 3) * beyond)
            start_all(far_from_2(c))
            add_piece(c, 2 * channels, far_share(zero_flags, 2) * near)
            add_piece(c, channels, near_share(flag_ref, 1) * ahead)
            swap(c).start()

        over_bands(2 * m, bands - 1 + m, band)

    @pl.when(z == 3)
    def _():
        flags_to(0, 3, 0).wait_recv()
        flags_to(1, 3, 0).wait_recv()

        @pl.when(first)
        def _():
            @pl.loop(0, bands - 1)
            def _(c):
                swap(c).start()

        @pl.when(second)
        def _():
            @pl.loop(2, bands)
            def _(c):
                swap(c).start()

        def band(c):
            clear(sums_a)

            def step(q):
                s = c * groups + q
                arrived(2, s)
                two[...] = transform(white2, s)
                cross_into(sums_a, two, spec.at[s])

            over_windows(step)
            piece = lags_of(sums_a[...], 2 * points)
            store_rows(far_out, c, 0, near_share(two_flags, 1) * piece)
            start_all(near_pair_23(c))
            add_piece(c, channels, far_share(two_flags, 1) * piece)

            @pl.when(second & (c == 1))
            def _():
                clear(sums_c)

                def late_step(q):
                    s = c * groups + q
                    arrived(0, s)
                    one[...] = transform(white0, s)
                    cross_into(sums_c, one, spec.at[s])

                over_windows(late_step)
                distant = lags_of(sums_c[...], 2 * points)
                store_rows(near_out, c, points, near_share(zero_flags, 3) * distant)
                start_all(near_from_3(c))
                add_piece(c, 3 * channels, far_share(zero_flags, 3) * distant)

            swap(c).start()

        over_bands((1 - m) * (bands - 1), (1 - m) * bands + 2 * m, band)

    def lanes_of(core, c):
        return pl.ds(pl.multiple_of(core * half + place(c) * BAND, BAND), BAND)

    def collect(c):
        out_ref[:, :, lanes_of(m, c)] = stack[c, :, pl.ds(pl.multiple_of(m * kept, 8), kept)]
        swap(c).wait_recv()
        out_ref[:, :, lanes_of(1 - m, c)] = swapped[c]
        swap(c).wait_send()

    over_bands(0, bands, collect)

    def take(target, c, source, sender, low, high):
        top, end = max(low, target * kept), min(high, (target + 1) * kept)
        if top < end:
            rows = slice(top - target * kept, end - target * kept)
            results(c, source, sender, near_out, low, low, high, 0, 0)[target].wait_recv()
            out_ref[:, rows, lanes_of(sender, c)] += inbox[source, sender, c, :, rows].astype(F32)

    def take_at_0(target):
        for sender in range(halves):
            def band(c):
                take(target, c, 1, sender, channels, one_pair)
                take(target, c, 2, sender, 2 * channels, three_pairs)

            over_bands(sender, sender + bands - 1, band)
        take(target, 1, 3, 1, 3 * channels, three_pairs)
        take(target, bands - 1, 1, 0, channels, three_pairs)

    def take_at_1(target):
        take(target, 0, 0, 1, channels, one_pair)

    def take_at_2(target):
        take(target, 0, 0, 1, 2 * channels, two_pairs)
        take(target, 0, 3, 1, channels, one_pair)
        take(target, 1, 3, 1, channels, one_pair)
        take(target, bands - 1, 3, 0, channels, one_pair)
        take(target, bands - 1, 1, 0, 2 * channels, two_pairs)

    def take_at_3(target):
        take(target, 0, 0, 1, 3 * channels, three_pairs)
        for sender in range(halves):
            def band(c):
                take(target, c, 2, sender, channels, three_pairs)

            over_bands(2 * sender, bands - 1 + sender, band)
        take(target, bands - 1, 1, 0, 3 * channels, three_pairs)

    for block, step in enumerate((take_at_0, take_at_1, take_at_2, take_at_3)):
        for target in range(halves):
            @pl.when((z == block) & (m == target))
            def _():
                step(target)

    @pl.when(sends_edge)
    def _():
        edge().wait_send()

    def sent_range(begin, end, lane):
        @pl.loop(begin, end)
        def _(s):
            sent(s, lane)

    @pl.when(z == 0)
    def _():
        for device in range(1, blocks):
            flags_to(0, device, device - 1).wait_send()
        sent_range(groups * m, pieces, 0)

        @pl.when(second)
        def _():
            finish_all(far_pair_01(0, 0))
            finish_all(far_pair_02(0, 0))
            finish_all(far_pair_03(0, 0))

    @pl.when(z == 1)
    def _():
        sent_range(groups * m, groups * m + 3 * groups, 0)
        over_bands(m, m + bands - 1, lambda c: finish_all(near_from_1(c)))

        @pl.when(second)
        def _():
            sent_range(0, groups, 1)

        @pl.when(first)
        def _():
            finish_all(near_from_1_all(bands - 1))
            finish_all(far_pair_03(bands - 1, 1))
            finish_all(far_pair_02(bands - 1, 1))

    @pl.when(z == 2)
    def _():
        flags_to(1, 3, 0).wait_send()

        @pl.when(first)
        def _():
            sent_range((bands - 1) * groups, pieces, 0)
            sent_range((bands - 1) * groups, pieces, 1)

        @pl.when(second)
        def _():
            sent_range(0, groups, 0)
            sent_range(0, 2 * groups, 1)
            sent_range(groups, 2 * groups, 2)
            finish_all(near_from_2(1))

        def band(c):
            finish_all(near_from_2(c))
            finish_all(far_from_2(c))

        over_bands(2 * m, bands - 1 + m, band)

    @pl.when(z == 3)
    def _():
        @pl.when(first)
        def _():
            sent_range(0, pieces, 0)
            finish_all(near_pair_23(bands - 1))

        @pl.when(second)
        def _():
            sent_range(0, groups, 0)
            sent_range(2 * groups, pieces, 0)
            finish_all(near_pair_23(0))
            finish_all(near_pair_23(1))
            finish_all(near_from_3(1))


def four_block_shards(spectra, counts, owners):
    parts, windows, channels, bins = spectra.shape
    halves, blocks = lax.axis_size("pairs"), lax.axis_size("cable")
    half, points = bins // halves, 2 * channels
    forward, inverse = channel_transforms(channels, 1.0 / math.sqrt(windows * channels))
    window = smoothing_window()
    bands, groups = half // BAND, windows // GROUP
    pieces = bands * groups
    rows = (REACH + 2) * channels
    kept = rows // halves
    block = pltpu.VMEM((pieces, GROUP, points, BAND), BF16)
    spectrum = pltpu.VMEM((2 * points, GROUP * BAND), F32)
    sums = pltpu.VMEM((2 * points, BAND), F32)
    shares = pltpu.VMEM((bands, 2, 2 * points, BAND), BF16)
    flags = (2 * (REACH + 1), BAND)
    dma = pltpu.SemaphoreType.DMA
    width = inverse.shape[1]
    tables = np.zeros((TABLE_ROWS, width), jnp.bfloat16)
    top = 0
    for table in (window, forward, inverse):
        tables[top : top + table.shape[0], : table.shape[1]] = table
        top += table.shape[0]
    hbm = pl.BlockSpec(memory_space=pl.ANY)
    smem = pl.BlockSpec(memory_space=pltpu.SMEM)
    out = pl.pallas_call(
        stack_kernel,
        out_shape=jax.ShapeDtypeStruct((2, kept, bins), F32),
        in_specs=[hbm, smem, smem, hbm],
        out_specs=pl.BlockSpec(memory_space=pltpu.VMEM),
        scratch_shapes=[
            pltpu.VMEM((2, windows, channels, half + 2 * EDGE), BF16),
            pltpu.VMEM(window.shape, BF16),
            pltpu.VMEM(forward.shape, BF16),
            pltpu.VMEM(inverse.shape, BF16),
            pltpu.VMEM(flags, F32),
            pltpu.VMEM((2,) + flags, F32),
            block, block, block, block, block,
            pltpu.VMEM((pieces, 2 * points, GROUP * BAND), F32),
            spectrum, spectrum, spectrum, sums, sums, sums,
            pltpu.VMEM((bands, 2, rows, BAND), F32),
            shares, shares,
            pltpu.VMEM((blocks, halves, bands, 2, kept, BAND), BF16),
            pltpu.VMEM((bands, 2, kept, BAND), F32),
            dma((groups,)), dma((3,)), dma((1,)), dma((1,)), dma((3,)), dma((2,)),
            dma((3, pieces)), dma((blocks, pieces)),
            dma((3, halves, bands)), dma((blocks, halves, bands)),
            dma((bands,)), dma((bands,)),
        ],
        compiler_params=pltpu.CompilerParams(
            collective_id=0, has_side_effects=True, vmem_limit_bytes=55000000
        ),
    )(spectra, counts, owners, jnp.asarray(tables))
    return out[:, None]


def solution(mesh):
    sizes = dict(mesh.shape)
    fits = sizes["cable"] == REACH + 1 and sizes["pairs"] == 2 and sizes["bins"] == 2
    shards = four_block_shards if fits else general_shards
    placed = (
        P("groups", None, "cable", "bins"),
        P(("groups", "cable")),
        P(("groups", "cable"), None),
    )
    return jax.shard_map(
        shards,
        mesh=mesh,
        in_specs=placed,
        out_specs=P("groups", "cable", "pairs", "bins"),
        check_vma=False,
    )
```

```python
import math

import jax
import jax.numpy as jnp
import numpy as np
from jax import lax
from jax.experimental import pallas as pl
from jax.experimental.pallas import tpu as pltpu
from jax.sharding import PartitionSpec as P

REACH = 3
HALF_WIDTH = 32


epsilon = 1e-06
band_rows = 16


def with_halo(x, sides, width):
    for axis, dim in sides:
        count, length = (lax.axis_size(axis), x.shape[dim])
        up = [(i, (i + 1) % count) for i in range(count - 1)]
        down = [(j, i) for i, j in up]
        last = lax.slice_in_dim(x, length - width, length, axis=dim)
        first = lax.slice_in_dim(x, 0, width, axis=dim)
        before = lax.ppermute(last, axis, up)
        after = lax.ppermute(first, axis, down)
        x = jnp.concatenate([before, x, after], axis=dim)
    return x


def from_behind(block, axis, distance):
    devices = range(lax.axis_size(axis))
    route = [(i - distance, i) for i in devices if i - distance in devices]
    return lax.ppermute(block, axis, route)


def whiten_rows(spectra):
    real_part = spectra[0].astype(jnp.float32)
    imag_part = spectra[1].astype(jnp.float32)
    power_sum = real_part * real_part + imag_part * imag_part
    padded = with_halo(power_sum, (("bins", 2),), HALF_WIDTH)
    window_len = 2 * HALF_WIDTH + 1
    window_sum = lax.reduce_window(
        padded, jnp.zeros((), padded.dtype), lax.add, (1, 1, window_len), (1, 1, 1), "VALID"
    )
    inverse_amp = lax.rsqrt(window_sum / window_len + epsilon)
    return jnp.stack(
        [
            (real_part * inverse_amp).astype(jnp.bfloat16),
            (imag_part * inverse_amp).astype(jnp.bfloat16),
        ]
    )


def make_lag_table(col_count):
    flattened = jnp.arange(band_rows * col_count)
    row_of = flattened // col_count
    col_of = flattened % col_count
    lag_lanes = jnp.arange(col_count + band_rows - 1)
    return (lag_lanes[None, :] == (col_of - row_of + band_rows - 1)[:, None]).astype(jnp.bfloat16)


def lag_stack(pair_block, lag_table):
    freq_count, row_count, col_count = pair_block.shape
    group_count = row_count // band_rows
    grouped = pair_block.reshape(freq_count, group_count, band_rows * col_count)
    banded = jnp.einsum("fgk,ku->fgu", grouped, lag_table, preferred_element_type=jnp.float32)
    lag_sums = jnp.zeros((freq_count, col_count + row_count - 1), jnp.float32)
    for row_group in range(group_count):
        first_lag = row_count - band_rows * (row_group + 1)
        lag_sums = lag_sums.at[:, first_lag : first_lag + col_count + band_rows - 1].add(
            banded[:, row_group]
        )
    return lag_sums.T


def correlate(left_rows, right_rows, factor, lag_table):
    left_real = jnp.concatenate([left_rows[0], left_rows[1]], axis=0)
    left_imag = jnp.concatenate([left_rows[1], -left_rows[0]], axis=0)
    right_both = jnp.concatenate([right_rows[0], right_rows[1]], axis=0)
    corr_real = (
        jnp.einsum("wif,wjf->fij", left_real, right_both, preferred_element_type=jnp.float32)
        * factor
    ).astype(jnp.bfloat16)
    corr_imag = (
        jnp.einsum("wif,wjf->fij", left_imag, right_both, preferred_element_type=jnp.float32)
        * factor
    ).astype(jnp.bfloat16)
    return jnp.stack([lag_stack(corr_real, lag_table), lag_stack(corr_imag, lag_table)])


def general_shards(spectra, counts, owners):
    pair_devs = lax.axis_size("pairs")
    member = lax.axis_index("pairs")
    channels = spectra.shape[2]
    half_rows = channels // pair_devs
    source = whiten_rows(spectra)
    receiver = lax.dynamic_slice_in_dim(source, member * half_rows, half_rows, 2)
    block_count = lax.axis_size("cable")
    cable_index = lax.axis_index("cable")
    live_count = jnp.minimum(counts[0], block_count - cable_index)
    panels = {0: receiver}
    for offset in range(1, REACH + 1):
        panels[offset] = from_behind(receiver, "cable", -offset)
    factor = 1.0 / math.sqrt(source.shape[1] * channels)
    lag_table = make_lag_table(half_rows)
    freq_count = source.shape[3]
    stacks = jnp.zeros((2, (REACH + 2) * channels, freq_count), jnp.float32)
    for offset in range(REACH + 1):
        lag_piece = correlate(source, panels[offset], factor, lag_table)
        weight = (offset < live_count).astype(jnp.float32)
        if offset == 0:
            kept_here = weight * lag_piece
        else:
            sent_away = owners[0, offset].astype(jnp.float32)
            arrived = from_behind(weight * sent_away * lag_piece, "cable", offset)
            kept_here = weight * (1.0 - sent_away) * lag_piece + arrived
        first_lag = offset * channels + member * half_rows
        current = lax.dynamic_slice_in_dim(stacks, first_lag, kept_here.shape[1], 1)
        stacks = lax.dynamic_update_slice_in_dim(stacks, current + kept_here, first_lag, 1)
    summed = lax.psum_scatter(stacks, "pairs", scatter_dimension=1, tiled=True)
    return summed[:, None]


EDGE = 128
BAND = 128
GROUP = 2
EARLY = 9
TABLE_ROWS = 2048
F32 = jnp.float32
BF16 = jnp.bfloat16
MESH = pl.DeviceIdType.MESH


def channel_transforms(channels, factor):
    points = 2 * channels
    index = np.arange(points)
    angle = 2 * np.pi * np.outer(index, np.arange(channels)) / points
    cos, sin = np.cos(angle), np.sin(angle)
    forward = split_high_low(np.block([[cos, sin], [-sin, cos]]))
    angle = 2 * np.pi * np.outer(index - (channels - 1), index) / points
    cos, sin = np.cos(angle), np.sin(angle)
    cos[-1], sin[-1] = 0.0, 0.0
    inverse = split_high_low(np.block([[cos, sin], [-sin, cos]]) * (factor / points))
    return forward, inverse


def split_high_low(full):
    high = full.astype(jnp.bfloat16)
    low = (full - high.astype(np.float64)).astype(jnp.bfloat16)
    return np.concatenate([high, low], axis=1)


def smoothing_window():
    distance = np.arange(BAND + 2 * EDGE)[:, None] - (np.arange(BAND)[None, :] + EDGE)
    ones = (np.abs(distance) <= HALF_WIDTH).astype(jnp.bfloat16)
    return np.concatenate([ones, ones], axis=0)


def stack_kernel(
    spectra_ref, counts_ref, owners_ref, tables_ref, out_ref,
    x_ref, window_ref, forward_ref, inverse_ref, flag_ref, seen,
    white, white0, white1, white2, white3, spec, one, two, three, sums_a, sums_b, sums_c,
    stack, near_out, far_out, inbox, swapped,
    load_sem, constant_sem, edge_send, edge_recv, flag_send, flag_recv,
    block_send, block_recv, result_send, result_recv, swap_send, swap_recv, known, spread, drained,
):
    windows, channels = x_ref.shape[1:3]
    half = x_ref.shape[3] - 2 * EDGE
    bands, groups = half // BAND, windows // GROUP
    pieces = bands * groups
    points = 2 * channels
    kept = out_ref.shape[1]
    blocks, halves = lax.axis_size("cable"), lax.axis_size("pairs")
    z, m = lax.axis_index("cable"), lax.axis_index("pairs")
    cuts, x = lax.axis_size("bins"), lax.axis_index("bins")
    bins = spectra_ref.shape[3]
    first = m == 0
    second = m == 1
    mirrored = x
    partner = {"pairs": 1 - m}

    def remote(source, target, send, recv, device):
        return pltpu.make_async_remote_copy(
            src_ref=source, dst_ref=target, send_sem=send, recv_sem=recv, device_id=device, device_id_type=MESH
        )

    received = (white0, white1, white2, white3)

    def own_to(block, s, lane, device):
        return remote(
            white.at[s], received[block].at[s], block_send.at[lane, s], block_recv.at[block, s], {"cable": device}
        )

    def pass_on(s, lane, device):
        return remote(
            white0.at[s], white0.at[s], block_send.at[lane, s], block_recv.at[0, s], {"cable": device}
        )

    def arrived(block, s):
        own_to(block, s, 0, 0).wait_recv()

    def sent(s, lane):
        own_to(0, s, lane, 0).wait_send()

    def place(c):
        return c + mirrored * (bands - 1 - 2 * c)

    def results(c, source, sender, buffer, begin, low, high, device, lane):
        copies = {}
        for target in range(halves):
            top, end = max(low, target * kept), min(high, (target + 1) * kept)
            if top < end:
                copies[target] = remote(
                    buffer.at[c, :, top - begin : end - begin],
                    inbox.at[source, sender, c, :, top - target * kept : end - target * kept],
                    result_send.at[lane, target, c],
                    result_recv.at[source, sender, c],
                    {"cable": device, "pairs": target},
                )
        return copies

    def start_all(copies):
        for copy in copies.values():
            copy.start()

    def finish_all(copies):
        for copy in copies.values():
            copy.wait_send()

    one_pair = channels + points
    two_pairs = 2 * channels + points
    three_pairs = 3 * channels + points

    def near_from_1(c, sender=m):
        return results(c, 1, sender, near_out, channels, channels, one_pair, 0, 0)

    def near_from_1_all(c, sender=m):
        return results(c, 1, sender, near_out, channels, channels, three_pairs, 0, 0)

    def near_from_2(c, sender=m):
        return results(c, 2, sender, near_out, 2 * channels, 2 * channels, three_pairs, 0, 0)

    def near_from_3(c, sender=m):
        return results(c, 3, sender, near_out, channels, 3 * channels, three_pairs, 0, 0)

    def near_pair_23(c, sender=m):
        return results(c, 3, sender, far_out, channels, channels, one_pair, 2, 1)

    def far_from_2(c, sender=m):
        return results(c, 2, sender, far_out, channels, channels, three_pairs, 3, 1)

    def far_pair_01(c, source, sender=m):
        return results(c, source, sender, near_out, channels, channels, one_pair, 1, 0)

    def far_pair_02(c, source, sender=m):
        return results(c, source, sender, far_out, 2 * channels, 2 * channels, two_pairs, 2, 1)

    def far_pair_03(c, source, sender=m):
        return results(c, source, sender, far_out, channels, 3 * channels, three_pairs, 3, 2)

    def swap(c):
        rows = pl.ds(pl.multiple_of((1 - m) * kept, 8), kept)
        return remote(stack.at[c, :, rows], swapped.at[c], swap_send.at[c], swap_recv.at[c], partner)

    def load(q):
        near = pl.multiple_of(m * (half - EDGE), EDGE)
        begin = pl.multiple_of((1 - m) * EDGE, EDGE)
        rows = pl.ds(q * GROUP, GROUP)
        return pltpu.make_async_copy(
            spectra_ref.at[:, rows, :, pl.ds(near, half + EDGE)],
            x_ref.at[:, rows, :, pl.ds(begin, half + EDGE)],
            load_sem.at[q],
        )

    constants, top = [], 0
    for i, table in enumerate((window_ref, forward_ref, inverse_ref)):
        rows, columns = table.shape
        source = tables_ref.at[top : top + rows, :columns]
        constants.append(pltpu.make_async_copy(source, table, constant_sem.at[i]))
        top += rows

    edge_lanes = pl.ds(pl.multiple_of(m * (half + EDGE), EDGE), EDGE)

    def edge():
        source = pl.ds(pl.multiple_of((1 - m) * (bins - EDGE), EDGE), EDGE)
        return remote(
            spectra_ref.at[:, :, :, source],
            x_ref.at[:, :, :, edge_lanes],
            edge_send.at[0],
            edge_recv.at[0],
            {"bins": 1 - x},
        )

    def flags_to(source, device, lane):
        return remote(
            flag_ref, seen.at[source], flag_send.at[lane], flag_recv.at[source], {"cable": device}
        )

    load(0).start()
    constants[0].start()
    for q in range(1, groups):
        load(q).start()
    constants[1].start()
    constants[2].start()
    live = jnp.minimum(counts_ref[0], blocks - z)
    for offset in range(REACH + 1):
        flag_ref[offset : offset + 1, :] = jnp.full((1, BAND), owners_ref[offset].astype(F32))
        weight = jnp.where(offset < live, 1.0, 0.0)
        flag_ref[REACH + 1 + offset : REACH + 2 + offset, :] = jnp.full((1, BAND), weight)
    barrier = pltpu.get_barrier_semaphore()
    beside = jnp.where((z > 0) & (z < blocks - 1), 2, 1)

    def tell_beside(semaphore):
        @pl.when(z > 0)
        def _():
            pl.semaphore_signal(semaphore, inc=1, device_id={"cable": z - 1}, device_id_type=MESH)

        @pl.when(z < blocks - 1)
        def _():
            pl.semaphore_signal(semaphore, inc=1, device_id={"cable": z + 1}, device_id_type=MESH)

    tell_beside(barrier)
    pl.semaphore_signal(barrier, inc=1, device_id=partner, device_id_type=MESH)
    pl.semaphore_signal(barrier, inc=1, device_id={"bins": 1 - x}, device_id_type=MESH)
    sends_edge = x == m
    takes_edge = x != m

    def whiten(q, begin, count, store):
        lanes = pl.ds(pl.multiple_of(begin, BAND), count * BAND + 2 * EDGE)
        reals, imags, highs, lows = [], [], [], []
        for i in range(GROUP):
            real = x_ref[0, q * GROUP + i, :, lanes].astype(F32)
            imag = x_ref[1, q * GROUP + i, :, lanes].astype(F32)
            power = real * real + imag * imag
            high = power.astype(BF16)
            reals.append(real)
            imags.append(imag)
            highs.append(high)
            lows.append((power - high.astype(F32)).astype(BF16))
        high = jnp.concatenate(highs, axis=0)
        low = jnp.concatenate(lows, axis=0)
        for j in range(count):
            reach = slice(j * BAND, (j + 1) * BAND + 2 * EDGE)
            terms = jnp.concatenate([high[:, reach], low[:, reach]], axis=1)
            total = jnp.dot(terms, window_ref[...], preferred_element_type=F32)
            gain = lax.rsqrt(total / (2 * HALF_WIDTH + 1) + epsilon)
            here = slice(EDGE + j * BAND, EDGE + (j + 1) * BAND)
            slot = store(j) * groups + q
            for i in range(GROUP):
                rows = gain[i * channels : (i + 1) * channels]
                white[slot, i, :channels] = (reals[i][:, here] * rows).astype(BF16)
                white[slot, i, channels:] = (imags[i][:, here] * rows).astype(BF16)

    def whiten_inner(q):
        load(q).wait()
        whiten(q, mirrored * BAND, bands - 1, lambda j: j + mirrored * (bands - 2 - 2 * j))

    def send_inner(q):
        @pl.when(z == 0)
        def _():
            own_to(0, q + groups * m, 0, 1).start()

        @pl.when((z == 1) & second)
        def _():
            own_to(1, q, 1, 0).start()

        @pl.when(z == 2)
        def _():
            own_to(2, q, 1, 3).start()

        @pl.when(z == 3)
        def _():
            own_to(3, q + groups * (1 + m), 0, 2).start()

    def relay(i):
        s = i + groups * m
        arrived(0, s)
        pass_on(s, 0, 2).start()

    def relay_if(condition, i):
        @pl.when((z == 1) & condition)
        def _():
            relay(i)

    def send_range(block, begin, end, lane, device):
        @pl.loop(begin, end)
        def _(s):
            own_to(block, s, lane, device).start()

    constants[0].wait()
    whiten_inner(0)
    pl.semaphore_wait(barrier, beside + 2)
    tell_beside(known)

    @pl.when(sends_edge)
    def _():
        edge().start()

    send_inner(0)

    @pl.when(z == 0)
    def _():
        flags_to(0, 1, 0).start()

    @pl.when(z == 2)
    def _():
        flags_to(1, 3, 0).start()

    @pl.when(~takes_edge)
    def _():
        x_ref[:, :, :, edge_lanes] = jnp.zeros((2, windows, channels, EDGE), x_ref.dtype)

    def inner_step(q, carry):
        whiten_inner(q)
        send_inner(q)
        relay_if((q >= 3) & (lax.rem(q, 2) == 1), lax.div(q - 3, 2))
        return carry

    lax.fori_loop(1, groups // 2, inner_step, 0)
    pl.semaphore_wait(known, beside)
    tell_beside(spread)
    lax.fori_loop(groups // 2, groups, inner_step, 0)
    pl.semaphore_wait(spread, beside)

    @pl.when(z == 0)
    def _():
        for device in range(2, blocks):
            flags_to(0, device, device - 1).start()
        send_range(0, groups + groups * m, 3 * groups, 0, 1)

    @pl.when((z == 2) & second)
    def _():
        send_range(2, 0, groups, 0, 0)
        send_range(2, groups, 2 * groups, 1, 3)

    @pl.when((z == 3) & second)
    def _():
        send_range(3, 0, groups, 0, 0)

    @pl.when(takes_edge)
    def _():
        edge().wait_recv()

    def last_step(q, carry):
        whiten(q, (1 - mirrored) * (bands - 1) * BAND, 1, lambda j: bands - 1)
        s = (bands - 1) * groups + q

        @pl.when(z == 0)
        def _():
            own_to(0, s, 0, 1).start()

        @pl.when((z == 2) & first)
        def _():
            own_to(2, s, 0, 1).start()
            own_to(2, s, 1, 3).start()

        @pl.when(z == 3)
        def _():
            own_to(3, s, 0, 1 + m).start()

        relay_if(lax.rem(q, 4) == 3, 3 + lax.div(q, 4))
        return carry

    lax.fori_loop(0, groups, last_step, 0)

    @pl.when((z == 3) & first)
    def _():
        send_range(3, 2 * groups, 3 * groups, 0, 2)

    constants[1].wait()
    constants[2].wait()

    def transform(buffer, s):
        wide = jnp.concatenate([buffer[s, i] for i in range(GROUP)], axis=1)
        return jnp.dot(forward_ref[...], jnp.concatenate([wide, wide], axis=0), preferred_element_type=F32)

    tile = 32

    def power_into(total, s):
        for k in range(0, points, tile):
            gained = total[k : k + tile]
            for i in range(GROUP):
                lanes = slice(i * BAND, (i + 1) * BAND)
                real = spec[s, k : k + tile, lanes]
                imag = spec[s, points + k : points + k + tile, lanes]
                gained = gained + (real * real + imag * imag)
            total[k : k + tile] = gained

    def cross_into(total, near, far):
        for k in range(0, points, tile):
            gained_real = total[k : k + tile]
            gained_imag = total[points + k : points + k + tile]
            for i in range(GROUP):
                lanes = slice(i * BAND, (i + 1) * BAND)
                near_real = near[k : k + tile, lanes]
                near_imag = near[points + k : points + k + tile, lanes]
                far_real = far[k : k + tile, lanes]
                far_imag = far[points + k : points + k + tile, lanes]
                gained_real = gained_real + (near_real * far_real + near_imag * far_imag)
                gained_imag = gained_imag + (near_imag * far_real - near_real * far_imag)
            total[k : k + tile] = gained_real
            total[points + k : points + k + tile] = gained_imag

    def lags_of(values, columns):
        high = values.astype(BF16)
        low = (values - high.astype(F32)).astype(BF16)
        table = inverse_ref[:, :columns]
        rest = inverse_ref[:, 2 * points : 2 * points + columns]
        return jnp.dot(
            jnp.concatenate([table, rest, table], axis=1),
            jnp.concatenate([high, high, low], axis=0),
            preferred_element_type=F32,
        )

    def lags_of_many(*totals):
        both = lags_of(jnp.concatenate([total[...] for total in totals], axis=1), 2 * points)
        return [both[:, i * BAND : (i + 1) * BAND] for i in range(len(totals))]

    def add_piece(c, begin, piece):
        rows = pl.ds(begin, points)
        stack[c, 0, rows] += piece[:points]
        stack[c, 1, rows] += piece[points:]

    def clear(*totals):
        for total in totals:
            total[...] = jnp.zeros_like(total)

    def over_windows(step):
        def body(q, carry):
            step(q)
            return carry

        lax.fori_loop(0, groups, body, 0)

    def over_bands(begin, end, band):
        def body(c, carry):
            band(c)
            return carry

        lax.fori_loop(begin, end, body, 0)

    def own_band(c):
        clear(sums_a)

        def step(q):
            s = c * groups + q
            spec[s] = transform(white, s)
            power_into(sums_a, s)

        over_windows(step)
        stack[c] = jnp.zeros(stack.shape[1:], F32)
        add_piece(c, 0, flag_ref[REACH + 1 : REACH + 2, :] * lags_of(sums_a[:points], points))
        relay_if(c >= 0, EARLY - bands + c)

    over_bands(0, bands, own_band)

    def owner_of(flags, offset):
        return flags[offset : offset + 1, :]

    def far_share(flags, offset):
        return owner_of(flags, offset) * flags[REACH + 1 + offset : REACH + 2 + offset, :]

    def near_share(flags, offset):
        return (1.0 - owner_of(flags, offset)) * flags[REACH + 1 + offset : REACH + 2 + offset, :]

    def store_rows(buffer, c, begin, piece, rows=slice(0, 2 * channels)):
        count = rows.stop - rows.start
        for part in range(2):
            top = part * points
            buffer[c, part, begin : begin + count] = piece[top + rows.start : top + rows.stop].astype(buffer.dtype)

    def store_sums(buffer, c, parts):
        for part in range(2):
            top = part * points
            for k in range(len(parts) + 1):
                terms = []
                if k < len(parts):
                    terms.append(parts[k][top : top + channels])
                if k > 0:
                    terms.append(parts[k - 1][top + channels : top + points])
                total = terms[0] if len(terms) == 1 else terms[0] + terms[1]
                buffer[c, part, k * channels : (k + 1) * channels] = total.astype(buffer.dtype)

    zero_flags, two_flags = seen.at[0], seen.at[1]

    @pl.when(z == 0)
    def _():
        @pl.when(second)
        def _():
            clear(sums_a, sums_b, sums_c)

            def step(q):
                for block, total, held in ((1, sums_a, one), (2, sums_b, two), (3, sums_c, three)):
                    arrived(block, q)
                    held[...] = transform(received[block], q)
                    cross_into(total, spec.at[q], held)

            over_windows(step)
            pairs = lags_of_many(sums_a, sums_b, sums_c)
            for offset in range(1, REACH + 1):
                add_piece(0, offset * channels, near_share(flag_ref, offset) * pairs[offset - 1])
            store_rows(near_out, 0, 0, far_share(flag_ref, 1) * pairs[0])
            store_rows(far_out, 0, 0, far_share(flag_ref, 2) * pairs[1])
            store_rows(far_out, 0, points, far_share(flag_ref, 3) * pairs[2])

        @pl.loop(0, bands)
        def _(c):
            swap(c).start()

        @pl.when(first)
        def _():
            sent(pieces - 1, 0)
            pl.semaphore_signal(drained, inc=1, device_id=partner, device_id_type=MESH)

        @pl.when(second)
        def _():
            pl.semaphore_wait(drained, 1)
            start_all(far_pair_03(0, 0))
            start_all(far_pair_02(0, 0))
            start_all(far_pair_01(0, 0))

    @pl.when(z == 1)
    def _():
        flags_to(0, 1, 0).wait_recv()

        @pl.when(second)
        def _():
            swap(0).start()

        def band(c):
            clear(sums_a)

            def step(q):
                s = c * groups + q
                i = s - groups * m

                @pl.when(i + EARLY < 3 * groups)
                def _():
                    relay(i + EARLY)

                one[...] = transform(white0, s)
                cross_into(sums_a, one, spec.at[s])

                @pl.when(first & (c == bands - 2))
                def _():
                    late = (bands - 1) * groups + q
                    arrived(2, late)
                    spec[q] = transform(white2, late)
                    arrived(3, late)
                    spec[groups + q] = transform(white3, late)

            over_windows(step)
            piece = lags_of(sums_a[...], 2 * points)
            store_rows(near_out, c, 0, near_share(zero_flags, 1) * piece)
            start_all(near_from_1(c))
            add_piece(c, channels, far_share(zero_flags, 1) * piece)
            swap(c).start()

        over_bands(m, m + bands - 1, band)

        @pl.when(first)
        def _():
            c = bands - 1
            clear(sums_a, sums_b, sums_c)

            def step(q):
                s = c * groups + q
                arrived(0, s)
                one[...] = transform(white0, s)
                cross_into(sums_a, one, spec.at[s])
                cross_into(sums_b, one, spec.at[q])
                cross_into(sums_c, one, spec.at[groups + q])

            over_windows(step)
            pairs = lags_of_many(sums_a, sums_b, sums_c)
            store_sums(near_out, c, [near_share(zero_flags, o) * pairs[o - 1] for o in range(1, REACH + 1)])
            start_all(near_from_1_all(c))
            store_rows(far_out, c, points, far_share(zero_flags, 3) * pairs[2])
            start_all(far_pair_03(c, 1))
            store_rows(far_out, c, 0, far_share(zero_flags, 2) * pairs[1])
            start_all(far_pair_02(c, 1))
            add_piece(c, channels, far_share(zero_flags, 1) * pairs[0])
            swap(c).start()

    @pl.when(z == 2)
    def _():
        flags_to(0, 2, 0).wait_recv()

        @pl.when(first)
        def _():
            swap(bands - 1).start()

        @pl.when(second)
        def _():
            swap(0).start()

        clear(sums_a)

        def early_step(q):
            s = m * groups + q
            arrived(0, s)
            pass_on(s, 2, 3).start()
            one[...] = transform(white0, s)
            cross_into(sums_a, one, spec.at[s])

        over_windows(early_step)
        piece = lags_of(sums_a[...], 2 * points)
        store_rows(near_out, m, 0, near_share(zero_flags, 2) * piece)
        near_out[m, :, points : points + channels] = jnp.zeros((2, channels, BAND), near_out.dtype)
        start_all(near_from_2(m))
        add_piece(m, 2 * channels, far_share(zero_flags, 2) * piece)
        swap(m).start()

        def band(c):
            clear(sums_a, sums_b, sums_c)

            def step(q):
                s = c * groups + q
                arrived(3, s)
                three[...] = transform(white3, s)
                cross_into(sums_b, spec.at[s], three)

                @pl.when(q == groups - 1)
                def _():
                    sums_b[...] = lags_of(sums_b[...], 2 * points)

                arrived(0, s)
                one[...] = transform(white0, s)
                cross_into(sums_a, one, spec.at[s])
                cross_into(sums_c, one, three)

            over_windows(step)
            near, beyond = lags_of_many(sums_a, sums_c)
            store_sums(near_out, c, [near_share(zero_flags, 2) * near, near_share(zero_flags, 3) * beyond])
            start_all(near_from_2(c))
            ahead = sums_b[...]
            store_rows(far_out, c, 0, far_share(flag_ref, 1) * ahead)
            store_rows(far_out, c, points, far_share(zero_flags, 3) * beyond)
            start_all(far_from_2(c))
            add_piece(c, 2 * channels, far_share(zero_flags, 2) * near)
            add_piece(c, channels, near_share(flag_ref, 1) * ahead)
            swap(c).start()

        over_bands(1 + m, bands - 1 + m, band)

    @pl.when(z == 3)
    def _():
        flags_to(0, 3, 0).wait_recv()
        flags_to(1, 3, 0).wait_recv()

        @pl.loop(1 + m, bands - 1 + m)
        def _(c):
            swap(c).start()

        def band(c):
            clear(sums_a)

            def step(q):
                s = c * groups + q
                arrived(2, s)
                two[...] = transform(white2, s)
                cross_into(sums_a, two, spec.at[s])

            over_windows(step)
            piece = lags_of(sums_a[...], 2 * points)
            store_rows(far_out, c, 0, near_share(two_flags, 1) * piece)
            start_all(near_pair_23(c))
            add_piece(c, channels, far_share(two_flags, 1) * piece)

            @pl.when(c == m)
            def _():
                clear(sums_c)

                def late_step(q):
                    s = c * groups + q
                    arrived(0, s)
                    one[...] = transform(white0, s)
                    cross_into(sums_c, one, spec.at[s])

                over_windows(late_step)
                distant = lags_of(sums_c[...], 2 * points)
                store_rows(near_out, c, points, near_share(zero_flags, 3) * distant)
                start_all(near_from_3(c))
                add_piece(c, 3 * channels, far_share(zero_flags, 3) * distant)

            swap(c).start()

        over_bands(0, 2, lambda i: band(i * (bands - 1 - (bands - 2) * m)))

    def lanes_of(core, c):
        return pl.ds(pl.multiple_of(core * half + place(c) * BAND, BAND), BAND)

    def collect(c):
        out_ref[:, :, lanes_of(m, c)] = stack[c, :, pl.ds(pl.multiple_of(m * kept, 8), kept)]
        swap(c).wait_recv()
        out_ref[:, :, lanes_of(1 - m, c)] = swapped[c]
        swap(c).wait_send()

    over_bands(0, bands, collect)

    def take(target, c, source, sender, low, high):
        top, end = max(low, target * kept), min(high, (target + 1) * kept)
        if top < end:
            rows = slice(top - target * kept, end - target * kept)
            results(c, source, sender, near_out, low, low, high, 0, 0)[target].wait_recv()
            out_ref[:, rows, lanes_of(sender, c)] += inbox[source, sender, c, :, rows].astype(F32)

    def take_at_0(target):
        for sender in range(halves):
            def band(c):
                take(target, c, 1, sender, channels, one_pair)
                take(target, c, 2, sender, 2 * channels, three_pairs)

            over_bands(sender, sender + bands - 1, band)
            take(target, sender, 3, sender, 3 * channels, three_pairs)
        take(target, bands - 1, 1, 0, channels, three_pairs)

    def take_at_1(target):
        take(target, 0, 0, 1, channels, one_pair)

    def take_at_2(target):
        take(target, 0, 0, 1, 2 * channels, two_pairs)
        take(target, 0, 3, 1, channels, one_pair)
        take(target, 1, 3, 1, channels, one_pair)
        take(target, 0, 3, 0, channels, one_pair)
        take(target, bands - 1, 3, 0, channels, one_pair)
        take(target, bands - 1, 1, 0, 2 * channels, two_pairs)

    def take_at_3(target):
        take(target, 0, 0, 1, 3 * channels, three_pairs)
        for sender in range(halves):
            def band(c):
                take(target, c, 2, sender, channels, three_pairs)

            over_bands(1 + sender, bands - 1 + sender, band)
        take(target, bands - 1, 1, 0, 3 * channels, three_pairs)

    for block, step in enumerate((take_at_0, take_at_1, take_at_2, take_at_3)):
        for target in range(halves):
            @pl.when((z == block) & (m == target))
            def _():
                step(target)

    @pl.when(sends_edge)
    def _():
        edge().wait_send()

    def sent_range(begin, end, lane):
        @pl.loop(begin, end)
        def _(s):
            sent(s, lane)

    @pl.when(z == 0)
    def _():
        for device in range(1, blocks):
            flags_to(0, device, device - 1).wait_send()
        sent_range(groups * m, pieces - 1 + m, 0)

        @pl.when(second)
        def _():
            finish_all(far_pair_01(0, 0))
            finish_all(far_pair_02(0, 0))
            finish_all(far_pair_03(0, 0))

    @pl.when(z == 1)
    def _():
        sent_range(groups * m, groups * m + 3 * groups, 0)
        over_bands(m, m + bands - 1, lambda c: finish_all(near_from_1(c)))

        @pl.when(second)
        def _():
            sent_range(0, groups, 1)

        @pl.when(first)
        def _():
            finish_all(near_from_1_all(bands - 1))
            finish_all(far_pair_03(bands - 1, 1))
            finish_all(far_pair_02(bands - 1, 1))

    @pl.when(z == 2)
    def _():
        flags_to(1, 3, 0).wait_send()

        @pl.when(first)
        def _():
            sent_range((bands - 1) * groups, pieces, 0)
            sent_range((bands - 1) * groups, pieces, 1)

        @pl.when(second)
        def _():
            sent_range(0, groups, 0)

        sent_range(0, groups + groups * m, 1)
        sent_range(groups * m, groups + groups * m, 2)
        finish_all(near_from_2(m))

        def band(c):
            finish_all(near_from_2(c))
            finish_all(far_from_2(c))

        over_bands(1 + m, bands - 1 + m, band)

    @pl.when(z == 3)
    def _():
        @pl.when(first)
        def _():
            sent_range(groups, pieces, 0)
            finish_all(near_pair_23(bands - 1))

        @pl.when(second)
        def _():
            sent_range(0, groups, 0)
            sent_range(2 * groups, pieces, 0)
            finish_all(near_pair_23(0))

        finish_all(near_pair_23(m))
        finish_all(near_from_3(m))


def four_block_shards(spectra, counts, owners):
    parts, windows, channels, bins = spectra.shape
    halves, blocks = lax.axis_size("pairs"), lax.axis_size("cable")
    half, points = bins // halves, 2 * channels
    forward, inverse = channel_transforms(channels, 1.0 / math.sqrt(windows * channels))
    window = smoothing_window()
    bands, groups = half // BAND, windows // GROUP
    pieces = bands * groups
    rows = (REACH + 2) * channels
    kept = rows // halves
    block = pltpu.VMEM((pieces, GROUP, points, BAND), BF16)
    spectrum = pltpu.VMEM((2 * points, GROUP * BAND), F32)
    sums = pltpu.VMEM((2 * points, BAND), F32)
    shares = pltpu.VMEM((bands, 2, 2 * points, BAND), BF16)
    flags = (2 * (REACH + 1), BAND)
    dma = pltpu.SemaphoreType.DMA
    width = inverse.shape[1]
    tables = np.zeros((TABLE_ROWS, width), jnp.bfloat16)
    top = 0
    for table in (window, forward, inverse):
        tables[top : top + table.shape[0], : table.shape[1]] = table
        top += table.shape[0]
    hbm = pl.BlockSpec(memory_space=pl.ANY)
    smem = pl.BlockSpec(memory_space=pltpu.SMEM)
    out = pl.pallas_call(
        stack_kernel,
        out_shape=jax.ShapeDtypeStruct((2, kept, bins), F32),
        in_specs=[hbm, smem, smem, hbm],
        out_specs=pl.BlockSpec(memory_space=pltpu.VMEM),
        scratch_shapes=[
            pltpu.VMEM((2, windows, channels, half + 2 * EDGE), BF16),
            pltpu.VMEM(window.shape, BF16),
            pltpu.VMEM(forward.shape, BF16),
            pltpu.VMEM(inverse.shape, BF16),
            pltpu.VMEM(flags, F32),
            pltpu.VMEM((2,) + flags, F32),
            block, block, block, block, block,
            pltpu.VMEM((pieces, 2 * points, GROUP * BAND), F32),
            spectrum, spectrum, spectrum, sums, sums, sums,
            pltpu.VMEM((bands, 2, rows, BAND), F32),
            shares, shares,
            pltpu.VMEM((blocks, halves, bands, 2, kept, BAND), BF16),
            pltpu.VMEM((bands, 2, kept, BAND), F32),
            dma((groups,)), dma((3,)), dma((1,)), dma((1,)), dma((3,)), dma((2,)),
            dma((3, pieces)), dma((blocks, pieces)),
            dma((3, halves, bands)), dma((blocks, halves, bands)),
            dma((bands,)), dma((bands,)),
            pltpu.SemaphoreType.REGULAR, pltpu.SemaphoreType.REGULAR, pltpu.SemaphoreType.REGULAR,
        ],
        compiler_params=pltpu.CompilerParams(
            collective_id=0, has_side_effects=True, vmem_limit_bytes=55000000
        ),
    )(spectra, counts, owners.reshape(-1), jnp.asarray(tables))
    return out[:, None]


def solution(mesh):
    sizes = dict(mesh.shape)
    fits = sizes["cable"] == REACH + 1 and sizes["pairs"] == 2 and sizes["bins"] == 2
    shards = four_block_shards if fits else general_shards
    placed = (
        P("groups", None, "cable", "bins"),
        P(("groups", "cable")),
        P(("groups", "cable"), None),
    )
    return jax.shard_map(
        shards,
        mesh=mesh,
        in_specs=placed,
        out_specs=P("groups", "cable", "pairs", "bins"),
        check_vma=False,
    )
```

```python
import math

import jax
import jax.numpy as jnp
import numpy as np
from jax import lax
from jax.experimental import pallas as pl
from jax.experimental.pallas import tpu as pltpu
from jax.sharding import PartitionSpec as P

REACH = 3
HALF_WIDTH = 32


epsilon = 1e-06
band_rows = 16


def with_halo(x, sides, width):
    for axis, dim in sides:
        count, length = (lax.axis_size(axis), x.shape[dim])
        up = [(i, (i + 1) % count) for i in range(count - 1)]
        down = [(j, i) for i, j in up]
        last = lax.slice_in_dim(x, length - width, length, axis=dim)
        first = lax.slice_in_dim(x, 0, width, axis=dim)
        before = lax.ppermute(last, axis, up)
        after = lax.ppermute(first, axis, down)
        x = jnp.concatenate([before, x, after], axis=dim)
    return x


def from_behind(block, axis, distance):
    devices = range(lax.axis_size(axis))
    route = [(i - distance, i) for i in devices if i - distance in devices]
    return lax.ppermute(block, axis, route)


def whiten_rows(spectra):
    real_part = spectra[0].astype(jnp.float32)
    imag_part = spectra[1].astype(jnp.float32)
    power_sum = real_part * real_part + imag_part * imag_part
    padded = with_halo(power_sum, (("bins", 2),), HALF_WIDTH)
    window_len = 2 * HALF_WIDTH + 1
    window_sum = lax.reduce_window(
        padded, jnp.zeros((), padded.dtype), lax.add, (1, 1, window_len), (1, 1, 1), "VALID"
    )
    inverse_amp = lax.rsqrt(window_sum / window_len + epsilon)
    return jnp.stack(
        [
            (real_part * inverse_amp).astype(jnp.bfloat16),
            (imag_part * inverse_amp).astype(jnp.bfloat16),
        ]
    )


def make_lag_table(col_count):
    flattened = jnp.arange(band_rows * col_count)
    row_of = flattened // col_count
    col_of = flattened % col_count
    lag_lanes = jnp.arange(col_count + band_rows - 1)
    return (lag_lanes[None, :] == (col_of - row_of + band_rows - 1)[:, None]).astype(jnp.bfloat16)


def lag_stack(pair_block, lag_table):
    freq_count, row_count, col_count = pair_block.shape
    group_count = row_count // band_rows
    grouped = pair_block.reshape(freq_count, group_count, band_rows * col_count)
    banded = jnp.einsum("fgk,ku->fgu", grouped, lag_table, preferred_element_type=jnp.float32)
    lag_sums = jnp.zeros((freq_count, col_count + row_count - 1), jnp.float32)
    for row_group in range(group_count):
        first_lag = row_count - band_rows * (row_group + 1)
        lag_sums = lag_sums.at[:, first_lag : first_lag + col_count + band_rows - 1].add(
            banded[:, row_group]
        )
    return lag_sums.T


def correlate(left_rows, right_rows, factor, lag_table):
    left_real = jnp.concatenate([left_rows[0], left_rows[1]], axis=0)
    left_imag = jnp.concatenate([left_rows[1], -left_rows[0]], axis=0)
    right_both = jnp.concatenate([right_rows[0], right_rows[1]], axis=0)
    corr_real = (
        jnp.einsum("wif,wjf->fij", left_real, right_both, preferred_element_type=jnp.float32)
        * factor
    ).astype(jnp.bfloat16)
    corr_imag = (
        jnp.einsum("wif,wjf->fij", left_imag, right_both, preferred_element_type=jnp.float32)
        * factor
    ).astype(jnp.bfloat16)
    return jnp.stack([lag_stack(corr_real, lag_table), lag_stack(corr_imag, lag_table)])


def general_shards(spectra, counts, owners):
    pair_devs = lax.axis_size("pairs")
    member = lax.axis_index("pairs")
    channels = spectra.shape[2]
    half_rows = channels // pair_devs
    source = whiten_rows(spectra)
    receiver = lax.dynamic_slice_in_dim(source, member * half_rows, half_rows, 2)
    block_count = lax.axis_size("cable")
    cable_index = lax.axis_index("cable")
    live_count = jnp.minimum(counts[0], block_count - cable_index)
    panels = {0: receiver}
    for offset in range(1, REACH + 1):
        panels[offset] = from_behind(receiver, "cable", -offset)
    factor = 1.0 / math.sqrt(source.shape[1] * channels)
    lag_table = make_lag_table(half_rows)
    freq_count = source.shape[3]
    stacks = jnp.zeros((2, (REACH + 2) * channels, freq_count), jnp.float32)
    for offset in range(REACH + 1):
        lag_piece = correlate(source, panels[offset], factor, lag_table)
        weight = (offset < live_count).astype(jnp.float32)
        if offset == 0:
            kept_here = weight * lag_piece
        else:
            sent_away = owners[0, offset].astype(jnp.float32)
            arrived = from_behind(weight * sent_away * lag_piece, "cable", offset)
            kept_here = weight * (1.0 - sent_away) * lag_piece + arrived
        first_lag = offset * channels + member * half_rows
        current = lax.dynamic_slice_in_dim(stacks, first_lag, kept_here.shape[1], 1)
        stacks = lax.dynamic_update_slice_in_dim(stacks, current + kept_here, first_lag, 1)
    summed = lax.psum_scatter(stacks, "pairs", scatter_dimension=1, tiled=True)
    return summed[:, None]


EDGE = 128
BAND = 128
GROUP = 2
EARLY = 9
CATCH_UP = 14
TABLE_ROWS = 2048
F32 = jnp.float32
BF16 = jnp.bfloat16
MESH = pl.DeviceIdType.MESH


def channel_transforms(channels, factor):
    points = 2 * channels
    index = np.arange(points)
    angle = 2 * np.pi * np.outer(index, np.arange(channels)) / points
    cos, sin = np.cos(angle), np.sin(angle)
    forward = split_high_low(np.block([[cos, sin], [-sin, cos]]))
    angle = 2 * np.pi * np.outer(index - (channels - 1), index) / points
    cos, sin = np.cos(angle), np.sin(angle)
    cos[-1], sin[-1] = 0.0, 0.0
    inverse = split_high_low(np.block([[cos, sin], [-sin, cos]]) * (factor / points))
    return forward, inverse


def split_high_low(full):
    high = full.astype(jnp.bfloat16)
    low = (full - high.astype(np.float64)).astype(jnp.bfloat16)
    return np.concatenate([high, low], axis=1)


def smoothing_window():
    distance = np.arange(BAND + 2 * EDGE)[:, None] - (np.arange(BAND)[None, :] + EDGE)
    ones = (np.abs(distance) <= HALF_WIDTH).astype(jnp.bfloat16)
    return np.concatenate([ones, ones], axis=0)


def stack_kernel(
    spectra_ref, counts_ref, owners_hbm, tables_ref, out_ref,
    owners_ref,
    x_ref, window_ref, forward_ref, inverse_ref, flag_ref, seen,
    white, white0, white1, white2, white3, spec, one, two, three, sums_a, sums_b, sums_c,
    stack, near_out, far_out, inbox, swapped,
    load_sem, constant_sem, edge_send, edge_recv, flag_send, flag_recv,
    block_send, block_recv, result_send, result_recv, swap_send, swap_recv, known, spread, drained,
):
    windows, channels = x_ref.shape[1:3]
    half = x_ref.shape[3] - 2 * EDGE
    bands, groups = half // BAND, windows // GROUP
    pieces = bands * groups
    points = 2 * channels
    kept = out_ref.shape[1]
    blocks, halves = lax.axis_size("cable"), lax.axis_size("pairs")
    z, m = lax.axis_index("cable"), lax.axis_index("pairs")
    cuts, x = lax.axis_size("bins"), lax.axis_index("bins")
    bins = spectra_ref.shape[3]
    first = m == 0
    second = m == 1
    mirrored = x
    partner = {"pairs": 1 - m}

    def remote(source, target, send, recv, device):
        return pltpu.make_async_remote_copy(
            src_ref=source, dst_ref=target, send_sem=send, recv_sem=recv, device_id=device, device_id_type=MESH
        )

    received = (white0, white1, white2, white3)

    def own_to(block, s, lane, device):
        return remote(
            white.at[s], received[block].at[s], block_send.at[lane, s], block_recv.at[block, s], {"cable": device}
        )

    def pass_on(s, lane, device):
        return remote(
            white0.at[s], white0.at[s], block_send.at[lane, s], block_recv.at[0, s], {"cable": device}
        )

    def arrived(block, s):
        own_to(block, s, 0, 0).wait_recv()

    def sent(s, lane):
        own_to(0, s, lane, 0).wait_send()

    def place(c):
        return c + mirrored * (bands - 1 - 2 * c)

    def results(c, source, sender, buffer, begin, low, high, device, lane):
        copies = {}
        for target in range(halves):
            top, end = max(low, target * kept), min(high, (target + 1) * kept)
            if top < end:
                copies[target] = remote(
                    buffer.at[c, :, top - begin : end - begin],
                    inbox.at[source, sender, c, :, top - target * kept : end - target * kept],
                    result_send.at[lane, target, c],
                    result_recv.at[source, sender, c],
                    {"cable": device, "pairs": target},
                )
        return copies

    def start_all(copies):
        for copy in copies.values():
            copy.start()

    def finish_all(copies):
        for copy in copies.values():
            copy.wait_send()

    one_pair = channels + points
    two_pairs = 2 * channels + points
    three_pairs = 3 * channels + points

    def near_from_1(c, sender=m):
        return results(c, 1, sender, near_out, channels, channels, one_pair, 0, 0)

    def near_from_1_all(c, sender=m):
        return results(c, 1, sender, near_out, channels, channels, three_pairs, 0, 0)

    def near_from_2(c, sender=m):
        return results(c, 2, sender, near_out, 2 * channels, 2 * channels, three_pairs, 0, 0)

    def near_from_3(c, sender=m):
        return results(c, 3, sender, near_out, channels, 3 * channels, three_pairs, 0, 0)

    def near_pair_23(c, sender=m):
        return results(c, 3, sender, far_out, channels, channels, one_pair, 2, 1)

    def far_from_2(c, sender=m):
        return results(c, 2, sender, far_out, channels, channels, three_pairs, 3, 1)

    def far_pair_01(c, source, sender=m):
        return results(c, source, sender, near_out, channels, channels, one_pair, 1, 0)

    def far_pair_02(c, source, sender=m):
        return results(c, source, sender, far_out, 2 * channels, 2 * channels, two_pairs, 2, 1)

    def far_pair_03(c, source, sender=m):
        return results(c, source, sender, far_out, channels, 3 * channels, three_pairs, 3, 2)

    def swap(c):
        rows = pl.ds(pl.multiple_of((1 - m) * kept, 8), kept)
        return remote(stack.at[c, :, rows], swapped.at[c], swap_send.at[c], swap_recv.at[c], partner)

    def load(q):
        near = pl.multiple_of(m * (half - EDGE), EDGE)
        begin = pl.multiple_of((1 - m) * EDGE, EDGE)
        rows = pl.ds(q * GROUP, GROUP)
        return pltpu.make_async_copy(
            spectra_ref.at[:, rows, :, pl.ds(near, half + EDGE)],
            x_ref.at[:, rows, :, pl.ds(begin, half + EDGE)],
            load_sem.at[q],
        )

    constants, top = [], 0
    for i, table in enumerate((window_ref, forward_ref, inverse_ref)):
        rows, columns = table.shape
        source = tables_ref.at[top : top + rows, :columns]
        constants.append(pltpu.make_async_copy(source, table, constant_sem.at[i]))
        top += rows

    def edge_lanes(core):
        return pl.ds(pl.multiple_of(core * (half + EDGE), EDGE), EDGE)

    def edge(q):
        begin = EDGE + (1 - x) * (half - EDGE)
        rows = pl.ds(q * GROUP, GROUP)
        return remote(
            x_ref.at[:, rows, :, pl.ds(pl.multiple_of(begin, EDGE), EDGE)],
            x_ref.at[:, rows, :, edge_lanes(x)],
            edge_send.at[q],
            edge_recv.at[q],
            {"bins": 1 - x, "pairs": x},
        )

    def flags_to(source, device, lane):
        return remote(
            flag_ref, seen.at[source], flag_send.at[lane], flag_recv.at[source], {"cable": device}
        )

    load(0).start()
    constants[0].start()
    settings = pltpu.make_async_copy(owners_hbm, owners_ref, flag_send.at[0])
    settings.start()
    for q in range(1, groups):
        load(q).start()
    constants[1].start()
    constants[2].start()
    barrier = pltpu.get_barrier_semaphore()
    beside = jnp.where((z > 0) & (z < blocks - 1), 2, 1)

    def tell_beside(semaphore):
        @pl.when(z > 0)
        def _():
            pl.semaphore_signal(semaphore, inc=1, device_id={"cable": z - 1}, device_id_type=MESH)

        @pl.when(z < blocks - 1)
        def _():
            pl.semaphore_signal(semaphore, inc=1, device_id={"cable": z + 1}, device_id_type=MESH)

    tell_beside(barrier)
    pl.semaphore_signal(barrier, inc=1, device_id=partner, device_id_type=MESH)
    at_cut = x != m

    @pl.when(at_cut)
    def _():
        pl.semaphore_signal(barrier, inc=1, device_id={"bins": 1 - x, "pairs": x}, device_id_type=MESH)

    def whiten(q, begin, count, store):
        lanes = pl.ds(pl.multiple_of(begin, BAND), count * BAND + 2 * EDGE)
        reals, imags, highs, lows = [], [], [], []
        for i in range(GROUP):
            real = x_ref[0, q * GROUP + i, :, lanes].astype(F32)
            imag = x_ref[1, q * GROUP + i, :, lanes].astype(F32)
            power = real * real + imag * imag
            high = power.astype(BF16)
            reals.append(real)
            imags.append(imag)
            highs.append(high)
            lows.append((power - high.astype(F32)).astype(BF16))
        high = jnp.concatenate(highs, axis=0)
        low = jnp.concatenate(lows, axis=0)
        for j in range(count):
            reach = slice(j * BAND, (j + 1) * BAND + 2 * EDGE)
            terms = jnp.concatenate([high[:, reach], low[:, reach]], axis=1)
            total = jnp.dot(terms, window_ref[...], preferred_element_type=F32)
            gain = lax.rsqrt(total / (2 * HALF_WIDTH + 1) + epsilon)
            here = slice(EDGE + j * BAND, EDGE + (j + 1) * BAND)
            slot = store(j) * groups + q
            for i in range(GROUP):
                rows = gain[i * channels : (i + 1) * channels]
                white[slot, i, :channels] = (reals[i][:, here] * rows).astype(BF16)
                white[slot, i, channels:] = (imags[i][:, here] * rows).astype(BF16)

    def whiten_inner(q):
        whiten(q, mirrored * BAND, bands - 1, lambda j: j + mirrored * (bands - 2 - 2 * j))

    def send_edge(q):
        @pl.when(at_cut)
        def _():
            edge(q).start()

    def send_first(q):
        @pl.when(z == 0)
        def _():
            own_to(0, q, 0, 1).start()

    def send_inner(q):
        @pl.when((z == 1) & second)
        def _():
            own_to(1, q + 2 * groups, 1, 0).start()

        @pl.when(z == 2)
        def _():
            own_to(2, q, 1, 3).start()

        @pl.when(z == 3)
        def _():
            own_to(3, q + groups, 0, 2).start()

    def relay(i):
        s = i + groups * m * lax.div(i, 2 * groups)
        arrived(0, s)
        pass_on(s, 0, 2).start()

    def relay_if(condition, i):
        @pl.when((z == 1) & condition)
        def _():
            relay(i)

    def send_range(block, begin, end, lane, device):
        @pl.loop(begin, end)
        def _(s):
            own_to(block, s, lane, device).start()

    constants[0].wait()
    load(0).wait()
    whiten(0, mirrored * (bands - 1) * BAND, 1, lambda j: 0)
    pl.semaphore_wait(barrier, beside + 1 + jnp.where(at_cut, 1, 0))
    send_first(0)
    send_edge(0)
    tell_beside(known)
    whiten(0, BAND, bands - 2, lambda j: 1 + j + mirrored * (bands - 3 - 2 * j))
    send_inner(0)

    settings.wait()
    live = jnp.minimum(counts_ref[0], blocks - z)
    for offset in range(REACH + 1):
        flag_ref[offset : offset + 1, :] = jnp.full((1, BAND), owners_ref[0, offset].astype(F32))
        weight = jnp.where(offset < live, 1.0, 0.0)
        flag_ref[REACH + 1 + offset : REACH + 2 + offset, :] = jnp.full((1, BAND), weight)

    @pl.when(z == 0)
    def _():
        flags_to(0, 1, 0).start()

    @pl.when(z == 2)
    def _():
        flags_to(1, 3, 0).start()

    @pl.when(~at_cut)
    def _():
        x_ref[:, :, :, edge_lanes(m)] = jnp.zeros((2, windows, channels, EDGE), x_ref.dtype)

    def inner_step(q, carry):
        load(q).wait()
        send_edge(q)
        whiten_inner(q)
        send_first(q)
        send_inner(q)
        relay_if((q >= 3) & (lax.rem(q, 2) == 1), lax.div(q - 3, 2))
        return carry

    lax.fori_loop(1, groups // 2, inner_step, 0)
    pl.semaphore_wait(known, beside)
    tell_beside(spread)
    lax.fori_loop(groups // 2, groups, inner_step, 0)
    pl.semaphore_wait(spread, beside)

    @pl.when(z == 0)
    def _():
        for device in range(2, blocks):
            flags_to(0, device, device - 1).start()
        send_range(0, groups, (3 - m) * groups, 0, 1)

    @pl.when((z == 2) & second)
    def _():
        send_range(2, 2 * groups, 3 * groups, 0, 0)
        send_range(2, 2 * groups, 3 * groups, 1, 3)

    @pl.when((z == 3) & second)
    def _():
        send_range(3, 2 * groups, 3 * groups, 0, 0)

    constants[1].wait()
    constants[2].wait()

    def transform(buffer, s):
        wide = jnp.concatenate([buffer[s, i] for i in range(GROUP)], axis=1)
        return jnp.dot(forward_ref[...], jnp.concatenate([wide, wide], axis=0), preferred_element_type=F32)

    tile = 32

    def power_into(total, s):
        for k in range(0, points, tile):
            gained = total[k : k + tile]
            for i in range(GROUP):
                lanes = slice(i * BAND, (i + 1) * BAND)
                real = spec[s, k : k + tile, lanes]
                imag = spec[s, points + k : points + k + tile, lanes]
                gained = gained + (real * real + imag * imag)
            total[k : k + tile] = gained

    def cross_into(total, near, far):
        for k in range(0, points, tile):
            gained_real = total[k : k + tile]
            gained_imag = total[points + k : points + k + tile]
            for i in range(GROUP):
                lanes = slice(i * BAND, (i + 1) * BAND)
                near_real = near[k : k + tile, lanes]
                near_imag = near[points + k : points + k + tile, lanes]
                far_real = far[k : k + tile, lanes]
                far_imag = far[points + k : points + k + tile, lanes]
                gained_real = gained_real + (near_real * far_real + near_imag * far_imag)
                gained_imag = gained_imag + (near_imag * far_real - near_real * far_imag)
            total[k : k + tile] = gained_real
            total[points + k : points + k + tile] = gained_imag

    def lags_of(values, columns):
        high = values.astype(BF16)
        low = (values - high.astype(F32)).astype(BF16)
        table = inverse_ref[:, :columns]
        rest = inverse_ref[:, 2 * points : 2 * points + columns]
        return jnp.dot(
            jnp.concatenate([table, rest, table], axis=1),
            jnp.concatenate([high, high, low], axis=0),
            preferred_element_type=F32,
        )

    def lags_of_many(*totals):
        both = lags_of(jnp.concatenate([total[...] for total in totals], axis=1), 2 * points)
        return [both[:, i * BAND : (i + 1) * BAND] for i in range(len(totals))]

    def add_piece(c, begin, piece):
        rows = pl.ds(begin, points)
        stack[c, 0, rows] += piece[:points]
        stack[c, 1, rows] += piece[points:]

    def clear(*totals):
        for total in totals:
            total[...] = jnp.zeros_like(total)

    def over_windows(step):
        def body(q, carry):
            step(q)
            return carry

        lax.fori_loop(0, groups, body, 0)

    def over_bands(begin, end, band):
        def body(c, carry):
            band(c)
            return carry

        lax.fori_loop(begin, end, body, 0)

    def own_band(c):
        clear(sums_a)

        def step(q):
            s = c * groups + q
            spec[s] = transform(white, s)
            power_into(sums_a, s)

        over_windows(step)
        stack[c] = jnp.zeros(stack.shape[1:], F32)
        add_piece(c, 0, flag_ref[REACH + 1 : REACH + 2, :] * lags_of(sums_a[:points], points))
        relay_if(c >= 0, EARLY - bands - 2 + c + 2 * lax.div(c, bands - 1))

    over_bands(0, bands - 1, own_band)

    def last_step(q, carry):
        @pl.when(at_cut)
        def _():
            edge(q).wait_recv()

        whiten(q, (1 - mirrored) * (bands - 1) * BAND, 1, lambda j: bands - 1)
        s = (bands - 1) * groups + q

        @pl.when(z == 0)
        def _():
            own_to(0, s, 0, 1).start()

        @pl.when((z == 2) & first)
        def _():
            own_to(2, s, 0, 1).start()
            own_to(2, s, 1, 3).start()

        @pl.when(z == 3)
        def _():
            own_to(3, s, 0, 1 + m).start()

        relay_if(lax.rem(q, 4) == 3, EARLY - 3 + lax.div(q, 4))
        return carry

    lax.fori_loop(0, groups, last_step, 0)

    @pl.when((z == 3) & first)
    def _():
        send_range(3, 2 * groups, 3 * groups, 0, 2)

    over_bands(bands - 1, bands, own_band)

    def owner_of(flags, offset):
        return flags[offset : offset + 1, :]

    def far_share(flags, offset):
        return owner_of(flags, offset) * flags[REACH + 1 + offset : REACH + 2 + offset, :]

    def near_share(flags, offset):
        return (1.0 - owner_of(flags, offset)) * flags[REACH + 1 + offset : REACH + 2 + offset, :]

    def store_rows(buffer, c, begin, piece, rows=slice(0, 2 * channels)):
        count = rows.stop - rows.start
        for part in range(2):
            top = part * points
            buffer[c, part, begin : begin + count] = piece[top + rows.start : top + rows.stop].astype(buffer.dtype)

    def store_sums(buffer, c, parts):
        for part in range(2):
            top = part * points
            for k in range(len(parts) + 1):
                terms = []
                if k < len(parts):
                    terms.append(parts[k][top : top + channels])
                if k > 0:
                    terms.append(parts[k - 1][top + channels : top + points])
                total = terms[0] if len(terms) == 1 else terms[0] + terms[1]
                buffer[c, part, k * channels : (k + 1) * channels] = total.astype(buffer.dtype)

    zero_flags, two_flags = seen.at[0], seen.at[1]

    @pl.when(z == 0)
    def _():
        @pl.when(second)
        def _():
            clear(sums_a, sums_b, sums_c)

            def step(q):
                for block, total, held in ((1, sums_a, one), (2, sums_b, two), (3, sums_c, three)):
                    s = 2 * groups + q
                    arrived(block, s)
                    held[...] = transform(received[block], s)
                    cross_into(total, spec.at[s], held)

            over_windows(step)
            pairs = lags_of_many(sums_a, sums_b, sums_c)
            for offset in range(1, REACH + 1):
                add_piece(2, offset * channels, near_share(flag_ref, offset) * pairs[offset - 1])
            store_rows(near_out, 2, 0, far_share(flag_ref, 1) * pairs[0])
            store_rows(far_out, 2, 0, far_share(flag_ref, 2) * pairs[1])
            store_rows(far_out, 2, points, far_share(flag_ref, 3) * pairs[2])

        @pl.loop(0, bands)
        def _(c):
            swap(c).start()

        @pl.when(first)
        def _():
            sent(pieces - 1, 0)
            pl.semaphore_signal(drained, inc=1, device_id=partner, device_id_type=MESH)

        @pl.when(second)
        def _():
            pl.semaphore_wait(drained, 1)
            start_all(far_pair_03(2, 0))
            start_all(far_pair_02(2, 0))
            start_all(far_pair_01(2, 0))

    @pl.when(z == 1)
    def _():
        flags_to(0, 1, 0).wait_recv()

        @pl.when(second)
        def _():
            swap(2).start()

        def band(turn):
            c = turn + m * lax.div(turn, 2)
            clear(sums_a)

            def step(q):
                s = c * groups + q
                i = turn * groups + q

                @pl.when((i < CATCH_UP) & (lax.rem(i, 2) == 0))
                def _():
                    relay(EARLY + lax.div(i, 2))

                @pl.when((i >= CATCH_UP) & (i + EARLY - CATCH_UP // 2 < 3 * groups))
                def _():
                    relay(i + EARLY - CATCH_UP // 2)

                one[...] = transform(white0, s)
                cross_into(sums_a, one, spec.at[s])

                @pl.when(first & (turn == bands - 2))
                def _():
                    late = (bands - 1) * groups + q
                    arrived(2, late)
                    spec[q] = transform(white2, late)
                    arrived(3, late)
                    spec[groups + q] = transform(white3, late)

            over_windows(step)
            piece = lags_of(sums_a[...], 2 * points)
            store_rows(near_out, c, 0, near_share(zero_flags, 1) * piece)
            start_all(near_from_1(c))
            add_piece(c, channels, far_share(zero_flags, 1) * piece)
            swap(c).start()

        over_bands(0, bands - 1, band)

        @pl.when(first)
        def _():
            c = bands - 1
            clear(sums_a, sums_b, sums_c)

            def step(q):
                s = c * groups + q
                arrived(0, s)
                one[...] = transform(white0, s)
                cross_into(sums_a, one, spec.at[s])
                cross_into(sums_b, one, spec.at[q])
                cross_into(sums_c, one, spec.at[groups + q])

            over_windows(step)
            pairs = lags_of_many(sums_a, sums_b, sums_c)
            store_sums(near_out, c, [near_share(zero_flags, o) * pairs[o - 1] for o in range(1, REACH + 1)])
            start_all(near_from_1_all(c))
            store_rows(far_out, c, points, far_share(zero_flags, 3) * pairs[2])
            start_all(far_pair_03(c, 1))
            store_rows(far_out, c, 0, far_share(zero_flags, 2) * pairs[1])
            start_all(far_pair_02(c, 1))
            add_piece(c, channels, far_share(zero_flags, 1) * pairs[0])
            swap(c).start()

    @pl.when(z == 2)
    def _():
        flags_to(0, 2, 0).wait_recv()

        @pl.when(first)
        def _():
            swap(bands - 1).start()

        @pl.when(second)
        def _():
            swap(2).start()

        clear(sums_a)

        def early_step(q):
            arrived(0, q)
            pass_on(q, 2, 3).start()
            one[...] = transform(white0, q)
            cross_into(sums_a, one, spec.at[q])

        over_windows(early_step)
        piece = lags_of(sums_a[...], 2 * points)
        store_rows(near_out, 0, 0, near_share(zero_flags, 2) * piece)
        near_out[0, :, points : points + channels] = jnp.zeros((2, channels, BAND), near_out.dtype)
        start_all(near_from_2(0))
        add_piece(0, 2 * channels, far_share(zero_flags, 2) * piece)
        swap(0).start()

        def band(turn):
            c = turn + m * lax.div(turn, 2)
            clear(sums_a, sums_b, sums_c)

            def step(q):
                s = c * groups + q
                arrived(3, s)
                three[...] = transform(white3, s)
                cross_into(sums_b, spec.at[s], three)

                @pl.when(q == groups - 1)
                def _():
                    sums_b[...] = lags_of(sums_b[...], 2 * points)

                arrived(0, s)
                one[...] = transform(white0, s)
                cross_into(sums_a, one, spec.at[s])
                cross_into(sums_c, one, three)

            over_windows(step)
            near, beyond = lags_of_many(sums_a, sums_c)
            store_sums(near_out, c, [near_share(zero_flags, 2) * near, near_share(zero_flags, 3) * beyond])
            start_all(near_from_2(c))
            ahead = sums_b[...]
            store_rows(far_out, c, 0, far_share(flag_ref, 1) * ahead)
            store_rows(far_out, c, points, far_share(zero_flags, 3) * beyond)
            start_all(far_from_2(c))
            add_piece(c, 2 * channels, far_share(zero_flags, 2) * near)
            add_piece(c, channels, near_share(flag_ref, 1) * ahead)
            swap(c).start()

        over_bands(1, bands - 1, band)

    @pl.when(z == 3)
    def _():
        flags_to(0, 3, 0).wait_recv()
        flags_to(1, 3, 0).wait_recv()

        @pl.loop(1, bands - 1)
        def _(turn):
            swap(turn + m * lax.div(turn, 2)).start()

        def band(c):
            clear(sums_a)

            def step(q):
                s = c * groups + q
                arrived(2, s)
                two[...] = transform(white2, s)
                cross_into(sums_a, two, spec.at[s])

            over_windows(step)
            piece = lags_of(sums_a[...], 2 * points)
            store_rows(far_out, c, 0, near_share(two_flags, 1) * piece)
            start_all(near_pair_23(c))
            add_piece(c, channels, far_share(two_flags, 1) * piece)

            @pl.when(c == 0)
            def _():
                clear(sums_c)

                def late_step(q):
                    s = c * groups + q
                    arrived(0, s)
                    one[...] = transform(white0, s)
                    cross_into(sums_c, one, spec.at[s])

                over_windows(late_step)
                distant = lags_of(sums_c[...], 2 * points)
                store_rows(near_out, c, points, near_share(zero_flags, 3) * distant)
                start_all(near_from_3(c))
                add_piece(c, 3 * channels, far_share(zero_flags, 3) * distant)

            swap(c).start()

        over_bands(0, 2, lambda turn: band(turn * (bands - 1 - m)))

    def lanes_of(core, c):
        return pl.ds(pl.multiple_of(core * half + place(c) * BAND, BAND), BAND)

    def collect(c):
        out_ref[:, :, lanes_of(m, c)] = stack[c, :, pl.ds(pl.multiple_of(m * kept, 8), kept)]
        swap(c).wait_recv()
        out_ref[:, :, lanes_of(1 - m, c)] = swapped[c]
        swap(c).wait_send()

    over_bands(0, bands, collect)

    def take(target, c, source, sender, low, high):
        top, end = max(low, target * kept), min(high, (target + 1) * kept)
        if top < end:
            rows = slice(top - target * kept, end - target * kept)
            results(c, source, sender, near_out, low, low, high, 0, 0)[target].wait_recv()
            out_ref[:, rows, lanes_of(sender, c)] += inbox[source, sender, c, :, rows].astype(F32)

    def take_at_0(target):
        for sender in range(halves):
            def band(turn):
                c = turn + sender * lax.div(turn, 2)
                take(target, c, 1, sender, channels, one_pair)
                take(target, c, 2, sender, 2 * channels, three_pairs)

            over_bands(0, bands - 1, band)
            take(target, 0, 3, sender, 3 * channels, three_pairs)
        take(target, bands - 1, 1, 0, channels, three_pairs)

    def take_at_1(target):
        take(target, 2, 0, 1, channels, one_pair)

    def take_at_2(target):
        for sender in range(halves):
            take(target, 0, 3, sender, channels, one_pair)
            take(target, bands - 1 - sender, 3, sender, channels, one_pair)
        take(target, 2, 0, 1, 2 * channels, two_pairs)
        take(target, bands - 1, 1, 0, 2 * channels, two_pairs)

    def take_at_3(target):
        for sender in range(halves):
            def band(turn):
                take(target, turn + sender * lax.div(turn, 2), 2, sender, channels, three_pairs)

            over_bands(1, bands - 1, band)
        take(target, 2, 0, 1, 3 * channels, three_pairs)
        take(target, bands - 1, 1, 0, 3 * channels, three_pairs)

    for block, step in enumerate((take_at_0, take_at_1, take_at_2, take_at_3)):
        for target in range(halves):
            @pl.when((z == block) & (m == target))
            def _():
                step(target)

    @pl.when(at_cut)
    def _():
        @pl.loop(0, groups)
        def _(q):
            edge(q).wait_send()

    def sent_range(begin, end, lane):
        @pl.loop(begin, end)
        def _(s):
            sent(s, lane)

    @pl.when(z == 0)
    def _():
        for device in range(1, blocks):
            flags_to(0, device, device - 1).wait_send()
        sent_range(0, (3 - m) * groups, 0)
        sent_range(3 * groups, pieces - 1 + m, 0)

        @pl.when(second)
        def _():
            finish_all(far_pair_01(2, 0))
            finish_all(far_pair_02(2, 0))
            finish_all(far_pair_03(2, 0))

    @pl.when(z == 1)
    def _():
        sent_range(0, 2 * groups, 0)
        sent_range((2 + m) * groups, (3 + m) * groups, 0)
        over_bands(0, bands - 1, lambda turn: finish_all(near_from_1(turn + m * lax.div(turn, 2))))

        @pl.when(second)
        def _():
            sent_range(2 * groups, 3 * groups, 1)

        @pl.when(first)
        def _():
            finish_all(near_from_1_all(bands - 1))
            finish_all(far_pair_03(bands - 1, 1))
            finish_all(far_pair_02(bands - 1, 1))

    @pl.when(z == 2)
    def _():
        flags_to(1, 3, 0).wait_send()

        @pl.when(first)
        def _():
            sent_range((bands - 1) * groups, pieces, 0)
            sent_range((bands - 1) * groups, pieces, 1)

        @pl.when(second)
        def _():
            sent_range(2 * groups, 3 * groups, 0)
            sent_range(2 * groups, 3 * groups, 1)

        sent_range(0, groups, 1)
        sent_range(0, groups, 2)
        finish_all(near_from_2(0))

        def band(turn):
            c = turn + m * lax.div(turn, 2)
            finish_all(near_from_2(c))
            finish_all(far_from_2(c))

        over_bands(1, bands - 1, band)

    @pl.when(z == 3)
    def _():
        sent_range(groups, pieces, 0)
        finish_all(near_pair_23(0))
        finish_all(near_pair_23(bands - 1 - m))
        finish_all(near_from_3(0))


def in_hbm(array):
    return pltpu.with_memory_space_constraint(array, pltpu.HBM)


def four_block_shards(spectra, counts, owners):
    parts, windows, channels, bins = spectra.shape
    halves, blocks = lax.axis_size("pairs"), lax.axis_size("cable")
    half, points = bins // halves, 2 * channels
    forward, inverse = channel_transforms(channels, 1.0 / math.sqrt(windows * channels))
    window = smoothing_window()
    bands, groups = half // BAND, windows // GROUP
    pieces = bands * groups
    rows = (REACH + 2) * channels
    kept = rows // halves
    block = pltpu.VMEM((pieces, GROUP, points, BAND), BF16)
    spectrum = pltpu.VMEM((2 * points, GROUP * BAND), F32)
    sums = pltpu.VMEM((2 * points, BAND), F32)
    shares = pltpu.VMEM((bands, 2, 2 * points, BAND), BF16)
    flags = (2 * (REACH + 1), BAND)
    dma = pltpu.SemaphoreType.DMA
    width = inverse.shape[1]
    tables = np.zeros((TABLE_ROWS, width), jnp.bfloat16)
    top = 0
    for table in (window, forward, inverse):
        tables[top : top + table.shape[0], : table.shape[1]] = table
        top += table.shape[0]
    hbm = pl.BlockSpec(memory_space=pl.ANY)
    smem = pl.BlockSpec(memory_space=pltpu.SMEM)
    out = pl.pallas_call(
        stack_kernel,
        out_shape=jax.ShapeDtypeStruct((2, kept, bins), F32),
        in_specs=[hbm, smem, hbm, hbm],
        out_specs=pl.BlockSpec(memory_space=pltpu.VMEM),
        scratch_shapes=[
            pltpu.SMEM(owners.shape, owners.dtype),
            pltpu.VMEM((2, windows, channels, half + 2 * EDGE), BF16),
            pltpu.VMEM(window.shape, BF16),
            pltpu.VMEM(forward.shape, BF16),
            pltpu.VMEM(inverse.shape, BF16),
            pltpu.VMEM(flags, F32),
            pltpu.VMEM((2,) + flags, F32),
            block, block, block, block, block,
            pltpu.VMEM((pieces, 2 * points, GROUP * BAND), F32),
            spectrum, spectrum, spectrum, sums, sums, sums,
            pltpu.VMEM((bands, 2, rows, BAND), F32),
            shares, shares,
            pltpu.VMEM((blocks, halves, bands, 2, kept, BAND), BF16),
            pltpu.VMEM((bands, 2, kept, BAND), F32),
            dma((groups,)), dma((3,)), dma((groups,)), dma((groups,)), dma((3,)), dma((2,)),
            dma((3, pieces)), dma((blocks, pieces)),
            dma((3, halves, bands)), dma((blocks, halves, bands)),
            dma((bands,)), dma((bands,)),
            pltpu.SemaphoreType.REGULAR, pltpu.SemaphoreType.REGULAR, pltpu.SemaphoreType.REGULAR,
        ],
        compiler_params=pltpu.CompilerParams(
            collective_id=0, has_side_effects=True, vmem_limit_bytes=40 * 1024 * 1024
        ),
    )(in_hbm(spectra), counts, in_hbm(owners), in_hbm(jnp.asarray(tables)))
    return out[:, None]


def solution(mesh):
    sizes = dict(mesh.shape)
    fits = sizes["cable"] == REACH + 1 and sizes["pairs"] == 2 and sizes["bins"] == 2
    shards = four_block_shards if fits else general_shards
    placed = (
        P("groups", None, "cable", "bins"),
        P(("groups", "cable")),
        P(("groups", "cable"), None),
    )
    return jax.shard_map(
        shards,
        mesh=mesh,
        in_specs=placed,
        out_specs=P("groups", "cable", "pairs", "bins"),
        check_vma=False,
    )
```

```python
import math

import jax
import jax.numpy as jnp
import numpy as np
from jax import lax
from jax.experimental import pallas as pl
from jax.experimental.pallas import tpu as pltpu
from jax.sharding import PartitionSpec as P

REACH = 3
HALF_WIDTH = 32


epsilon = 1e-06
band_rows = 16


def with_halo(x, sides, width):
    for axis, dim in sides:
        count, length = (lax.axis_size(axis), x.shape[dim])
        up = [(i, (i + 1) % count) for i in range(count - 1)]
        down = [(j, i) for i, j in up]
        last = lax.slice_in_dim(x, length - width, length, axis=dim)
        first = lax.slice_in_dim(x, 0, width, axis=dim)
        before = lax.ppermute(last, axis, up)
        after = lax.ppermute(first, axis, down)
        x = jnp.concatenate([before, x, after], axis=dim)
    return x


def from_behind(block, axis, distance):
    devices = range(lax.axis_size(axis))
    route = [(i - distance, i) for i in devices if i - distance in devices]
    return lax.ppermute(block, axis, route)


def whiten_rows(spectra):
    real_part = spectra[0].astype(jnp.float32)
    imag_part = spectra[1].astype(jnp.float32)
    power_sum = real_part * real_part + imag_part * imag_part
    padded = with_halo(power_sum, (("bins", 2),), HALF_WIDTH)
    window_len = 2 * HALF_WIDTH + 1
    window_sum = lax.reduce_window(
        padded, jnp.zeros((), padded.dtype), lax.add, (1, 1, window_len), (1, 1, 1), "VALID"
    )
    inverse_amp = lax.rsqrt(window_sum / window_len + epsilon)
    return jnp.stack(
        [
            (real_part * inverse_amp).astype(jnp.bfloat16),
            (imag_part * inverse_amp).astype(jnp.bfloat16),
        ]
    )


def make_lag_table(col_count):
    flattened = jnp.arange(band_rows * col_count)
    row_of = flattened // col_count
    col_of = flattened % col_count
    lag_lanes = jnp.arange(col_count + band_rows - 1)
    return (lag_lanes[None, :] == (col_of - row_of + band_rows - 1)[:, None]).astype(jnp.bfloat16)


def lag_stack(pair_block, lag_table):
    freq_count, row_count, col_count = pair_block.shape
    group_count = row_count // band_rows
    grouped = pair_block.reshape(freq_count, group_count, band_rows * col_count)
    banded = jnp.einsum("fgk,ku->fgu", grouped, lag_table, preferred_element_type=jnp.float32)
    lag_sums = jnp.zeros((freq_count, col_count + row_count - 1), jnp.float32)
    for row_group in range(group_count):
        first_lag = row_count - band_rows * (row_group + 1)
        lag_sums = lag_sums.at[:, first_lag : first_lag + col_count + band_rows - 1].add(
            banded[:, row_group]
        )
    return lag_sums.T


def correlate(left_rows, right_rows, factor, lag_table):
    left_real = jnp.concatenate([left_rows[0], left_rows[1]], axis=0)
    left_imag = jnp.concatenate([left_rows[1], -left_rows[0]], axis=0)
    right_both = jnp.concatenate([right_rows[0], right_rows[1]], axis=0)
    corr_real = (
        jnp.einsum("wif,wjf->fij", left_real, right_both, preferred_element_type=jnp.float32)
        * factor
    ).astype(jnp.bfloat16)
    corr_imag = (
        jnp.einsum("wif,wjf->fij", left_imag, right_both, preferred_element_type=jnp.float32)
        * factor
    ).astype(jnp.bfloat16)
    return jnp.stack([lag_stack(corr_real, lag_table), lag_stack(corr_imag, lag_table)])


def general_shards(spectra, counts, owners):
    pair_devs = lax.axis_size("pairs")
    member = lax.axis_index("pairs")
    channels = spectra.shape[2]
    half_rows = channels // pair_devs
    source = whiten_rows(spectra)
    receiver = lax.dynamic_slice_in_dim(source, member * half_rows, half_rows, 2)
    block_count = lax.axis_size("cable")
    cable_index = lax.axis_index("cable")
    live_count = jnp.minimum(counts[0], block_count - cable_index)
    panels = {0: receiver}
    for offset in range(1, REACH + 1):
        panels[offset] = from_behind(receiver, "cable", -offset)
    factor = 1.0 / math.sqrt(source.shape[1] * channels)
    lag_table = make_lag_table(half_rows)
    freq_count = source.shape[3]
    stacks = jnp.zeros((2, (REACH + 2) * channels, freq_count), jnp.float32)
    for offset in range(REACH + 1):
        lag_piece = correlate(source, panels[offset], factor, lag_table)
        weight = (offset < live_count).astype(jnp.float32)
        if offset == 0:
            kept_here = weight * lag_piece
        else:
            sent_away = owners[0, offset].astype(jnp.float32)
            arrived = from_behind(weight * sent_away * lag_piece, "cable", offset)
            kept_here = weight * (1.0 - sent_away) * lag_piece + arrived
        first_lag = offset * channels + member * half_rows
        current = lax.dynamic_slice_in_dim(stacks, first_lag, kept_here.shape[1], 1)
        stacks = lax.dynamic_update_slice_in_dim(stacks, current + kept_here, first_lag, 1)
    summed = lax.psum_scatter(stacks, "pairs", scatter_dimension=1, tiled=True)
    return summed[:, None]


EDGE = 128
BAND = 128
GROUP = 2
EARLY = 9
CATCH_UP = 14
TABLE_ROWS = 2048
F32 = jnp.float32
BF16 = jnp.bfloat16
MESH = pl.DeviceIdType.MESH


def channel_transforms(channels, factor):
    points = 2 * channels
    index = np.arange(points)
    angle = 2 * np.pi * np.outer(index, np.arange(channels)) / points
    cos, sin = np.cos(angle), np.sin(angle)
    forward = split_high_low(np.block([[cos, sin], [-sin, cos]]))
    angle = 2 * np.pi * np.outer(index - (channels - 1), index) / points
    cos, sin = np.cos(angle), np.sin(angle)
    cos[-1], sin[-1] = 0.0, 0.0
    inverse = split_high_low(np.block([[cos, sin], [-sin, cos]]) * (factor / points))
    return forward, inverse


def split_high_low(full):
    high = full.astype(jnp.bfloat16)
    low = (full - high.astype(np.float64)).astype(jnp.bfloat16)
    return np.concatenate([high, low], axis=1)


def smoothing_window():
    distance = np.arange(BAND + 2 * EDGE)[:, None] - (np.arange(BAND)[None, :] + EDGE)
    ones = (np.abs(distance) <= HALF_WIDTH).astype(jnp.bfloat16)
    return np.concatenate([ones, ones], axis=0)


def stack_kernel(
    spectra_ref, counts_ref, owners_hbm, tables_ref, out_ref,
    owners_ref,
    x_ref, window_ref, forward_ref, inverse_ref, flag_ref, seen,
    white, white0, white1, white2, white3, spec, one, two, three, sums_a, sums_b, sums_c,
    stack, near_out, far_out, inbox, swapped,
    load_sem, constant_sem, edge_send, edge_recv, flag_send, flag_recv,
    block_send, block_recv, result_send, result_recv, swap_send, swap_recv, known, spread, drained, across,
):
    windows, channels = x_ref.shape[1:3]
    half = x_ref.shape[3] - 2 * EDGE
    bands, groups = half // BAND, windows // GROUP
    pieces = bands * groups
    points = 2 * channels
    kept = out_ref.shape[1]
    blocks, halves = lax.axis_size("cable"), lax.axis_size("pairs")
    z, m = lax.axis_index("cable"), lax.axis_index("pairs")
    cuts, x = lax.axis_size("bins"), lax.axis_index("bins")
    bins = spectra_ref.shape[3]
    first = m == 0
    second = m == 1
    mirrored = x
    partner = {"pairs": 1 - m}

    def remote(source, target, send, recv, device):
        return pltpu.make_async_remote_copy(
            src_ref=source, dst_ref=target, send_sem=send, recv_sem=recv, device_id=device, device_id_type=MESH
        )

    received = (white0, white1, white2, white3)

    def own_to(block, s, lane, device):
        return remote(
            white.at[s], received[block].at[s], block_send.at[lane, s], block_recv.at[block, s], {"cable": device}
        )

    def pass_on(s, lane, device):
        return remote(
            white0.at[s], white0.at[s], block_send.at[lane, s], block_recv.at[0, s], {"cable": device}
        )

    def arrived(block, s):
        own_to(block, s, 0, 0).wait_recv()

    def sent(s, lane):
        own_to(0, s, lane, 0).wait_send()

    def place(c):
        return c + mirrored * (bands - 1 - 2 * c)

    def results(c, source, sender, buffer, begin, low, high, device, lane):
        copies = {}
        for target in range(halves):
            top, end = max(low, target * kept), min(high, (target + 1) * kept)
            if top < end:
                copies[target] = remote(
                    buffer.at[c, :, top - begin : end - begin],
                    inbox.at[source, sender, c, :, top - target * kept : end - target * kept],
                    result_send.at[lane, target, c],
                    result_recv.at[source, sender, c],
                    {"cable": device, "pairs": target},
                )
        return copies

    def start_all(copies):
        for copy in copies.values():
            copy.start()

    def finish_all(copies):
        for copy in copies.values():
            copy.wait_send()

    one_pair = channels + points
    two_pairs = 2 * channels + points
    three_pairs = 3 * channels + points

    def near_from_1(c, sender=m):
        return results(c, 1, sender, near_out, channels, channels, one_pair, 0, 0)

    def near_from_1_all(c, sender=m):
        return results(c, 1, sender, near_out, channels, channels, three_pairs, 0, 0)

    def near_from_2(c, sender=m):
        return results(c, 2, sender, near_out, 2 * channels, 2 * channels, three_pairs, 0, 0)

    def near_from_3(c, sender=m):
        return results(c, 3, sender, near_out, channels, 3 * channels, three_pairs, 0, 0)

    def near_pair_23(c, sender=m):
        return results(c, 3, sender, far_out, channels, channels, one_pair, 2, 1)

    def far_from_2(c, sender=m):
        return results(c, 2, sender, far_out, channels, channels, three_pairs, 3, 1)

    def far_pair_01(c, source, sender=m):
        return results(c, source, sender, near_out, channels, channels, one_pair, 1, 0)

    def far_pair_02(c, source, sender=m):
        return results(c, source, sender, far_out, 2 * channels, 2 * channels, two_pairs, 2, 1)

    def far_pair_03(c, source, sender=m):
        return results(c, source, sender, far_out, channels, 3 * channels, three_pairs, 3, 2)

    def swap(c):
        rows = pl.ds(pl.multiple_of((1 - m) * kept, 8), kept)
        return remote(stack.at[c, :, rows], swapped.at[c], swap_send.at[c], swap_recv.at[c], partner)

    def load(q):
        near = pl.multiple_of(m * (half - EDGE), EDGE)
        begin = pl.multiple_of((1 - m) * EDGE, EDGE)
        rows = pl.ds(q * GROUP, GROUP)
        return pltpu.make_async_copy(
            spectra_ref.at[:, rows, :, pl.ds(near, half + EDGE)],
            x_ref.at[:, rows, :, pl.ds(begin, half + EDGE)],
            load_sem.at[q],
        )

    constants, top = [], 0
    for i, table in enumerate((window_ref, forward_ref, inverse_ref)):
        rows, columns = table.shape
        source = tables_ref.at[top : top + rows, :columns]
        constants.append(pltpu.make_async_copy(source, table, constant_sem.at[i]))
        top += rows

    def edge_lanes(core):
        return pl.ds(pl.multiple_of(core * (half + EDGE), EDGE), EDGE)

    def edge(q):
        begin = EDGE + (1 - x) * (half - EDGE)
        rows = pl.ds(q * GROUP, GROUP)
        return remote(
            x_ref.at[:, rows, :, pl.ds(pl.multiple_of(begin, EDGE), EDGE)],
            x_ref.at[:, rows, :, edge_lanes(x)],
            edge_send.at[q],
            edge_recv.at[q],
            {"bins": 1 - x, "pairs": x},
        )

    def flags_to(source, device, lane):
        return remote(
            flag_ref, seen.at[source], flag_send.at[lane], flag_recv.at[source], {"cable": device}
        )

    load(0).start()
    constants[0].start()
    settings = pltpu.make_async_copy(owners_hbm, owners_ref, flag_send.at[0])
    settings.start()
    for q in range(1, groups):
        load(q).start()
    constants[1].start()
    constants[2].start()
    barrier = pltpu.get_barrier_semaphore()
    beside = jnp.where((z > 0) & (z < blocks - 1), 2, 1)

    def tell_beside(semaphore):
        @pl.when(z > 0)
        def _():
            pl.semaphore_signal(semaphore, inc=1, device_id={"cable": z - 1}, device_id_type=MESH)

        @pl.when(z < blocks - 1)
        def _():
            pl.semaphore_signal(semaphore, inc=1, device_id={"cable": z + 1}, device_id_type=MESH)

    tell_beside(barrier)
    pl.semaphore_signal(barrier, inc=1, device_id=partner, device_id_type=MESH)
    at_cut = x != m

    @pl.when(at_cut & (z > 0))
    def _():
        pl.semaphore_signal(barrier, inc=1, device_id={"bins": 1 - x, "pairs": x}, device_id_type=MESH)

    def whiten(q, begin, count, store):
        lanes = pl.ds(pl.multiple_of(begin, BAND), count * BAND + 2 * EDGE)
        reals, imags, highs, lows = [], [], [], []
        for i in range(GROUP):
            real = x_ref[0, q * GROUP + i, :, lanes].astype(F32)
            imag = x_ref[1, q * GROUP + i, :, lanes].astype(F32)
            power = real * real + imag * imag
            high = power.astype(BF16)
            reals.append(real)
            imags.append(imag)
            highs.append(high)
            lows.append((power - high.astype(F32)).astype(BF16))
        high = jnp.concatenate(highs, axis=0)
        low = jnp.concatenate(lows, axis=0)
        for j in range(count):
            reach = slice(j * BAND, (j + 1) * BAND + 2 * EDGE)
            terms = jnp.concatenate([high[:, reach], low[:, reach]], axis=1)
            total = jnp.dot(terms, window_ref[...], preferred_element_type=F32)
            gain = lax.rsqrt(total / (2 * HALF_WIDTH + 1) + epsilon)
            here = slice(EDGE + j * BAND, EDGE + (j + 1) * BAND)
            slot = store(j) * groups + q
            for i in range(GROUP):
                rows = gain[i * channels : (i + 1) * channels]
                white[slot, i, :channels] = (reals[i][:, here] * rows).astype(BF16)
                white[slot, i, channels:] = (imags[i][:, here] * rows).astype(BF16)

    def whiten_inner(q):
        whiten(q, mirrored * BAND, bands - 1, lambda j: j + mirrored * (bands - 2 - 2 * j))

    def send_edge(q):
        @pl.when(at_cut & (z > 0))
        def _():
            edge(q).start()

    def send_first(q):
        @pl.when(z == 0)
        def _():
            own_to(0, q, 0, 1).start()

    def send_inner(q):
        @pl.when((z == 1) & second)
        def _():
            own_to(1, q + 2 * groups, 1, 0).start()

        @pl.when(z == 2)
        def _():
            own_to(2, q, 1, 3).start()

        @pl.when(z == 3)
        def _():
            own_to(3, q + groups, 0, 2).start()

    def relay(i):
        s = i + groups * m * lax.div(i, 2 * groups)
        arrived(0, s)
        pass_on(s, 0, 2).start()

    def relay_if(condition, i):
        @pl.when((z == 1) & condition)
        def _():
            relay(i)

    def send_range(block, begin, end, lane, device):
        @pl.loop(begin, end)
        def _(s):
            own_to(block, s, lane, device).start()

    constants[0].wait()
    load(0).wait()
    whiten(0, mirrored * (bands - 1) * BAND, 1, lambda j: 0)
    pl.semaphore_wait(barrier, beside + 1 + jnp.where(at_cut & (z > 0), 1, 0))
    send_first(0)
    send_edge(0)
    tell_beside(known)

    @pl.when(at_cut & (z == 1))
    def _():
        pl.semaphore_signal(across, inc=1, device_id={"bins": 1 - x, "pairs": x}, device_id_type=MESH)

    whiten(0, BAND, bands - 2, lambda j: 1 + j + mirrored * (bands - 3 - 2 * j))
    send_inner(0)

    settings.wait()
    live = jnp.minimum(counts_ref[0], blocks - z)
    for offset in range(REACH + 1):
        flag_ref[offset : offset + 1, :] = jnp.full((1, BAND), owners_ref[0, offset].astype(F32))
        weight = jnp.where(offset < live, 1.0, 0.0)
        flag_ref[REACH + 1 + offset : REACH + 2 + offset, :] = jnp.full((1, BAND), weight)

    @pl.when(z == 0)
    def _():
        flags_to(0, 1, 0).start()

    @pl.when(z == 2)
    def _():
        flags_to(1, 3, 0).start()

    @pl.when(~at_cut)
    def _():
        x_ref[:, :, :, edge_lanes(m)] = jnp.zeros((2, windows, channels, EDGE), x_ref.dtype)

    def inner_step(q, carry):
        load(q).wait()
        send_edge(q)
        whiten_inner(q)
        send_first(q)
        send_inner(q)
        relay_if((q >= 3) & (lax.rem(q, 2) == 1), lax.div(q - 3, 2))
        return carry

    lax.fori_loop(1, groups // 2, inner_step, 0)
    pl.semaphore_wait(known, beside)

    @pl.when(at_cut & (z == 1))
    def _():
        pl.semaphore_wait(across, 1)

    tell_beside(spread)
    lax.fori_loop(groups // 2, groups, inner_step, 0)
    pl.semaphore_wait(spread, beside)

    @pl.when(at_cut & (z == 0))
    def _():
        @pl.loop(0, groups)
        def _(q):
            edge(q).start()

    @pl.when(z == 0)
    def _():
        for device in range(2, blocks):
            flags_to(0, device, device - 1).start()
        send_range(0, groups, (3 - m) * groups, 0, 1)

    @pl.when((z == 2) & second)
    def _():
        send_range(2, 2 * groups, 3 * groups, 0, 0)
        send_range(2, 2 * groups, 3 * groups, 1, 3)

    @pl.when((z == 3) & second)
    def _():
        send_range(3, 2 * groups, 3 * groups, 0, 0)

    constants[1].wait()
    constants[2].wait()

    def transform(buffer, s):
        wide = jnp.concatenate([buffer[s, i] for i in range(GROUP)], axis=1)
        return jnp.dot(forward_ref[...], jnp.concatenate([wide, wide], axis=0), preferred_element_type=F32)

    tile = 32

    def power_into(total, s):
        for k in range(0, points, tile):
            gained = total[k : k + tile]
            for i in range(GROUP):
                lanes = slice(i * BAND, (i + 1) * BAND)
                real = spec[s, k : k + tile, lanes]
                imag = spec[s, points + k : points + k + tile, lanes]
                gained = gained + (real * real + imag * imag)
            total[k : k + tile] = gained

    def cross_into(total, near, far):
        for k in range(0, points, tile):
            gained_real = total[k : k + tile]
            gained_imag = total[points + k : points + k + tile]
            for i in range(GROUP):
                lanes = slice(i * BAND, (i + 1) * BAND)
                near_real = near[k : k + tile, lanes]
                near_imag = near[points + k : points + k + tile, lanes]
                far_real = far[k : k + tile, lanes]
                far_imag = far[points + k : points + k + tile, lanes]
                gained_real = gained_real + (near_real * far_real + near_imag * far_imag)
                gained_imag = gained_imag + (near_imag * far_real - near_real * far_imag)
            total[k : k + tile] = gained_real
            total[points + k : points + k + tile] = gained_imag

    def lags_of(values, columns):
        high = values.astype(BF16)
        low = (values - high.astype(F32)).astype(BF16)
        table = inverse_ref[:, :columns]
        rest = inverse_ref[:, 2 * points : 2 * points + columns]
        return jnp.dot(
            jnp.concatenate([table, rest, table], axis=1),
            jnp.concatenate([high, high, low], axis=0),
            preferred_element_type=F32,
        )

    def lags_of_many(*totals):
        both = lags_of(jnp.concatenate([total[...] for total in totals], axis=1), 2 * points)
        return [both[:, i * BAND : (i + 1) * BAND] for i in range(len(totals))]

    def add_piece(c, begin, piece):
        rows = pl.ds(begin, points)
        stack[c, 0, rows] += piece[:points]
        stack[c, 1, rows] += piece[points:]

    def clear(*totals):
        for total in totals:
            total[...] = jnp.zeros_like(total)

    def over_windows(step):
        def body(q, carry):
            step(q)
            return carry

        lax.fori_loop(0, groups, body, 0)

    def over_bands(begin, end, band):
        def body(c, carry):
            band(c)
            return carry

        lax.fori_loop(begin, end, body, 0)

    def own_band(c):
        clear(sums_a)

        def step(q):
            s = c * groups + q
            spec[s] = transform(white, s)
            power_into(sums_a, s)

        over_windows(step)
        stack[c] = jnp.zeros(stack.shape[1:], F32)
        add_piece(c, 0, flag_ref[REACH + 1 : REACH + 2, :] * lags_of(sums_a[:points], points))
        relay_if(c >= 0, EARLY - bands - 2 + c + 2 * lax.div(c, bands - 1))

    over_bands(0, bands - 1, own_band)

    def last_step(q, carry):
        @pl.when(at_cut)
        def _():
            edge(q).wait_recv()

        whiten(q, (1 - mirrored) * (bands - 1) * BAND, 1, lambda j: bands - 1)
        s = (bands - 1) * groups + q

        @pl.when(z == 0)
        def _():
            own_to(0, s, 0, 1).start()

        @pl.when((z == 2) & first)
        def _():
            own_to(2, s, 0, 1).start()
            own_to(2, s, 1, 3).start()

        @pl.when(z == 3)
        def _():
            own_to(3, s, 0, 1 + m).start()

        relay_if(lax.rem(q, 4) == 3, EARLY - 3 + lax.div(q, 4))
        return carry

    lax.fori_loop(0, groups, last_step, 0)

    @pl.when((z == 3) & first)
    def _():
        send_range(3, 2 * groups, 3 * groups, 0, 2)

    over_bands(bands - 1, bands, own_band)

    def owner_of(flags, offset):
        return flags[offset : offset + 1, :]

    def far_share(flags, offset):
        return owner_of(flags, offset) * flags[REACH + 1 + offset : REACH + 2 + offset, :]

    def near_share(flags, offset):
        return (1.0 - owner_of(flags, offset)) * flags[REACH + 1 + offset : REACH + 2 + offset, :]

    def store_rows(buffer, c, begin, piece, rows=slice(0, 2 * channels)):
        count = rows.stop - rows.start
        for part in range(2):
            top = part * points
            buffer[c, part, begin : begin + count] = piece[top + rows.start : top + rows.stop].astype(buffer.dtype)

    def store_sums(buffer, c, parts):
        for part in range(2):
            top = part * points
            for k in range(len(parts) + 1):
                terms = []
                if k < len(parts):
                    terms.append(parts[k][top : top + channels])
                if k > 0:
                    terms.append(parts[k - 1][top + channels : top + points])
                total = terms[0] if len(terms) == 1 else terms[0] + terms[1]
                buffer[c, part, k * channels : (k + 1) * channels] = total.astype(buffer.dtype)

    zero_flags, two_flags = seen.at[0], seen.at[1]

    @pl.when(z == 0)
    def _():
        @pl.when(second)
        def _():
            clear(sums_a, sums_b, sums_c)

            def step(q):
                for block, total, held in ((1, sums_a, one), (2, sums_b, two), (3, sums_c, three)):
                    s = 2 * groups + q
                    arrived(block, s)
                    held[...] = transform(received[block], s)
                    cross_into(total, spec.at[s], held)

            over_windows(step)
            pairs = lags_of_many(sums_a, sums_b, sums_c)
            for offset in range(1, REACH + 1):
                add_piece(2, offset * channels, near_share(flag_ref, offset) * pairs[offset - 1])
            store_rows(near_out, 2, 0, far_share(flag_ref, 1) * pairs[0])
            store_rows(far_out, 2, 0, far_share(flag_ref, 2) * pairs[1])
            store_rows(far_out, 2, points, far_share(flag_ref, 3) * pairs[2])

        @pl.loop(0, bands)
        def _(c):
            swap(c).start()

        @pl.when(first)
        def _():
            sent(pieces - 1, 0)
            pl.semaphore_signal(drained, inc=1, device_id=partner, device_id_type=MESH)

        @pl.when(second)
        def _():
            pl.semaphore_wait(drained, 1)
            start_all(far_pair_03(2, 0))
            start_all(far_pair_02(2, 0))
            start_all(far_pair_01(2, 0))

    @pl.when(z == 1)
    def _():
        flags_to(0, 1, 0).wait_recv()

        @pl.when(second)
        def _():
            swap(2).start()

        def band(turn):
            c = turn + m * lax.div(turn, 2)
            clear(sums_a)

            def step(q):
                s = c * groups + q
                i = turn * groups + q

                @pl.when((i < CATCH_UP) & (lax.rem(i, 2) == 0))
                def _():
                    relay(EARLY + lax.div(i, 2))

                @pl.when((i >= CATCH_UP) & (i + EARLY - CATCH_UP // 2 < 3 * groups))
                def _():
                    relay(i + EARLY - CATCH_UP // 2)

                one[...] = transform(white0, s)
                cross_into(sums_a, one, spec.at[s])

                @pl.when(first & (turn == bands - 2))
                def _():
                    late = (bands - 1) * groups + q
                    arrived(2, late)
                    spec[q] = transform(white2, late)
                    arrived(3, late)
                    spec[groups + q] = transform(white3, late)

            over_windows(step)
            piece = lags_of(sums_a[...], 2 * points)
            store_rows(near_out, c, 0, near_share(zero_flags, 1) * piece)
            start_all(near_from_1(c))
            add_piece(c, channels, far_share(zero_flags, 1) * piece)
            swap(c).start()

        over_bands(0, bands - 1, band)

        @pl.when(first)
        def _():
            c = bands - 1
            clear(sums_a, sums_b, sums_c)

            def step(q):
                s = c * groups + q
                arrived(0, s)
                one[...] = transform(white0, s)
                cross_into(sums_a, one, spec.at[s])
                cross_into(sums_b, one, spec.at[q])
                cross_into(sums_c, one, spec.at[groups + q])

            over_windows(step)
            pairs = lags_of_many(sums_a, sums_b, sums_c)
            store_sums(near_out, c, [near_share(zero_flags, o) * pairs[o - 1] for o in range(1, REACH + 1)])
            start_all(near_from_1_all(c))
            store_rows(far_out, c, points, far_share(zero_flags, 3) * pairs[2])
            start_all(far_pair_03(c, 1))
            store_rows(far_out, c, 0, far_share(zero_flags, 2) * pairs[1])
            start_all(far_pair_02(c, 1))
            add_piece(c, channels, far_share(zero_flags, 1) * pairs[0])
            swap(c).start()

    @pl.when(z == 2)
    def _():
        flags_to(0, 2, 0).wait_recv()

        @pl.when(first)
        def _():
            swap(bands - 1).start()

        @pl.when(second)
        def _():
            swap(2).start()

        clear(sums_a)

        def early_step(q):
            arrived(0, q)
            pass_on(q, 2, 3).start()
            one[...] = transform(white0, q)
            cross_into(sums_a, one, spec.at[q])

        over_windows(early_step)
        piece = lags_of(sums_a[...], 2 * points)
        store_rows(near_out, 0, 0, near_share(zero_flags, 2) * piece)
        near_out[0, :, points : points + channels] = jnp.zeros((2, channels, BAND), near_out.dtype)
        start_all(near_from_2(0))
        add_piece(0, 2 * channels, far_share(zero_flags, 2) * piece)
        swap(0).start()

        def band(turn):
            c = turn + m * lax.div(turn, 2)
            clear(sums_a, sums_b, sums_c)

            def step(q):
                s = c * groups + q
                arrived(3, s)
                three[...] = transform(white3, s)
                cross_into(sums_b, spec.at[s], three)

                @pl.when(q == groups - 1)
                def _():
                    sums_b[...] = lags_of(sums_b[...], 2 * points)

                arrived(0, s)
                one[...] = transform(white0, s)
                cross_into(sums_a, one, spec.at[s])
                cross_into(sums_c, one, three)

            over_windows(step)
            near, beyond = lags_of_many(sums_a, sums_c)
            store_sums(near_out, c, [near_share(zero_flags, 2) * near, near_share(zero_flags, 3) * beyond])
            start_all(near_from_2(c))
            ahead = sums_b[...]
            store_rows(far_out, c, 0, far_share(flag_ref, 1) * ahead)
            store_rows(far_out, c, points, far_share(zero_flags, 3) * beyond)
            start_all(far_from_2(c))
            add_piece(c, 2 * channels, far_share(zero_flags, 2) * near)
            add_piece(c, channels, near_share(flag_ref, 1) * ahead)
            swap(c).start()

        over_bands(1, bands - 1, band)

    @pl.when(z == 3)
    def _():
        flags_to(0, 3, 0).wait_recv()
        flags_to(1, 3, 0).wait_recv()

        @pl.loop(1, bands - 1)
        def _(turn):
            swap(turn + m * lax.div(turn, 2)).start()

        def band(c):
            clear(sums_a)

            def step(q):
                s = c * groups + q
                arrived(2, s)
                two[...] = transform(white2, s)
                cross_into(sums_a, two, spec.at[s])

            over_windows(step)
            piece = lags_of(sums_a[...], 2 * points)
            store_rows(far_out, c, 0, near_share(two_flags, 1) * piece)
            start_all(near_pair_23(c))
            add_piece(c, channels, far_share(two_flags, 1) * piece)

            @pl.when(c == 0)
            def _():
                clear(sums_c)

                def late_step(q):
                    s = c * groups + q
                    arrived(0, s)
                    one[...] = transform(white0, s)
                    cross_into(sums_c, one, spec.at[s])

                over_windows(late_step)
                distant = lags_of(sums_c[...], 2 * points)
                store_rows(near_out, c, points, near_share(zero_flags, 3) * distant)
                start_all(near_from_3(c))
                add_piece(c, 3 * channels, far_share(zero_flags, 3) * distant)

            swap(c).start()

        over_bands(0, 2, lambda turn: band(turn * (bands - 1 - m)))

    def lanes_of(core, c):
        return pl.ds(pl.multiple_of(core * half + place(c) * BAND, BAND), BAND)

    def collect(c):
        out_ref[:, :, lanes_of(m, c)] = stack[c, :, pl.ds(pl.multiple_of(m * kept, 8), kept)]
        swap(c).wait_recv()
        out_ref[:, :, lanes_of(1 - m, c)] = swapped[c]
        swap(c).wait_send()

    over_bands(0, bands, collect)

    def take(target, c, source, sender, low, high):
        top, end = max(low, target * kept), min(high, (target + 1) * kept)
        if top < end:
            rows = slice(top - target * kept, end - target * kept)
            results(c, source, sender, near_out, low, low, high, 0, 0)[target].wait_recv()
            out_ref[:, rows, lanes_of(sender, c)] += inbox[source, sender, c, :, rows].astype(F32)

    def take_at_0(target):
        for sender in range(halves):
            def band(turn):
                c = turn + sender * lax.div(turn, 2)
                take(target, c, 1, sender, channels, one_pair)
                take(target, c, 2, sender, 2 * channels, three_pairs)

            over_bands(0, bands - 1, band)
            take(target, 0, 3, sender, 3 * channels, three_pairs)
        take(target, bands - 1, 1, 0, channels, three_pairs)

    def take_at_1(target):
        take(target, 2, 0, 1, channels, one_pair)

    def take_at_2(target):
        for sender in range(halves):
            take(target, 0, 3, sender, channels, one_pair)
            take(target, bands - 1 - sender, 3, sender, channels, one_pair)
        take(target, 2, 0, 1, 2 * channels, two_pairs)
        take(target, bands - 1, 1, 0, 2 * channels, two_pairs)

    def take_at_3(target):
        for sender in range(halves):
            def band(turn):
                take(target, turn + sender * lax.div(turn, 2), 2, sender, channels, three_pairs)

            over_bands(1, bands - 1, band)
        take(target, 2, 0, 1, 3 * channels, three_pairs)
        take(target, bands - 1, 1, 0, 3 * channels, three_pairs)

    for block, step in enumerate((take_at_0, take_at_1, take_at_2, take_at_3)):
        for target in range(halves):
            @pl.when((z == block) & (m == target))
            def _():
                step(target)

    @pl.when(at_cut)
    def _():
        @pl.loop(0, groups)
        def _(q):
            edge(q).wait_send()

    def sent_range(begin, end, lane):
        @pl.loop(begin, end)
        def _(s):
            sent(s, lane)

    @pl.when(z == 0)
    def _():
        for device in range(1, blocks):
            flags_to(0, device, device - 1).wait_send()
        sent_range(0, (3 - m) * groups, 0)
        sent_range(3 * groups, pieces - 1 + m, 0)

        @pl.when(second)
        def _():
            finish_all(far_pair_01(2, 0))
            finish_all(far_pair_02(2, 0))
            finish_all(far_pair_03(2, 0))

    @pl.when(z == 1)
    def _():
        sent_range(0, 2 * groups, 0)
        sent_range((2 + m) * groups, (3 + m) * groups, 0)
        over_bands(0, bands - 1, lambda turn: finish_all(near_from_1(turn + m * lax.div(turn, 2))))

        @pl.when(second)
        def _():
            sent_range(2 * groups, 3 * groups, 1)

        @pl.when(first)
        def _():
            finish_all(near_from_1_all(bands - 1))
            finish_all(far_pair_03(bands - 1, 1))
            finish_all(far_pair_02(bands - 1, 1))

    @pl.when(z == 2)
    def _():
        flags_to(1, 3, 0).wait_send()

        @pl.when(first)
        def _():
            sent_range((bands - 1) * groups, pieces, 0)
            sent_range((bands - 1) * groups, pieces, 1)

        @pl.when(second)
        def _():
            sent_range(2 * groups, 3 * groups, 0)
            sent_range(2 * groups, 3 * groups, 1)

        sent_range(0, groups, 1)
        sent_range(0, groups, 2)
        finish_all(near_from_2(0))

        def band(turn):
            c = turn + m * lax.div(turn, 2)
            finish_all(near_from_2(c))
            finish_all(far_from_2(c))

        over_bands(1, bands - 1, band)

    @pl.when(z == 3)
    def _():
        sent_range(groups, pieces, 0)
        finish_all(near_pair_23(0))
        finish_all(near_pair_23(bands - 1 - m))
        finish_all(near_from_3(0))


def in_hbm(array):
    return pltpu.with_memory_space_constraint(array, pltpu.HBM)


def four_block_shards(spectra, counts, owners):
    parts, windows, channels, bins = spectra.shape
    halves, blocks = lax.axis_size("pairs"), lax.axis_size("cable")
    half, points = bins // halves, 2 * channels
    forward, inverse = channel_transforms(channels, 1.0 / math.sqrt(windows * channels))
    window = smoothing_window()
    bands, groups = half // BAND, windows // GROUP
    pieces = bands * groups
    rows = (REACH + 2) * channels
    kept = rows // halves
    block = pltpu.VMEM((pieces, GROUP, points, BAND), BF16)
    spectrum = pltpu.VMEM((2 * points, GROUP * BAND), F32)
    sums = pltpu.VMEM((2 * points, BAND), F32)
    shares = pltpu.VMEM((bands, 2, 2 * points, BAND), BF16)
    flags = (2 * (REACH + 1), BAND)
    dma = pltpu.SemaphoreType.DMA
    width = inverse.shape[1]
    tables = np.zeros((TABLE_ROWS, width), jnp.bfloat16)
    top = 0
    for table in (window, forward, inverse):
        tables[top : top + table.shape[0], : table.shape[1]] = table
        top += table.shape[0]
    hbm = pl.BlockSpec(memory_space=pl.ANY)
    smem = pl.BlockSpec(memory_space=pltpu.SMEM)
    out = pl.pallas_call(
        stack_kernel,
        out_shape=jax.ShapeDtypeStruct((2, kept, bins), F32),
        in_specs=[hbm, smem, hbm, hbm],
        out_specs=pl.BlockSpec(memory_space=pltpu.VMEM),
        scratch_shapes=[
            pltpu.SMEM(owners.shape, owners.dtype),
            pltpu.VMEM((2, windows, channels, half + 2 * EDGE), BF16),
            pltpu.VMEM(window.shape, BF16),
            pltpu.VMEM(forward.shape, BF16),
            pltpu.VMEM(inverse.shape, BF16),
            pltpu.VMEM(flags, F32),
            pltpu.VMEM((2,) + flags, F32),
            block, block, block, block, block,
            pltpu.VMEM((pieces, 2 * points, GROUP * BAND), F32),
            spectrum, spectrum, spectrum, sums, sums, sums,
            pltpu.VMEM((bands, 2, rows, BAND), F32),
            shares, shares,
            pltpu.VMEM((blocks, halves, bands, 2, kept, BAND), BF16),
            pltpu.VMEM((bands, 2, kept, BAND), F32),
            dma((groups,)), dma((3,)), dma((groups,)), dma((groups,)), dma((3,)), dma((2,)),
            dma((3, pieces)), dma((blocks, pieces)),
            dma((3, halves, bands)), dma((blocks, halves, bands)),
            dma((bands,)), dma((bands,)),
            pltpu.SemaphoreType.REGULAR, pltpu.SemaphoreType.REGULAR,
            pltpu.SemaphoreType.REGULAR, pltpu.SemaphoreType.REGULAR,
        ],
        compiler_params=pltpu.CompilerParams(
            collective_id=0, has_side_effects=True, vmem_limit_bytes=40 * 1024 * 1024
        ),
    )(in_hbm(spectra), counts, in_hbm(owners), in_hbm(jnp.asarray(tables)))
    return out[:, None]


def solution(mesh):
    sizes = dict(mesh.shape)
    fits = sizes["cable"] == REACH + 1 and sizes["pairs"] == 2 and sizes["bins"] == 2
    shards = four_block_shards if fits else general_shards
    placed = (
        P("groups", None, "cable", "bins"),
        P(("groups", "cable")),
        P(("groups", "cable"), None),
    )
    return jax.shard_map(
        shards,
        mesh=mesh,
        in_specs=placed,
        out_specs=P("groups", "cable", "pairs", "bins"),
        check_vma=False,
    )
```

```python
import math

import jax
import jax.numpy as jnp
import numpy as np
from jax import lax
from jax.experimental import pallas as pl
from jax.experimental.pallas import tpu as pltpu
from jax.sharding import PartitionSpec as P

REACH = 3
HALF_WIDTH = 32


epsilon = 1e-06
band_rows = 16


def with_halo(x, sides, width):
    for axis, dim in sides:
        count, length = (lax.axis_size(axis), x.shape[dim])
        up = [(i, (i + 1) % count) for i in range(count - 1)]
        down = [(j, i) for i, j in up]
        last = lax.slice_in_dim(x, length - width, length, axis=dim)
        first = lax.slice_in_dim(x, 0, width, axis=dim)
        before = lax.ppermute(last, axis, up)
        after = lax.ppermute(first, axis, down)
        x = jnp.concatenate([before, x, after], axis=dim)
    return x


def from_behind(block, axis, distance):
    devices = range(lax.axis_size(axis))
    route = [(i - distance, i) for i in devices if i - distance in devices]
    return lax.ppermute(block, axis, route)


def whiten_rows(spectra):
    real_part = spectra[0].astype(jnp.float32)
    imag_part = spectra[1].astype(jnp.float32)
    power_sum = real_part * real_part + imag_part * imag_part
    padded = with_halo(power_sum, (("bins", 2),), HALF_WIDTH)
    window_len = 2 * HALF_WIDTH + 1
    window_sum = lax.reduce_window(
        padded, jnp.zeros((), padded.dtype), lax.add, (1, 1, window_len), (1, 1, 1), "VALID"
    )
    inverse_amp = lax.rsqrt(window_sum / window_len + epsilon)
    return jnp.stack(
        [
            (real_part * inverse_amp).astype(jnp.bfloat16),
            (imag_part * inverse_amp).astype(jnp.bfloat16),
        ]
    )


def make_lag_table(col_count):
    flattened = jnp.arange(band_rows * col_count)
    row_of = flattened // col_count
    col_of = flattened % col_count
    lag_lanes = jnp.arange(col_count + band_rows - 1)
    return (lag_lanes[None, :] == (col_of - row_of + band_rows - 1)[:, None]).astype(jnp.bfloat16)


def lag_stack(pair_block, lag_table):
    freq_count, row_count, col_count = pair_block.shape
    group_count = row_count // band_rows
    grouped = pair_block.reshape(freq_count, group_count, band_rows * col_count)
    banded = jnp.einsum("fgk,ku->fgu", grouped, lag_table, preferred_element_type=jnp.float32)
    lag_sums = jnp.zeros((freq_count, col_count + row_count - 1), jnp.float32)
    for row_group in range(group_count):
        first_lag = row_count - band_rows * (row_group + 1)
        lag_sums = lag_sums.at[:, first_lag : first_lag + col_count + band_rows - 1].add(
            banded[:, row_group]
        )
    return lag_sums.T


def correlate(left_rows, right_rows, factor, lag_table):
    left_real = jnp.concatenate([left_rows[0], left_rows[1]], axis=0)
    left_imag = jnp.concatenate([left_rows[1], -left_rows[0]], axis=0)
    right_both = jnp.concatenate([right_rows[0], right_rows[1]], axis=0)
    corr_real = (
        jnp.einsum("wif,wjf->fij", left_real, right_both, preferred_element_type=jnp.float32)
        * factor
    ).astype(jnp.bfloat16)
    corr_imag = (
        jnp.einsum("wif,wjf->fij", left_imag, right_both, preferred_element_type=jnp.float32)
        * factor
    ).astype(jnp.bfloat16)
    return jnp.stack([lag_stack(corr_real, lag_table), lag_stack(corr_imag, lag_table)])


def general_shards(spectra, counts, owners):
    pair_devs = lax.axis_size("pairs")
    member = lax.axis_index("pairs")
    channels = spectra.shape[2]
    half_rows = channels // pair_devs
    source = whiten_rows(spectra)
    receiver = lax.dynamic_slice_in_dim(source, member * half_rows, half_rows, 2)
    block_count = lax.axis_size("cable")
    cable_index = lax.axis_index("cable")
    live_count = jnp.minimum(counts[0], block_count - cable_index)
    panels = {0: receiver}
    for offset in range(1, REACH + 1):
        panels[offset] = from_behind(receiver, "cable", -offset)
    factor = 1.0 / math.sqrt(source.shape[1] * channels)
    lag_table = make_lag_table(half_rows)
    freq_count = source.shape[3]
    stacks = jnp.zeros((2, (REACH + 2) * channels, freq_count), jnp.float32)
    for offset in range(REACH + 1):
        lag_piece = correlate(source, panels[offset], factor, lag_table)
        weight = (offset < live_count).astype(jnp.float32)
        if offset == 0:
            kept_here = weight * lag_piece
        else:
            sent_away = owners[0, offset].astype(jnp.float32)
            arrived = from_behind(weight * sent_away * lag_piece, "cable", offset)
            kept_here = weight * (1.0 - sent_away) * lag_piece + arrived
        first_lag = offset * channels + member * half_rows
        current = lax.dynamic_slice_in_dim(stacks, first_lag, kept_here.shape[1], 1)
        stacks = lax.dynamic_update_slice_in_dim(stacks, current + kept_here, first_lag, 1)
    summed = lax.psum_scatter(stacks, "pairs", scatter_dimension=1, tiled=True)
    return summed[:, None]


EDGE = 128
BAND = 128
GROUP = 2
EARLY = 9
CATCH_UP = 14
TABLE_ROWS = 2048
F32 = jnp.float32
BF16 = jnp.bfloat16
MESH = pl.DeviceIdType.MESH


def channel_transforms(channels, factor):
    points = 2 * channels
    index = np.arange(points)
    angle = 2 * np.pi * np.outer(index, np.arange(channels)) / points
    cos, sin = np.cos(angle), np.sin(angle)
    forward = split_high_low(np.block([[cos, sin], [-sin, cos]]))
    angle = 2 * np.pi * np.outer(index - (channels - 1), index) / points
    cos, sin = np.cos(angle), np.sin(angle)
    cos[-1], sin[-1] = 0.0, 0.0
    inverse = split_high_low(np.block([[cos, sin], [-sin, cos]]) * (factor / points))
    return forward, inverse


def split_high_low(full):
    high = full.astype(jnp.bfloat16)
    low = (full - high.astype(np.float64)).astype(jnp.bfloat16)
    return np.concatenate([high, low], axis=1)


def smoothing_window():
    distance = np.arange(BAND + 2 * EDGE)[:, None] - (np.arange(BAND)[None, :] + EDGE)
    ones = (np.abs(distance) <= HALF_WIDTH).astype(jnp.bfloat16)
    return np.concatenate([ones, ones], axis=0)


def stack_kernel(
    spectra_ref, counts_ref, owners_hbm, tables_ref, out_ref,
    owners_ref,
    x_ref, window_ref, forward_ref, inverse_ref, flag_ref, seen,
    white, white0, white1, white2, white3, spec, one, two, three, sums_a, sums_b, sums_c,
    stack, near_out, far_out, inbox, swapped,
    load_sem, constant_sem, edge_send, edge_recv, flag_send, flag_recv,
    block_send, block_recv, result_send, result_recv, swap_send, swap_recv, known, spread, drained, across,
):
    windows, channels = x_ref.shape[1:3]
    half = x_ref.shape[3] - 2 * EDGE
    bands, groups = half // BAND, windows // GROUP
    pieces = bands * groups
    points = 2 * channels
    kept = out_ref.shape[1]
    blocks, halves = lax.axis_size("cable"), lax.axis_size("pairs")
    z, m = lax.axis_index("cable"), lax.axis_index("pairs")
    cuts, x = lax.axis_size("bins"), lax.axis_index("bins")
    bins = spectra_ref.shape[3]
    first = m == 0
    second = m == 1
    mirrored = x
    partner = {"pairs": 1 - m}

    def remote(source, target, send, recv, device):
        return pltpu.make_async_remote_copy(
            src_ref=source, dst_ref=target, send_sem=send, recv_sem=recv, device_id=device, device_id_type=MESH
        )

    received = (white0, white1, white2, white3)

    def own_to(block, s, lane, device):
        return remote(
            white.at[s], received[block].at[s], block_send.at[lane, s], block_recv.at[block, s], {"cable": device}
        )

    def pass_on(s, lane, device):
        return remote(
            white0.at[s], white0.at[s], block_send.at[lane, s], block_recv.at[0, s], {"cable": device}
        )

    def arrived(block, s):
        own_to(block, s, 0, 0).wait_recv()

    def sent(s, lane):
        own_to(0, s, lane, 0).wait_send()

    def place(c):
        return c + mirrored * (bands - 1 - 2 * c)

    def results(c, source, sender, buffer, begin, low, high, device, lane):
        copies = {}
        for target in range(halves):
            top, end = max(low, target * kept), min(high, (target + 1) * kept)
            if top < end:
                copies[target] = remote(
                    buffer.at[c, :, top - begin : end - begin],
                    inbox.at[source, sender, c, :, top - target * kept : end - target * kept],
                    result_send.at[lane, target, c],
                    result_recv.at[source, sender, c],
                    {"cable": device, "pairs": target},
                )
        return copies

    def start_all(copies):
        for copy in copies.values():
            copy.start()

    def finish_all(copies):
        for copy in copies.values():
            copy.wait_send()

    one_pair = channels + points
    two_pairs = 2 * channels + points
    three_pairs = 3 * channels + points

    def near_from_1(c, sender=m):
        return results(c, 1, sender, near_out, channels, channels, one_pair, 0, 0)

    def near_from_1_all(c, sender=m):
        return results(c, 1, sender, near_out, channels, channels, three_pairs, 0, 0)

    def near_from_2(c, sender=m):
        return results(c, 2, sender, near_out, 2 * channels, 2 * channels, three_pairs, 0, 0)

    def near_from_3(c, sender=m):
        return results(c, 3, sender, near_out, channels, 3 * channels, three_pairs, 0, 0)

    def near_pair_23(c, sender=m):
        return results(c, 3, sender, far_out, channels, channels, one_pair, 2, 1)

    def far_from_2(c, sender=m):
        return results(c, 2, sender, far_out, channels, channels, three_pairs, 3, 1)

    def far_pair_01(c, source, sender=m):
        return results(c, source, sender, near_out, channels, channels, one_pair, 1, 0)

    def far_pair_02(c, source, sender=m):
        return results(c, source, sender, far_out, 2 * channels, 2 * channels, two_pairs, 2, 1)

    def far_pair_03(c, source, sender=m):
        return results(c, source, sender, far_out, channels, 3 * channels, three_pairs, 3, 2)

    def swap(c):
        rows = pl.ds(pl.multiple_of((1 - m) * kept, 8), kept)
        return remote(stack.at[c, :, rows], swapped.at[c], swap_send.at[c], swap_recv.at[c], partner)

    def load(q):
        near = pl.multiple_of(m * (half - EDGE), EDGE)
        begin = pl.multiple_of((1 - m) * EDGE, EDGE)
        rows = pl.ds(q * GROUP, GROUP)
        return pltpu.make_async_copy(
            spectra_ref.at[:, rows, :, pl.ds(near, half + EDGE)],
            x_ref.at[:, rows, :, pl.ds(begin, half + EDGE)],
            load_sem.at[q],
        )

    constants, top = [], 0
    for i, table in enumerate((window_ref, forward_ref, inverse_ref)):
        rows, columns = table.shape
        source = tables_ref.at[top : top + rows, :columns]
        constants.append(pltpu.make_async_copy(source, table, constant_sem.at[i]))
        top += rows

    def edge_lanes(core):
        return pl.ds(pl.multiple_of(core * (half + EDGE), EDGE), EDGE)

    def edge(q):
        begin = EDGE + (1 - x) * (half - EDGE)
        rows = pl.ds(q * GROUP, GROUP)
        return remote(
            x_ref.at[:, rows, :, pl.ds(pl.multiple_of(begin, EDGE), EDGE)],
            x_ref.at[:, rows, :, edge_lanes(x)],
            edge_send.at[q],
            edge_recv.at[q],
            {"bins": 1 - x, "pairs": x},
        )

    def flags_to(source, device, lane):
        return remote(
            flag_ref, seen.at[source], flag_send.at[lane], flag_recv.at[source], {"cable": device}
        )

    load(0).start()
    constants[0].start()
    settings = pltpu.make_async_copy(owners_hbm, owners_ref, flag_send.at[0])
    settings.start()
    for q in range(1, groups):
        load(q).start()
    constants[1].start()
    constants[2].start()
    barrier = pltpu.get_barrier_semaphore()
    beside = jnp.where((z > 0) & (z < blocks - 1), 2, 1)

    def tell_beside(semaphore):
        @pl.when(z > 0)
        def _():
            pl.semaphore_signal(semaphore, inc=1, device_id={"cable": z - 1}, device_id_type=MESH)

        @pl.when(z < blocks - 1)
        def _():
            pl.semaphore_signal(semaphore, inc=1, device_id={"cable": z + 1}, device_id_type=MESH)

    tell_beside(barrier)
    pl.semaphore_signal(barrier, inc=1, device_id=partner, device_id_type=MESH)
    at_cut = x != m

    @pl.when(at_cut & (z > 0))
    def _():
        pl.semaphore_signal(barrier, inc=1, device_id={"bins": 1 - x, "pairs": x}, device_id_type=MESH)

    def whiten(q, begin, count, store):
        lanes = pl.ds(pl.multiple_of(begin, BAND), count * BAND + 2 * EDGE)
        reals, imags, highs, lows = [], [], [], []
        for i in range(GROUP):
            real = x_ref[0, q * GROUP + i, :, lanes].astype(F32)
            imag = x_ref[1, q * GROUP + i, :, lanes].astype(F32)
            power = real * real + imag * imag
            high = power.astype(BF16)
            reals.append(real)
            imags.append(imag)
            highs.append(high)
            lows.append((power - high.astype(F32)).astype(BF16))
        high = jnp.concatenate(highs, axis=0)
        low = jnp.concatenate(lows, axis=0)
        for j in range(count):
            reach = slice(j * BAND, (j + 1) * BAND + 2 * EDGE)
            terms = jnp.concatenate([high[:, reach], low[:, reach]], axis=1)
            total = jnp.dot(terms, window_ref[...], preferred_element_type=F32)
            gain = lax.rsqrt(total / (2 * HALF_WIDTH + 1) + epsilon)
            here = slice(EDGE + j * BAND, EDGE + (j + 1) * BAND)
            slot = store(j) * groups + q
            for i in range(GROUP):
                rows = gain[i * channels : (i + 1) * channels]
                white[slot, i, :channels] = (reals[i][:, here] * rows).astype(BF16)
                white[slot, i, channels:] = (imags[i][:, here] * rows).astype(BF16)

    def whiten_inner(q):
        whiten(q, mirrored * BAND, bands - 1, lambda j: j + mirrored * (bands - 2 - 2 * j))

    def send_edge(q):
        @pl.when(at_cut & (z > 0))
        def _():
            edge(q).start()

    def send_first(q):
        @pl.when(z == 0)
        def _():
            own_to(0, q, 0, 1).start()

    def send_inner(q):
        @pl.when((z == 1) & second)
        def _():
            own_to(1, q + 2 * groups, 1, 0).start()

        @pl.when(z == 2)
        def _():
            own_to(2, q, 1, 3).start()

        @pl.when(z == 3)
        def _():
            own_to(3, q + groups, 0, 2).start()

    def relay(i):
        s = i + groups * m * lax.div(i, 2 * groups)
        arrived(0, s)
        pass_on(s, 0, 2).start()

    def relay_if(condition, i):
        @pl.when((z == 1) & condition)
        def _():
            relay(i)

    def send_range(block, begin, end, lane, device):
        @pl.loop(begin, end)
        def _(s):
            own_to(block, s, lane, device).start()

    def clear_edge(begin, count):
        @pl.when(~at_cut)
        def _():
            x_ref[:, begin : begin + count, :, edge_lanes(m)] = jnp.zeros((2, count, channels, EDGE), x_ref.dtype)

    clear_edge(0, GROUP)
    constants[0].wait()
    load(0).wait()
    whiten(0, mirrored * (bands - 1) * BAND, 1, lambda j: 0)
    pl.semaphore_wait(barrier, beside + 1 + jnp.where(at_cut & (z > 0), 1, 0))
    send_first(0)
    send_edge(0)
    tell_beside(known)

    @pl.when(at_cut & (z == 1))
    def _():
        pl.semaphore_signal(across, inc=1, device_id={"bins": 1 - x, "pairs": x}, device_id_type=MESH)

    whiten(0, BAND, bands - 2, lambda j: 1 + j + mirrored * (bands - 3 - 2 * j))
    send_inner(0)

    settings.wait()
    live = jnp.minimum(counts_ref[0], blocks - z)
    for offset in range(REACH + 1):
        flag_ref[offset : offset + 1, :] = jnp.full((1, BAND), owners_ref[0, offset].astype(F32))
        weight = jnp.where(offset < live, 1.0, 0.0)
        flag_ref[REACH + 1 + offset : REACH + 2 + offset, :] = jnp.full((1, BAND), weight)

    @pl.when(z == 0)
    def _():
        flags_to(0, 1, 0).start()

    @pl.when(z == 2)
    def _():
        flags_to(1, 3, 0).start()

    clear_edge(GROUP, windows - GROUP)

    def inner_step(q, carry):
        load(q).wait()
        send_edge(q)
        whiten_inner(q)
        send_first(q)
        send_inner(q)
        relay_if((q >= 3) & (lax.rem(q, 2) == 1), lax.div(q - 3, 2))
        return carry

    lax.fori_loop(1, groups // 2, inner_step, 0)
    pl.semaphore_wait(known, beside)

    @pl.when(at_cut & (z == 1))
    def _():
        pl.semaphore_wait(across, 1)

    tell_beside(spread)
    lax.fori_loop(groups // 2, groups, inner_step, 0)
    pl.semaphore_wait(spread, beside)

    @pl.when(at_cut & (z == 0))
    def _():
        @pl.loop(0, groups)
        def _(q):
            edge(q).start()

    @pl.when(z == 0)
    def _():
        for device in range(2, blocks):
            flags_to(0, device, device - 1).start()
        send_range(0, groups, (3 - m) * groups, 0, 1)

    @pl.when((z == 2) & second)
    def _():
        send_range(2, 2 * groups, 3 * groups, 0, 0)
        send_range(2, 2 * groups, 3 * groups, 1, 3)

    @pl.when((z == 3) & second)
    def _():
        send_range(3, 2 * groups, 3 * groups, 0, 0)

    constants[1].wait()
    constants[2].wait()

    def transform(buffer, s):
        wide = jnp.concatenate([buffer[s, i] for i in range(GROUP)], axis=1)
        return jnp.dot(forward_ref[...], jnp.concatenate([wide, wide], axis=0), preferred_element_type=F32)

    tile = 32

    def power_into(total, s):
        for k in range(0, points, tile):
            gained = total[k : k + tile]
            for i in range(GROUP):
                lanes = slice(i * BAND, (i + 1) * BAND)
                real = spec[s, k : k + tile, lanes]
                imag = spec[s, points + k : points + k + tile, lanes]
                gained = gained + (real * real + imag * imag)
            total[k : k + tile] = gained

    def cross_into(total, near, far):
        for k in range(0, points, tile):
            gained_real = total[k : k + tile]
            gained_imag = total[points + k : points + k + tile]
            for i in range(GROUP):
                lanes = slice(i * BAND, (i + 1) * BAND)
                near_real = near[k : k + tile, lanes]
                near_imag = near[points + k : points + k + tile, lanes]
                far_real = far[k : k + tile, lanes]
                far_imag = far[points + k : points + k + tile, lanes]
                gained_real = gained_real + (near_real * far_real + near_imag * far_imag)
                gained_imag = gained_imag + (near_imag * far_real - near_real * far_imag)
            total[k : k + tile] = gained_real
            total[points + k : points + k + tile] = gained_imag

    def lags_of(values, columns):
        high = values.astype(BF16)
        low = (values - high.astype(F32)).astype(BF16)
        table = inverse_ref[:, :columns]
        rest = inverse_ref[:, 2 * points : 2 * points + columns]
        return jnp.dot(
            jnp.concatenate([table, rest, table], axis=1),
            jnp.concatenate([high, high, low], axis=0),
            preferred_element_type=F32,
        )

    def lags_of_many(*totals):
        both = lags_of(jnp.concatenate([total[...] for total in totals], axis=1), 2 * points)
        return [both[:, i * BAND : (i + 1) * BAND] for i in range(len(totals))]

    def add_piece(c, begin, piece):
        rows = pl.ds(begin, points)
        stack[c, 0, rows] += piece[:points]
        stack[c, 1, rows] += piece[points:]

    def clear(*totals):
        for total in totals:
            total[...] = jnp.zeros_like(total)

    def over_windows(step):
        def body(q, carry):
            step(q)
            return carry

        lax.fori_loop(0, groups, body, 0)

    def over_bands(begin, end, band):
        def body(c, carry):
            band(c)
            return carry

        lax.fori_loop(begin, end, body, 0)

    def own_band(c):
        clear(sums_a)

        def step(q):
            s = c * groups + q
            spec[s] = transform(white, s)
            power_into(sums_a, s)

        over_windows(step)
        stack[c] = jnp.zeros(stack.shape[1:], F32)
        add_piece(c, 0, flag_ref[REACH + 1 : REACH + 2, :] * lags_of(sums_a[:points], points))
        relay_if(c >= 0, EARLY - bands - 2 + c + 2 * lax.div(c, bands - 1))

    over_bands(0, bands - 1, own_band)

    def last_step(q, carry):
        @pl.when(at_cut)
        def _():
            edge(q).wait_recv()

        whiten(q, (1 - mirrored) * (bands - 1) * BAND, 1, lambda j: bands - 1)
        s = (bands - 1) * groups + q

        @pl.when(z == 0)
        def _():
            own_to(0, s, 0, 1).start()

        @pl.when((z == 2) & first)
        def _():
            own_to(2, s, 0, 1).start()
            own_to(2, s, 1, 3).start()

        @pl.when(z == 3)
        def _():
            own_to(3, s, 0, 1 + m).start()

        relay_if(lax.rem(q, 4) == 3, EARLY - 3 + lax.div(q, 4))
        return carry

    lax.fori_loop(0, groups, last_step, 0)

    @pl.when((z == 3) & first)
    def _():
        send_range(3, 2 * groups, 3 * groups, 0, 2)

    over_bands(bands - 1, bands, own_band)

    def owner_of(flags, offset):
        return flags[offset : offset + 1, :]

    def far_share(flags, offset):
        return owner_of(flags, offset) * flags[REACH + 1 + offset : REACH + 2 + offset, :]

    def near_share(flags, offset):
        return (1.0 - owner_of(flags, offset)) * flags[REACH + 1 + offset : REACH + 2 + offset, :]

    def store_rows(buffer, c, begin, piece, rows=slice(0, 2 * channels)):
        count = rows.stop - rows.start
        for part in range(2):
            top = part * points
            buffer[c, part, begin : begin + count] = piece[top + rows.start : top + rows.stop].astype(buffer.dtype)

    def store_sums(buffer, c, parts):
        for part in range(2):
            top = part * points
            for k in range(len(parts) + 1):
                terms = []
                if k < len(parts):
                    terms.append(parts[k][top : top + channels])
                if k > 0:
                    terms.append(parts[k - 1][top + channels : top + points])
                total = terms[0] if len(terms) == 1 else terms[0] + terms[1]
                buffer[c, part, k * channels : (k + 1) * channels] = total.astype(buffer.dtype)

    zero_flags, two_flags = seen.at[0], seen.at[1]

    @pl.when(z == 0)
    def _():
        @pl.when(second)
        def _():
            clear(sums_a, sums_b, sums_c)

            def step(q):
                for block, total, held in ((1, sums_a, one), (2, sums_b, two), (3, sums_c, three)):
                    s = 2 * groups + q
                    arrived(block, s)
                    held[...] = transform(received[block], s)
                    cross_into(total, spec.at[s], held)

            over_windows(step)
            pairs = lags_of_many(sums_a, sums_b, sums_c)
            for offset in range(1, REACH + 1):
                add_piece(2, offset * channels, near_share(flag_ref, offset) * pairs[offset - 1])
            store_rows(near_out, 2, 0, far_share(flag_ref, 1) * pairs[0])
            store_rows(far_out, 2, 0, far_share(flag_ref, 2) * pairs[1])
            store_rows(far_out, 2, points, far_share(flag_ref, 3) * pairs[2])

        @pl.loop(0, bands)
        def _(c):
            swap(c).start()

        @pl.when(first)
        def _():
            sent(pieces - 1, 0)
            pl.semaphore_signal(drained, inc=1, device_id=partner, device_id_type=MESH)

        @pl.when(second)
        def _():
            pl.semaphore_wait(drained, 1)
            start_all(far_pair_03(2, 0))
            start_all(far_pair_02(2, 0))
            start_all(far_pair_01(2, 0))

    @pl.when(z == 1)
    def _():
        flags_to(0, 1, 0).wait_recv()

        @pl.when(second)
        def _():
            swap(2).start()

        def band(turn):
            c = turn + m * lax.div(turn, 2)
            clear(sums_a)

            def step(q):
                s = c * groups + q
                i = turn * groups + q

                @pl.when((i < CATCH_UP) & (lax.rem(i, 2) == 0))
                def _():
                    relay(EARLY + lax.div(i, 2))

                @pl.when((i >= CATCH_UP) & (i + EARLY - CATCH_UP // 2 < 3 * groups))
                def _():
                    relay(i + EARLY - CATCH_UP // 2)

                one[...] = transform(white0, s)
                cross_into(sums_a, one, spec.at[s])

                @pl.when(first & (turn == bands - 2))
                def _():
                    late = (bands - 1) * groups + q
                    arrived(2, late)
                    spec[q] = transform(white2, late)
                    arrived(3, late)
                    spec[groups + q] = transform(white3, late)

            over_windows(step)
            piece = lags_of(sums_a[...], 2 * points)
            store_rows(near_out, c, 0, near_share(zero_flags, 1) * piece)
            start_all(near_from_1(c))
            add_piece(c, channels, far_share(zero_flags, 1) * piece)
            swap(c).start()

        over_bands(0, bands - 1, band)

        @pl.when(first)
        def _():
            c = bands - 1
            clear(sums_a, sums_b, sums_c)

            def step(q):
                s = c * groups + q
                arrived(0, s)
                one[...] = transform(white0, s)
                cross_into(sums_a, one, spec.at[s])
                cross_into(sums_b, one, spec.at[q])
                cross_into(sums_c, one, spec.at[groups + q])

            over_windows(step)
            pairs = lags_of_many(sums_a, sums_b, sums_c)
            store_sums(near_out, c, [near_share(zero_flags, o) * pairs[o - 1] for o in range(1, REACH + 1)])
            start_all(near_from_1_all(c))
            store_rows(far_out, c, points, far_share(zero_flags, 3) * pairs[2])
            start_all(far_pair_03(c, 1))
            store_rows(far_out, c, 0, far_share(zero_flags, 2) * pairs[1])
            start_all(far_pair_02(c, 1))
            add_piece(c, channels, far_share(zero_flags, 1) * pairs[0])
            swap(c).start()

    @pl.when(z == 2)
    def _():
        flags_to(0, 2, 0).wait_recv()

        @pl.when(first)
        def _():
            swap(bands - 1).start()

        @pl.when(second)
        def _():
            swap(2).start()

        clear(sums_a)

        def early_step(q):
            arrived(0, q)
            pass_on(q, 2, 3).start()
            one[...] = transform(white0, q)
            cross_into(sums_a, one, spec.at[q])

        over_windows(early_step)
        piece = lags_of(sums_a[...], 2 * points)
        store_rows(near_out, 0, 0, near_share(zero_flags, 2) * piece)
        near_out[0, :, points : points + channels] = jnp.zeros((2, channels, BAND), near_out.dtype)
        start_all(near_from_2(0))
        add_piece(0, 2 * channels, far_share(zero_flags, 2) * piece)
        swap(0).start()

        def band(turn):
            c = turn + m * lax.div(turn, 2)
            clear(sums_a, sums_b, sums_c)

            def step(q):
                s = c * groups + q
                arrived(3, s)
                three[...] = transform(white3, s)
                cross_into(sums_b, spec.at[s], three)

                @pl.when(q == groups - 1)
                def _():
                    sums_b[...] = lags_of(sums_b[...], 2 * points)

                arrived(0, s)
                one[...] = transform(white0, s)
                cross_into(sums_a, one, spec.at[s])
                cross_into(sums_c, one, three)

            over_windows(step)
            near, beyond = lags_of_many(sums_a, sums_c)
            store_sums(near_out, c, [near_share(zero_flags, 2) * near, near_share(zero_flags, 3) * beyond])
            start_all(near_from_2(c))
            ahead = sums_b[...]
            store_rows(far_out, c, 0, far_share(flag_ref, 1) * ahead)
            store_rows(far_out, c, points, far_share(zero_flags, 3) * beyond)
            start_all(far_from_2(c))
            add_piece(c, 2 * channels, far_share(zero_flags, 2) * near)
            add_piece(c, channels, near_share(flag_ref, 1) * ahead)
            swap(c).start()

        over_bands(1, bands - 1, band)

    @pl.when(z == 3)
    def _():
        flags_to(0, 3, 0).wait_recv()
        flags_to(1, 3, 0).wait_recv()

        @pl.loop(1, bands - 1)
        def _(turn):
            swap(turn + m * lax.div(turn, 2)).start()

        def band(c):
            clear(sums_a)

            def step(q):
                s = c * groups + q
                arrived(2, s)
                two[...] = transform(white2, s)
                cross_into(sums_a, two, spec.at[s])

            over_windows(step)
            piece = lags_of(sums_a[...], 2 * points)
            store_rows(far_out, c, 0, near_share(two_flags, 1) * piece)
            start_all(near_pair_23(c))
            add_piece(c, channels, far_share(two_flags, 1) * piece)

            @pl.when(c == 0)
            def _():
                clear(sums_c)

                def late_step(q):
                    s = c * groups + q
                    arrived(0, s)
                    one[...] = transform(white0, s)
                    cross_into(sums_c, one, spec.at[s])

                over_windows(late_step)
                distant = lags_of(sums_c[...], 2 * points)
                store_rows(near_out, c, points, near_share(zero_flags, 3) * distant)
                start_all(near_from_3(c))
                add_piece(c, 3 * channels, far_share(zero_flags, 3) * distant)

            swap(c).start()

        over_bands(0, 2, lambda turn: band(turn * (bands - 1 - m)))

    def lanes_of(core, c):
        return pl.ds(pl.multiple_of(core * half + place(c) * BAND, BAND), BAND)

    def collect(c):
        out_ref[:, :, lanes_of(m, c)] = stack[c, :, pl.ds(pl.multiple_of(m * kept, 8), kept)]
        swap(c).wait_recv()
        out_ref[:, :, lanes_of(1 - m, c)] = swapped[c]
        swap(c).wait_send()

    over_bands(0, bands, collect)

    def take(target, c, source, sender, low, high):
        top, end = max(low, target * kept), min(high, (target + 1) * kept)
        if top < end:
            rows = slice(top - target * kept, end - target * kept)
            results(c, source, sender, near_out, low, low, high, 0, 0)[target].wait_recv()
            out_ref[:, rows, lanes_of(sender, c)] += inbox[source, sender, c, :, rows].astype(F32)

    def take_at_0(target):
        for sender in range(halves):
            def band(turn):
                c = turn + sender * lax.div(turn, 2)
                take(target, c, 1, sender, channels, one_pair)
                take(target, c, 2, sender, 2 * channels, three_pairs)

            over_bands(0, bands - 1, band)
            take(target, 0, 3, sender, 3 * channels, three_pairs)
        take(target, bands - 1, 1, 0, channels, three_pairs)

    def take_at_1(target):
        take(target, 2, 0, 1, channels, one_pair)

    def take_at_2(target):
        for sender in range(halves):
            take(target, 0, 3, sender, channels, one_pair)
            take(target, bands - 1 - sender, 3, sender, channels, one_pair)
        take(target, 2, 0, 1, 2 * channels, two_pairs)
        take(target, bands - 1, 1, 0, 2 * channels, two_pairs)

    def take_at_3(target):
        for sender in range(halves):
            def band(turn):
                take(target, turn + sender * lax.div(turn, 2), 2, sender, channels, three_pairs)

            over_bands(1, bands - 1, band)
        take(target, 2, 0, 1, 3 * channels, three_pairs)
        take(target, bands - 1, 1, 0, 3 * channels, three_pairs)

    for block, step in enumerate((take_at_0, take_at_1, take_at_2, take_at_3)):
        for target in range(halves):
            @pl.when((z == block) & (m == target))
            def _():
                step(target)

    @pl.when(at_cut)
    def _():
        @pl.loop(0, groups)
        def _(q):
            edge(q).wait_send()

    def sent_range(begin, end, lane):
        @pl.loop(begin, end)
        def _(s):
            sent(s, lane)

    @pl.when(z == 0)
    def _():
        for device in range(1, blocks):
            flags_to(0, device, device - 1).wait_send()
        sent_range(0, (3 - m) * groups, 0)
        sent_range(3 * groups, pieces - 1 + m, 0)

        @pl.when(second)
        def _():
            finish_all(far_pair_01(2, 0))
            finish_all(far_pair_02(2, 0))
            finish_all(far_pair_03(2, 0))

    @pl.when(z == 1)
    def _():
        sent_range(0, 2 * groups, 0)
        sent_range((2 + m) * groups, (3 + m) * groups, 0)
        over_bands(0, bands - 1, lambda turn: finish_all(near_from_1(turn + m * lax.div(turn, 2))))

        @pl.when(second)
        def _():
            sent_range(2 * groups, 3 * groups, 1)

        @pl.when(first)
        def _():
            finish_all(near_from_1_all(bands - 1))
            finish_all(far_pair_03(bands - 1, 1))
            finish_all(far_pair_02(bands - 1, 1))

    @pl.when(z == 2)
    def _():
        flags_to(1, 3, 0).wait_send()

        @pl.when(first)
        def _():
            sent_range((bands - 1) * groups, pieces, 0)
            sent_range((bands - 1) * groups, pieces, 1)

        @pl.when(second)
        def _():
            sent_range(2 * groups, 3 * groups, 0)
            sent_range(2 * groups, 3 * groups, 1)

        sent_range(0, groups, 1)
        sent_range(0, groups, 2)
        finish_all(near_from_2(0))

        def band(turn):
            c = turn + m * lax.div(turn, 2)
            finish_all(near_from_2(c))
            finish_all(far_from_2(c))

        over_bands(1, bands - 1, band)

    @pl.when(z == 3)
    def _():
        sent_range(groups, pieces, 0)
        finish_all(near_pair_23(0))
        finish_all(near_pair_23(bands - 1 - m))
        finish_all(near_from_3(0))


def in_hbm(array):
    return pltpu.with_memory_space_constraint(array, pltpu.HBM)


def four_block_shards(spectra, counts, owners):
    parts, windows, channels, bins = spectra.shape
    halves, blocks = lax.axis_size("pairs"), lax.axis_size("cable")
    half, points = bins // halves, 2 * channels
    forward, inverse = channel_transforms(channels, 1.0 / math.sqrt(windows * channels))
    window = smoothing_window()
    bands, groups = half // BAND, windows // GROUP
    pieces = bands * groups
    rows = (REACH + 2) * channels
    kept = rows // halves
    block = pltpu.VMEM((pieces, GROUP, points, BAND), BF16)
    spectrum = pltpu.VMEM((2 * points, GROUP * BAND), F32)
    sums = pltpu.VMEM((2 * points, BAND), F32)
    shares = pltpu.VMEM((bands, 2, 2 * points, BAND), BF16)
    flags = (2 * (REACH + 1), BAND)
    dma = pltpu.SemaphoreType.DMA
    width = inverse.shape[1]
    tables = np.zeros((TABLE_ROWS, width), jnp.bfloat16)
    top = 0
    for table in (window, forward, inverse):
        tables[top : top + table.shape[0], : table.shape[1]] = table
        top += table.shape[0]
    hbm = pl.BlockSpec(memory_space=pl.ANY)
    smem = pl.BlockSpec(memory_space=pltpu.SMEM)
    out = pl.pallas_call(
        stack_kernel,
        out_shape=jax.ShapeDtypeStruct((2, kept, bins), F32),
        in_specs=[hbm, smem, hbm, hbm],
        out_specs=pl.BlockSpec(memory_space=pltpu.VMEM),
        scratch_shapes=[
            pltpu.SMEM(owners.shape, owners.dtype),
            pltpu.VMEM((2, windows, channels, half + 2 * EDGE), BF16),
            pltpu.VMEM(window.shape, BF16),
            pltpu.VMEM(forward.shape, BF16),
            pltpu.VMEM(inverse.shape, BF16),
            pltpu.VMEM(flags, F32),
            pltpu.VMEM((2,) + flags, F32),
            block, block, block, block, block,
            pltpu.VMEM((pieces, 2 * points, GROUP * BAND), F32),
            spectrum, spectrum, spectrum, sums, sums, sums,
            pltpu.VMEM((bands, 2, rows, BAND), F32),
            shares, shares,
            pltpu.VMEM((blocks, halves, bands, 2, kept, BAND), BF16),
            pltpu.VMEM((bands, 2, kept, BAND), F32),
            dma((groups,)), dma((3,)), dma((groups,)), dma((groups,)), dma((3,)), dma((2,)),
            dma((3, pieces)), dma((blocks, pieces)),
            dma((3, halves, bands)), dma((blocks, halves, bands)),
            dma((bands,)), dma((bands,)),
            pltpu.SemaphoreType.REGULAR, pltpu.SemaphoreType.REGULAR,
            pltpu.SemaphoreType.REGULAR, pltpu.SemaphoreType.REGULAR,
        ],
        compiler_params=pltpu.CompilerParams(
            collective_id=0, has_side_effects=True, vmem_limit_bytes=40 * 1024 * 1024
        ),
    )(in_hbm(spectra), counts, in_hbm(owners), in_hbm(jnp.asarray(tables)))
    return out[:, None]


def solution(mesh):
    sizes = dict(mesh.shape)
    fits = sizes["cable"] == REACH + 1 and sizes["pairs"] == 2 and sizes["bins"] == 2
    shards = four_block_shards if fits else general_shards
    placed = (
        P("groups", None, "cable", "bins"),
        P(("groups", "cable")),
        P(("groups", "cable"), None),
    )
    return jax.shard_map(
        shards,
        mesh=mesh,
        in_specs=placed,
        out_specs=P("groups", "cable", "pairs", "bins"),
        check_vma=False,
    )
```

```python
import math

import jax
import jax.numpy as jnp
import numpy as np
from jax import lax
from jax.experimental import pallas as pl
from jax.experimental.pallas import tpu as pltpu
from jax.sharding import PartitionSpec as P

REACH = 3
HALF_WIDTH = 32


epsilon = 1e-06
band_rows = 16


def with_halo(x, sides, width):
    for axis, dim in sides:
        count, length = (lax.axis_size(axis), x.shape[dim])
        up = [(i, (i + 1) % count) for i in range(count - 1)]
        down = [(j, i) for i, j in up]
        last = lax.slice_in_dim(x, length - width, length, axis=dim)
        first = lax.slice_in_dim(x, 0, width, axis=dim)
        before = lax.ppermute(last, axis, up)
        after = lax.ppermute(first, axis, down)
        x = jnp.concatenate([before, x, after], axis=dim)
    return x


def from_behind(block, axis, distance):
    devices = range(lax.axis_size(axis))
    route = [(i - distance, i) for i in devices if i - distance in devices]
    return lax.ppermute(block, axis, route)


def whiten_rows(spectra):
    real_part = spectra[0].astype(jnp.float32)
    imag_part = spectra[1].astype(jnp.float32)
    power_sum = real_part * real_part + imag_part * imag_part
    padded = with_halo(power_sum, (("bins", 2),), HALF_WIDTH)
    window_len = 2 * HALF_WIDTH + 1
    window_sum = lax.reduce_window(
        padded, jnp.zeros((), padded.dtype), lax.add, (1, 1, window_len), (1, 1, 1), "VALID"
    )
    inverse_amp = lax.rsqrt(window_sum / window_len + epsilon)
    return jnp.stack(
        [
            (real_part * inverse_amp).astype(jnp.bfloat16),
            (imag_part * inverse_amp).astype(jnp.bfloat16),
        ]
    )


def make_lag_table(col_count):
    flattened = jnp.arange(band_rows * col_count)
    row_of = flattened // col_count
    col_of = flattened % col_count
    lag_lanes = jnp.arange(col_count + band_rows - 1)
    return (lag_lanes[None, :] == (col_of - row_of + band_rows - 1)[:, None]).astype(jnp.bfloat16)


def lag_stack(pair_block, lag_table):
    freq_count, row_count, col_count = pair_block.shape
    group_count = row_count // band_rows
    grouped = pair_block.reshape(freq_count, group_count, band_rows * col_count)
    banded = jnp.einsum("fgk,ku->fgu", grouped, lag_table, preferred_element_type=jnp.float32)
    lag_sums = jnp.zeros((freq_count, col_count + row_count - 1), jnp.float32)
    for row_group in range(group_count):
        first_lag = row_count - band_rows * (row_group + 1)
        lag_sums = lag_sums.at[:, first_lag : first_lag + col_count + band_rows - 1].add(
            banded[:, row_group]
        )
    return lag_sums.T


def correlate(left_rows, right_rows, factor, lag_table):
    left_real = jnp.concatenate([left_rows[0], left_rows[1]], axis=0)
    left_imag = jnp.concatenate([left_rows[1], -left_rows[0]], axis=0)
    right_both = jnp.concatenate([right_rows[0], right_rows[1]], axis=0)
    corr_real = (
        jnp.einsum("wif,wjf->fij", left_real, right_both, preferred_element_type=jnp.float32)
        * factor
    ).astype(jnp.bfloat16)
    corr_imag = (
        jnp.einsum("wif,wjf->fij", left_imag, right_both, preferred_element_type=jnp.float32)
        * factor
    ).astype(jnp.bfloat16)
    return jnp.stack([lag_stack(corr_real, lag_table), lag_stack(corr_imag, lag_table)])


def general_shards(spectra, counts, owners):
    pair_devs = lax.axis_size("pairs")
    member = lax.axis_index("pairs")
    channels = spectra.shape[2]
    half_rows = channels // pair_devs
    source = whiten_rows(spectra)
    receiver = lax.dynamic_slice_in_dim(source, member * half_rows, half_rows, 2)
    block_count = lax.axis_size("cable")
    cable_index = lax.axis_index("cable")
    live_count = jnp.minimum(counts[0], block_count - cable_index)
    panels = {0: receiver}
    for offset in range(1, REACH + 1):
        panels[offset] = from_behind(receiver, "cable", -offset)
    factor = 1.0 / math.sqrt(source.shape[1] * channels)
    lag_table = make_lag_table(half_rows)
    freq_count = source.shape[3]
    stacks = jnp.zeros((2, (REACH + 2) * channels, freq_count), jnp.float32)
    for offset in range(REACH + 1):
        lag_piece = correlate(source, panels[offset], factor, lag_table)
        weight = (offset < live_count).astype(jnp.float32)
        if offset == 0:
            kept_here = weight * lag_piece
        else:
            sent_away = owners[0, offset].astype(jnp.float32)
            arrived = from_behind(weight * sent_away * lag_piece, "cable", offset)
            kept_here = weight * (1.0 - sent_away) * lag_piece + arrived
        first_lag = offset * channels + member * half_rows
        current = lax.dynamic_slice_in_dim(stacks, first_lag, kept_here.shape[1], 1)
        stacks = lax.dynamic_update_slice_in_dim(stacks, current + kept_here, first_lag, 1)
    summed = lax.psum_scatter(stacks, "pairs", scatter_dimension=1, tiled=True)
    return summed[:, None]


EDGE = 128
BAND = 128
GROUP = 2
EARLY = 9
CATCH_UP = 14
TABLE_ROWS = 2048
F32 = jnp.float32
BF16 = jnp.bfloat16
MESH = pl.DeviceIdType.MESH


def channel_transforms(channels, factor):
    points = 2 * channels
    index = np.arange(points)
    angle = 2 * np.pi * np.outer(index, np.arange(channels)) / points
    cos, sin = np.cos(angle), np.sin(angle)
    forward = split_high_low(np.block([[cos, sin], [-sin, cos]]))
    angle = 2 * np.pi * np.outer(index - (channels - 1), index) / points
    cos, sin = np.cos(angle), np.sin(angle)
    cos[-1], sin[-1] = 0.0, 0.0
    inverse = split_high_low(np.block([[cos, sin], [-sin, cos]]) * (factor / points))
    return forward, inverse


def split_high_low(full):
    high = full.astype(jnp.bfloat16)
    low = (full - high.astype(np.float64)).astype(jnp.bfloat16)
    return np.concatenate([high, low], axis=1)


def smoothing_window():
    distance = np.arange(BAND + 2 * EDGE)[:, None] - (np.arange(BAND)[None, :] + EDGE)
    ones = (np.abs(distance) <= HALF_WIDTH).astype(jnp.bfloat16)
    return np.concatenate([ones, ones], axis=0)


def stack_kernel(
    spectra_ref, counts_ref, owners_hbm, tables_ref, out_ref,
    owners_ref,
    x_ref, window_ref, forward_ref, inverse_ref, flag_ref, seen,
    white, white0, white1, white2, white3, spec, one, two, three, sums_a, sums_b, sums_c,
    stack, near_out, far_out, inbox, swapped,
    load_sem, constant_sem, edge_send, edge_recv, flag_send, flag_recv,
    block_send, block_recv, result_send, result_recv, swap_send, swap_recv, known, spread, drained, across,
):
    windows, channels = x_ref.shape[1:3]
    half = x_ref.shape[3] - 2 * EDGE
    bands, groups = half // BAND, windows // GROUP
    pieces = bands * groups
    points = 2 * channels
    kept = out_ref.shape[1]
    blocks, halves = lax.axis_size("cable"), lax.axis_size("pairs")
    z, m = lax.axis_index("cable"), lax.axis_index("pairs")
    cuts, x = lax.axis_size("bins"), lax.axis_index("bins")
    bins = spectra_ref.shape[3]
    first = m == 0
    second = m == 1
    mirrored = x
    partner = {"pairs": 1 - m}

    def remote(source, target, send, recv, device):
        return pltpu.make_async_remote_copy(
            src_ref=source, dst_ref=target, send_sem=send, recv_sem=recv, device_id=device, device_id_type=MESH
        )

    received = (white0, white1, white2, white3)

    def own_to(block, s, lane, device):
        return remote(
            white.at[s], received[block].at[s], block_send.at[lane, s], block_recv.at[block, s], {"cable": device}
        )

    def pass_on(s, lane, device):
        return remote(
            white0.at[s], white0.at[s], block_send.at[lane, s], block_recv.at[0, s], {"cable": device}
        )

    def arrived(block, s):
        own_to(block, s, 0, 0).wait_recv()

    def sent(s, lane):
        own_to(0, s, lane, 0).wait_send()

    def place(c):
        return c + mirrored * (bands - 1 - 2 * c)

    def results(c, source, sender, buffer, begin, low, high, device, lane):
        copies = {}
        for target in range(halves):
            top, end = max(low, target * kept), min(high, (target + 1) * kept)
            if top < end:
                copies[target] = remote(
                    buffer.at[c, :, top - begin : end - begin],
                    inbox.at[source, sender, c, :, top - target * kept : end - target * kept],
                    result_send.at[lane, target, c],
                    result_recv.at[source, sender, c],
                    {"cable": device, "pairs": target},
                )
        return copies

    def start_all(copies):
        for copy in copies.values():
            copy.start()

    def finish_all(copies):
        for copy in copies.values():
            copy.wait_send()

    one_pair = channels + points
    two_pairs = 2 * channels + points
    three_pairs = 3 * channels + points

    def near_from_1(c, sender=m):
        return results(c, 1, sender, near_out, channels, channels, one_pair, 0, 0)

    def near_from_1_all(c, sender=m):
        return results(c, 1, sender, near_out, channels, channels, three_pairs, 0, 0)

    def near_from_2(c, sender=m):
        return results(c, 2, sender, near_out, 2 * channels, 2 * channels, three_pairs, 0, 0)

    def near_from_3(c, sender=m):
        return results(c, 3, sender, near_out, channels, 3 * channels, three_pairs, 0, 0)

    def near_pair_23(c, sender=m):
        return results(c, 3, sender, far_out, channels, channels, one_pair, 2, 1)

    def far_from_2(c, sender=m):
        return results(c, 2, sender, far_out, channels, channels, three_pairs, 3, 1)

    def far_pair_01(c, source, sender=m):
        return results(c, source, sender, near_out, channels, channels, one_pair, 1, 0)

    def far_pair_02(c, source, sender=m):
        return results(c, source, sender, far_out, 2 * channels, 2 * channels, two_pairs, 2, 1)

    def far_pair_03(c, source, sender=m):
        return results(c, source, sender, far_out, channels, 3 * channels, three_pairs, 3, 2)

    def swap(c):
        rows = pl.ds(pl.multiple_of((1 - m) * kept, 8), kept)
        return remote(stack.at[c, :, rows], swapped.at[c], swap_send.at[c], swap_recv.at[c], partner)

    def load(q):
        near = pl.multiple_of(m * (half - EDGE), EDGE)
        begin = pl.multiple_of((1 - m) * EDGE, EDGE)
        rows = pl.ds(q * GROUP, GROUP)
        return pltpu.make_async_copy(
            spectra_ref.at[:, rows, :, pl.ds(near, half + EDGE)],
            x_ref.at[:, rows, :, pl.ds(begin, half + EDGE)],
            load_sem.at[q],
        )

    constants, top = [], 0
    for i, table in enumerate((window_ref, forward_ref, inverse_ref)):
        rows, columns = table.shape
        source = tables_ref.at[top : top + rows, :columns]
        constants.append(pltpu.make_async_copy(source, table, constant_sem.at[i]))
        top += rows

    def edge_lanes(core):
        return pl.ds(pl.multiple_of(core * (half + EDGE), EDGE), EDGE)

    def edge(q):
        begin = EDGE + (1 - x) * (half - EDGE)
        rows = pl.ds(q * GROUP, GROUP)
        return remote(
            x_ref.at[:, rows, :, pl.ds(pl.multiple_of(begin, EDGE), EDGE)],
            x_ref.at[:, rows, :, edge_lanes(x)],
            edge_send.at[q],
            edge_recv.at[q],
            {"bins": 1 - x, "pairs": x},
        )

    def flags_to(source, device, lane):
        return remote(
            flag_ref, seen.at[source], flag_send.at[lane], flag_recv.at[source], {"cable": device}
        )

    load(0).start()
    constants[0].start()
    settings = pltpu.make_async_copy(owners_hbm, owners_ref, flag_send.at[0])
    settings.start()
    for q in range(1, groups):
        load(q).start()
    constants[1].start()
    constants[2].start()
    barrier = pltpu.get_barrier_semaphore()
    beside = jnp.where((z > 0) & (z < blocks - 1), 2, 1)

    def tell_beside(semaphore):
        @pl.when(z > 0)
        def _():
            pl.semaphore_signal(semaphore, inc=1, device_id={"cable": z - 1}, device_id_type=MESH)

        @pl.when(z < blocks - 1)
        def _():
            pl.semaphore_signal(semaphore, inc=1, device_id={"cable": z + 1}, device_id_type=MESH)

    tell_beside(barrier)
    pl.semaphore_signal(barrier, inc=1, device_id=partner, device_id_type=MESH)
    at_cut = x != m

    @pl.when(at_cut & (z > 0))
    def _():
        pl.semaphore_signal(barrier, inc=1, device_id={"bins": 1 - x, "pairs": x}, device_id_type=MESH)

    def whiten(q, begin, count, store):
        lanes = pl.ds(pl.multiple_of(begin, BAND), count * BAND + 2 * EDGE)
        reals, imags, highs, lows = [], [], [], []
        for i in range(GROUP):
            real = x_ref[0, q * GROUP + i, :, lanes].astype(F32)
            imag = x_ref[1, q * GROUP + i, :, lanes].astype(F32)
            power = real * real + imag * imag
            high = power.astype(BF16)
            reals.append(real)
            imags.append(imag)
            highs.append(high)
            lows.append((power - high.astype(F32)).astype(BF16))
        high = jnp.concatenate(highs, axis=0)
        low = jnp.concatenate(lows, axis=0)
        for j in range(count):
            reach = slice(j * BAND, (j + 1) * BAND + 2 * EDGE)
            terms = jnp.concatenate([high[:, reach], low[:, reach]], axis=1)
            total = jnp.dot(terms, window_ref[...], preferred_element_type=F32)
            gain = lax.rsqrt(total / (2 * HALF_WIDTH + 1) + epsilon)
            here = slice(EDGE + j * BAND, EDGE + (j + 1) * BAND)
            slot = store(j) * groups + q
            for i in range(GROUP):
                rows = gain[i * channels : (i + 1) * channels]
                white[slot, i, :channels] = (reals[i][:, here] * rows).astype(BF16)
                white[slot, i, channels:] = (imags[i][:, here] * rows).astype(BF16)

    def whiten_inner(q):
        whiten(q, mirrored * BAND, bands - 1, lambda j: j + mirrored * (bands - 2 - 2 * j))

    def send_edge(q):
        @pl.when(at_cut & (z > 0))
        def _():
            edge(q).start()

    def send_first(q):
        @pl.when(z == 0)
        def _():
            own_to(0, q, 0, 1).start()

    def send_inner(q):
        @pl.when((z == 1) & second)
        def _():
            own_to(1, q + 2 * groups, 1, 0).start()

        @pl.when(z == 2)
        def _():
            own_to(2, q, 1, 3).start()

        @pl.when(z == 3)
        def _():
            own_to(3, q + groups, 0, 2).start()

    def relay(i):
        s = i + groups * m * lax.div(i, 2 * groups)
        arrived(0, s)
        pass_on(s, 0, 2).start()

    def relay_if(condition, i):
        @pl.when((z == 1) & condition)
        def _():
            relay(i)

    def send_range(block, begin, end, lane, device):
        @pl.loop(begin, end)
        def _(s):
            own_to(block, s, lane, device).start()

    def clear_edge(begin, count):
        @pl.when(~at_cut)
        def _():
            x_ref[:, begin : begin + count, :, edge_lanes(m)] = jnp.zeros((2, count, channels, EDGE), x_ref.dtype)

    clear_edge(0, GROUP)
    constants[0].wait()
    load(0).wait()
    whiten(0, mirrored * (bands - 1) * BAND, 1, lambda j: 0)
    pl.semaphore_wait(barrier, beside + 1 + jnp.where(at_cut & (z > 0), 1, 0))
    send_first(0)
    send_edge(0)
    tell_beside(known)

    @pl.when(at_cut & (z == 1))
    def _():
        pl.semaphore_signal(across, inc=1, device_id={"bins": 1 - x, "pairs": x}, device_id_type=MESH)

    whiten(0, BAND, bands - 2, lambda j: 1 + j + mirrored * (bands - 3 - 2 * j))
    send_inner(0)

    settings.wait()
    live = jnp.minimum(counts_ref[0], blocks - z)
    for offset in range(REACH + 1):
        flag_ref[offset : offset + 1, :] = jnp.full((1, BAND), owners_ref[0, offset].astype(F32))
        weight = jnp.where(offset < live, 1.0, 0.0)
        flag_ref[REACH + 1 + offset : REACH + 2 + offset, :] = jnp.full((1, BAND), weight)

    @pl.when(z == 0)
    def _():
        flags_to(0, 1, 0).start()

    @pl.when(z == 2)
    def _():
        flags_to(1, 3, 0).start()

    clear_edge(GROUP, windows - GROUP)

    def inner_step(q, carry):
        load(q).wait()
        send_edge(q)
        whiten_inner(q)
        send_first(q)
        send_inner(q)
        relay_if((q >= 3) & (lax.rem(q, 2) == 1), lax.div(q - 3, 2))
        return carry

    lax.fori_loop(1, groups // 2, inner_step, 0)
    pl.semaphore_wait(known, beside)

    @pl.when(at_cut & (z == 1))
    def _():
        pl.semaphore_wait(across, 1)

    tell_beside(spread)
    lax.fori_loop(groups // 2, groups, inner_step, 0)
    pl.semaphore_wait(spread, beside)

    @pl.when(at_cut & (z == 0))
    def _():
        @pl.loop(0, groups)
        def _(q):
            edge(q).start()

    @pl.when(z == 0)
    def _():
        for device in range(2, blocks):
            flags_to(0, device, device - 1).start()
        send_range(0, groups, (3 - m) * groups, 0, 1)

    @pl.when((z == 2) & second)
    def _():
        send_range(2, 2 * groups, 3 * groups, 0, 0)
        send_range(2, 2 * groups, 3 * groups, 1, 3)

    @pl.when((z == 3) & second)
    def _():
        send_range(3, 2 * groups, 3 * groups, 0, 0)

    constants[1].wait()
    constants[2].wait()

    def transform(buffer, s):
        wide = jnp.concatenate([buffer[s, i] for i in range(GROUP)], axis=1)
        return jnp.dot(forward_ref[...], jnp.concatenate([wide, wide], axis=0), preferred_element_type=F32)

    tile = 32

    def power_into(total, s):
        for k in range(0, points, tile):
            gained = total[k : k + tile]
            for i in range(GROUP):
                lanes = slice(i * BAND, (i + 1) * BAND)
                real = spec[s, k : k + tile, lanes]
                imag = spec[s, points + k : points + k + tile, lanes]
                gained = gained + (real * real + imag * imag)
            total[k : k + tile] = gained

    def cross_into(total, near, far):
        for k in range(0, points, tile):
            gained_real = total[k : k + tile]
            gained_imag = total[points + k : points + k + tile]
            for i in range(GROUP):
                lanes = slice(i * BAND, (i + 1) * BAND)
                near_real = near[k : k + tile, lanes]
                near_imag = near[points + k : points + k + tile, lanes]
                far_real = far[k : k + tile, lanes]
                far_imag = far[points + k : points + k + tile, lanes]
                gained_real = gained_real + (near_real * far_real + near_imag * far_imag)
                gained_imag = gained_imag + (near_imag * far_real - near_real * far_imag)
            total[k : k + tile] = gained_real
            total[points + k : points + k + tile] = gained_imag

    def lags_of(values, columns):
        high = values.astype(BF16)
        low = (values - high.astype(F32)).astype(BF16)
        table = inverse_ref[:, :columns]
        rest = inverse_ref[:, 2 * points : 2 * points + columns]
        return jnp.dot(
            jnp.concatenate([table, rest, table], axis=1),
            jnp.concatenate([high, high, low], axis=0),
            preferred_element_type=F32,
        )

    def lags_of_many(*totals):
        both = lags_of(jnp.concatenate([total[...] for total in totals], axis=1), 2 * points)
        return [both[:, i * BAND : (i + 1) * BAND] for i in range(len(totals))]

    def add_piece(c, begin, piece):
        rows = pl.ds(begin, points)
        stack[c, 0, rows] += piece[:points]
        stack[c, 1, rows] += piece[points:]

    def clear(*totals):
        for total in totals:
            total[...] = jnp.zeros_like(total)

    def over_windows(step):
        def body(q, carry):
            step(q)
            return carry

        lax.fori_loop(0, groups, body, 0)

    def over_bands(begin, end, band):
        def body(c, carry):
            band(c)
            return carry

        lax.fori_loop(begin, end, body, 0)

    def own_band(c):
        clear(sums_a)

        def step(q):
            s = c * groups + q
            spec[s] = transform(white, s)
            power_into(sums_a, s)

        over_windows(step)
        stack[c] = jnp.zeros(stack.shape[1:], F32)
        add_piece(c, 0, flag_ref[REACH + 1 : REACH + 2, :] * lags_of(sums_a[:points], points))
        relay_if(c >= 0, EARLY - bands - 2 + c + 2 * lax.div(c, bands - 1))

    over_bands(0, bands - 1, own_band)

    def last_step(q, carry):
        @pl.when(at_cut)
        def _():
            edge(q).wait_recv()

        whiten(q, (1 - mirrored) * (bands - 1) * BAND, 1, lambda j: bands - 1)
        s = (bands - 1) * groups + q

        @pl.when(z == 0)
        def _():
            own_to(0, s, 0, 1).start()

        @pl.when((z == 2) & first)
        def _():
            own_to(2, s, 0, 1).start()
            own_to(2, s, 1, 3).start()

        @pl.when(z == 3)
        def _():
            own_to(3, s, 0, 1 + m).start()

        relay_if(lax.rem(q, 4) == 3, EARLY - 3 + lax.div(q, 4))
        return carry

    lax.fori_loop(0, groups, last_step, 0)

    @pl.when((z == 3) & first)
    def _():
        send_range(3, 2 * groups, 3 * groups, 0, 2)

    over_bands(bands - 1, bands, own_band)

    def owner_of(flags, offset):
        return flags[offset : offset + 1, :]

    def far_share(flags, offset):
        return owner_of(flags, offset) * flags[REACH + 1 + offset : REACH + 2 + offset, :]

    def near_share(flags, offset):
        return (1.0 - owner_of(flags, offset)) * flags[REACH + 1 + offset : REACH + 2 + offset, :]

    def store_rows(buffer, c, begin, piece, rows=slice(0, 2 * channels)):
        count = rows.stop - rows.start
        for part in range(2):
            top = part * points
            buffer[c, part, begin : begin + count] = piece[top + rows.start : top + rows.stop].astype(buffer.dtype)

    def store_sums(buffer, c, parts):
        for part in range(2):
            top = part * points
            for k in range(len(parts) + 1):
                terms = []
                if k < len(parts):
                    terms.append(parts[k][top : top + channels])
                if k > 0:
                    terms.append(parts[k - 1][top + channels : top + points])
                total = terms[0] if len(terms) == 1 else terms[0] + terms[1]
                buffer[c, part, k * channels : (k + 1) * channels] = total.astype(buffer.dtype)

    zero_flags, two_flags = seen.at[0], seen.at[1]

    @pl.when(z == 0)
    def _():
        @pl.when(second)
        def _():
            clear(sums_a, sums_b, sums_c)

            def step(q):
                for block, total, held in ((1, sums_a, one), (2, sums_b, two), (3, sums_c, three)):
                    s = 2 * groups + q
                    arrived(block, s)
                    held[...] = transform(received[block], s)
                    cross_into(total, spec.at[s], held)

            over_windows(step)
            pairs = lags_of_many(sums_a, sums_b, sums_c)
            for offset in range(1, REACH + 1):
                add_piece(2, offset * channels, near_share(flag_ref, offset) * pairs[offset - 1])
            store_rows(near_out, 2, 0, far_share(flag_ref, 1) * pairs[0])
            store_rows(far_out, 2, 0, far_share(flag_ref, 2) * pairs[1])
            store_rows(far_out, 2, points, far_share(flag_ref, 3) * pairs[2])

        @pl.loop(0, bands)
        def _(c):
            swap(c).start()

        @pl.when(first)
        def _():
            sent(pieces - 1, 0)
            pl.semaphore_signal(drained, inc=1, device_id=partner, device_id_type=MESH)

        @pl.when(second)
        def _():
            pl.semaphore_wait(drained, 1)
            start_all(far_pair_03(2, 0))
            start_all(far_pair_02(2, 0))
            start_all(far_pair_01(2, 0))

    @pl.when(z == 1)
    def _():
        flags_to(0, 1, 0).wait_recv()

        @pl.when(second)
        def _():
            swap(2).start()

        def band(turn):
            c = turn + m * lax.div(turn, 2)
            clear(sums_a)

            def step(q):
                s = c * groups + q
                i = turn * groups + q

                @pl.when((i < CATCH_UP) & (lax.rem(i, 2) == 0))
                def _():
                    relay(EARLY + lax.div(i, 2))

                @pl.when((i >= CATCH_UP) & (i + EARLY - CATCH_UP // 2 < 3 * groups))
                def _():
                    relay(i + EARLY - CATCH_UP // 2)

                one[...] = transform(white0, s)
                cross_into(sums_a, one, spec.at[s])

                @pl.when(first & (turn == bands - 2))
                def _():
                    late = (bands - 1) * groups + q
                    arrived(2, late)
                    spec[q] = transform(white2, late)
                    arrived(3, late)
                    spec[groups + q] = transform(white3, late)

            over_windows(step)
            piece = lags_of(sums_a[...], 2 * points)
            store_rows(near_out, c, 0, near_share(zero_flags, 1) * piece)
            start_all(near_from_1(c))
            add_piece(c, channels, far_share(zero_flags, 1) * piece)
            swap(c).start()

        over_bands(0, bands - 1, band)

        @pl.when(first)
        def _():
            c = bands - 1
            clear(sums_a, sums_b, sums_c)

            def step(q):
                s = c * groups + q
                arrived(0, s)
                one[...] = transform(white0, s)
                cross_into(sums_a, one, spec.at[s])
                cross_into(sums_b, one, spec.at[q])
                cross_into(sums_c, one, spec.at[groups + q])

            over_windows(step)
            pairs = lags_of_many(sums_a, sums_b, sums_c)
            store_sums(near_out, c, [near_share(zero_flags, o) * pairs[o - 1] for o in range(1, REACH + 1)])
            start_all(near_from_1_all(c))
            store_rows(far_out, c, points, far_share(zero_flags, 3) * pairs[2])
            start_all(far_pair_03(c, 1))
            store_rows(far_out, c, 0, far_share(zero_flags, 2) * pairs[1])
            start_all(far_pair_02(c, 1))
            add_piece(c, channels, far_share(zero_flags, 1) * pairs[0])
            swap(c).start()

    @pl.when(z == 2)
    def _():
        flags_to(0, 2, 0).wait_recv()

        @pl.when(first)
        def _():
            swap(bands - 1).start()

        @pl.when(second)
        def _():
            swap(2).start()

        clear(sums_a)

        def early_step(q):
            arrived(0, q)
            pass_on(q, 2, 3).start()
            one[...] = transform(white0, q)
            cross_into(sums_a, one, spec.at[q])

        over_windows(early_step)
        piece = lags_of(sums_a[...], 2 * points)
        store_rows(near_out, 0, 0, near_share(zero_flags, 2) * piece)
        near_out[0, :, points : points + channels] = jnp.zeros((2, channels, BAND), near_out.dtype)
        start_all(near_from_2(0))
        add_piece(0, 2 * channels, far_share(zero_flags, 2) * piece)
        swap(0).start()

        def band(turn):
            c = turn + m * lax.div(turn, 2)
            clear(sums_a, sums_b, sums_c)

            def step(q):
                s = c * groups + q
                arrived(3, s)
                three[...] = transform(white3, s)
                cross_into(sums_b, spec.at[s], three)

                @pl.when(q == groups - 1)
                def _():
                    sums_b[...] = lags_of(sums_b[...], 2 * points)

                arrived(0, s)
                one[...] = transform(white0, s)
                cross_into(sums_a, one, spec.at[s])
                cross_into(sums_c, one, three)

            over_windows(step)
            near, beyond = lags_of_many(sums_a, sums_c)
            store_sums(near_out, c, [near_share(zero_flags, 2) * near, near_share(zero_flags, 3) * beyond])
            for copy in reversed(near_from_2(c).values()):
                copy.start()
            ahead = sums_b[...]
            store_rows(far_out, c, 0, far_share(flag_ref, 1) * ahead)
            store_rows(far_out, c, points, far_share(zero_flags, 3) * beyond)
            start_all(far_from_2(c))
            add_piece(c, 2 * channels, far_share(zero_flags, 2) * near)
            add_piece(c, channels, near_share(flag_ref, 1) * ahead)
            swap(c).start()

        over_bands(1, bands - 1, band)

    @pl.when(z == 3)
    def _():
        flags_to(0, 3, 0).wait_recv()
        flags_to(1, 3, 0).wait_recv()

        @pl.loop(1, bands - 1)
        def _(turn):
            swap(turn + m * lax.div(turn, 2)).start()

        def band(c):
            clear(sums_a)

            def step(q):
                s = c * groups + q
                arrived(2, s)
                two[...] = transform(white2, s)
                cross_into(sums_a, two, spec.at[s])

            over_windows(step)
            piece = lags_of(sums_a[...], 2 * points)
            store_rows(far_out, c, 0, near_share(two_flags, 1) * piece)
            start_all(near_pair_23(c))
            add_piece(c, channels, far_share(two_flags, 1) * piece)

            @pl.when(c == 0)
            def _():
                clear(sums_c)

                def late_step(q):
                    s = c * groups + q
                    arrived(0, s)
                    one[...] = transform(white0, s)
                    cross_into(sums_c, one, spec.at[s])

                over_windows(late_step)
                distant = lags_of(sums_c[...], 2 * points)
                store_rows(near_out, c, points, near_share(zero_flags, 3) * distant)
                start_all(near_from_3(c))
                add_piece(c, 3 * channels, far_share(zero_flags, 3) * distant)

            swap(c).start()

        over_bands(0, 2, lambda turn: band(turn * (bands - 1 - m)))

    def lanes_of(core, c):
        return pl.ds(pl.multiple_of(core * half + place(c) * BAND, BAND), BAND)

    def collect(c):
        out_ref[:, :, lanes_of(m, c)] = stack[c, :, pl.ds(pl.multiple_of(m * kept, 8), kept)]
        swap(c).wait_recv()
        out_ref[:, :, lanes_of(1 - m, c)] = swapped[c]
        swap(c).wait_send()

    over_bands(0, bands, collect)

    def take(target, c, source, sender, low, high):
        top, end = max(low, target * kept), min(high, (target + 1) * kept)
        if top < end:
            rows = slice(top - target * kept, end - target * kept)
            results(c, source, sender, near_out, low, low, high, 0, 0)[target].wait_recv()
            out_ref[:, rows, lanes_of(sender, c)] += inbox[source, sender, c, :, rows].astype(F32)

    def take_at_0(target):
        for sender in range(halves):
            def band(turn):
                c = turn + sender * lax.div(turn, 2)
                take(target, c, 1, sender, channels, one_pair)
                take(target, c, 2, sender, 2 * channels, three_pairs)

            over_bands(0, bands - 1, band)
            take(target, 0, 3, sender, 3 * channels, three_pairs)
        take(target, bands - 1, 1, 0, channels, three_pairs)

    def take_at_1(target):
        take(target, 2, 0, 1, channels, one_pair)

    def take_at_2(target):
        for sender in range(halves):
            take(target, 0, 3, sender, channels, one_pair)
            take(target, bands - 1 - sender, 3, sender, channels, one_pair)
        take(target, 2, 0, 1, 2 * channels, two_pairs)
        take(target, bands - 1, 1, 0, 2 * channels, two_pairs)

    def take_at_3(target):
        for sender in range(halves):
            def band(turn):
                take(target, turn + sender * lax.div(turn, 2), 2, sender, channels, three_pairs)

            over_bands(1, bands - 1, band)
        take(target, 2, 0, 1, 3 * channels, three_pairs)
        take(target, bands - 1, 1, 0, 3 * channels, three_pairs)

    for block, step in enumerate((take_at_0, take_at_1, take_at_2, take_at_3)):
        for target in range(halves):
            @pl.when((z == block) & (m == target))
            def _():
                step(target)

    @pl.when(at_cut)
    def _():
        @pl.loop(0, groups)
        def _(q):
            edge(q).wait_send()

    def sent_range(begin, end, lane):
        @pl.loop(begin, end)
        def _(s):
            sent(s, lane)

    @pl.when(z == 0)
    def _():
        for device in range(1, blocks):
            flags_to(0, device, device - 1).wait_send()
        sent_range(0, (3 - m) * groups, 0)
        sent_range(3 * groups, pieces - 1 + m, 0)

        @pl.when(second)
        def _():
            finish_all(far_pair_01(2, 0))
            finish_all(far_pair_02(2, 0))
            finish_all(far_pair_03(2, 0))

    @pl.when(z == 1)
    def _():
        sent_range(0, 2 * groups, 0)
        sent_range((2 + m) * groups, (3 + m) * groups, 0)
        over_bands(0, bands - 1, lambda turn: finish_all(near_from_1(turn + m * lax.div(turn, 2))))

        @pl.when(second)
        def _():
            sent_range(2 * groups, 3 * groups, 1)

        @pl.when(first)
        def _():
            finish_all(near_from_1_all(bands - 1))
            finish_all(far_pair_03(bands - 1, 1))
            finish_all(far_pair_02(bands - 1, 1))

    @pl.when(z == 2)
    def _():
        flags_to(1, 3, 0).wait_send()

        @pl.when(first)
        def _():
            sent_range((bands - 1) * groups, pieces, 0)
            sent_range((bands - 1) * groups, pieces, 1)

        @pl.when(second)
        def _():
            sent_range(2 * groups, 3 * groups, 0)
            sent_range(2 * groups, 3 * groups, 1)

        sent_range(0, groups, 1)
        sent_range(0, groups, 2)
        finish_all(near_from_2(0))

        def band(turn):
            c = turn + m * lax.div(turn, 2)
            finish_all(near_from_2(c))
            finish_all(far_from_2(c))

        over_bands(1, bands - 1, band)

    @pl.when(z == 3)
    def _():
        sent_range(groups, pieces, 0)
        finish_all(near_pair_23(0))
        finish_all(near_pair_23(bands - 1 - m))
        finish_all(near_from_3(0))


def in_hbm(array):
    return pltpu.with_memory_space_constraint(array, pltpu.HBM)


def four_block_shards(spectra, counts, owners):
    parts, windows, channels, bins = spectra.shape
    halves, blocks = lax.axis_size("pairs"), lax.axis_size("cable")
    half, points = bins // halves, 2 * channels
    forward, inverse = channel_transforms(channels, 1.0 / math.sqrt(windows * channels))
    window = smoothing_window()
    bands, groups = half // BAND, windows // GROUP
    pieces = bands * groups
    rows = (REACH + 2) * channels
    kept = rows // halves
    block = pltpu.VMEM((pieces, GROUP, points, BAND), BF16)
    spectrum = pltpu.VMEM((2 * points, GROUP * BAND), F32)
    sums = pltpu.VMEM((2 * points, BAND), F32)
    shares = pltpu.VMEM((bands, 2, 2 * points, BAND), BF16)
    flags = (2 * (REACH + 1), BAND)
    dma = pltpu.SemaphoreType.DMA
    width = inverse.shape[1]
    tables = np.zeros((TABLE_ROWS, width), jnp.bfloat16)
    top = 0
    for table in (window, forward, inverse):
        tables[top : top + table.shape[0], : table.shape[1]] = table
        top += table.shape[0]
    hbm = pl.BlockSpec(memory_space=pl.ANY)
    smem = pl.BlockSpec(memory_space=pltpu.SMEM)
    out = pl.pallas_call(
        stack_kernel,
        out_shape=jax.ShapeDtypeStruct((2, kept, bins), F32),
        in_specs=[hbm, smem, hbm, hbm],
        out_specs=pl.BlockSpec(memory_space=pltpu.VMEM),
        scratch_shapes=[
            pltpu.SMEM(owners.shape, owners.dtype),
            pltpu.VMEM((2, windows, channels, half + 2 * EDGE), BF16),
            pltpu.VMEM(window.shape, BF16),
            pltpu.VMEM(forward.shape, BF16),
            pltpu.VMEM(inverse.shape, BF16),
            pltpu.VMEM(flags, F32),
            pltpu.VMEM((2,) + flags, F32),
            block, block, block, block, block,
            pltpu.VMEM((pieces, 2 * points, GROUP * BAND), F32),
            spectrum, spectrum, spectrum, sums, sums, sums,
            pltpu.VMEM((bands, 2, rows, BAND), F32),
            shares, shares,
            pltpu.VMEM((blocks, halves, bands, 2, kept, BAND), BF16),
            pltpu.VMEM((bands, 2, kept, BAND), F32),
            dma((groups,)), dma((3,)), dma((groups,)), dma((groups,)), dma((3,)), dma((2,)),
            dma((3, pieces)), dma((blocks, pieces)),
            dma((3, halves, bands)), dma((blocks, halves, bands)),
            dma((bands,)), dma((bands,)),
            pltpu.SemaphoreType.REGULAR, pltpu.SemaphoreType.REGULAR,
            pltpu.SemaphoreType.REGULAR, pltpu.SemaphoreType.REGULAR,
        ],
        compiler_params=pltpu.CompilerParams(
            collective_id=0, has_side_effects=True, vmem_limit_bytes=40 * 1024 * 1024
        ),
    )(in_hbm(spectra), counts, in_hbm(owners), in_hbm(jnp.asarray(tables)))
    return out[:, None]


def solution(mesh):
    sizes = dict(mesh.shape)
    fits = sizes["cable"] == REACH + 1 and sizes["pairs"] == 2 and sizes["bins"] == 2
    shards = four_block_shards if fits else general_shards
    placed = (
        P("groups", None, "cable", "bins"),
        P(("groups", "cable")),
        P(("groups", "cable"), None),
    )
    return jax.shard_map(
        shards,
        mesh=mesh,
        in_specs=placed,
        out_specs=P("groups", "cable", "pairs", "bins"),
        check_vma=False,
    )
```
